32 devices in a mesh: section: 2 (over y), rows: 8 (over z, x), tensor: 2 (over core).
Axes of the slice: x: 2, y: 2, z: 4, core: 2. Of those that a mesh axis runs over, the one named last changes fastest.
Arguments:
- tokens: bfloat16 [2, 8192, 1024], P(None, ('rows', 'tensor')), may hold values from -6 to 6
- segment_ids: int32 [2, 8, 1024], P(None, 'rows'), may hold values from 0 to 7, never falling along the last dimension, each value on 1 to 256 neighbouring positions
- cotangent: bfloat16 [2, 8192, 1024], P(None, ('rows', 'tensor')), may hold values from -6 to 6
- ln_gain: float32 [2, 2, 1024], P('section'), may hold values from 0.5 to 1.5
- ln_bias: float32 [2, 2, 1024], P('section'), may hold values from -1.75 to 1.75
- w_qkv: float32 [2, 1024, 3, 1024], P('section', 'rows', None, 'tensor'), may hold values from -0.1875 to 0.1875
- query_key_value_bias: float32 [2, 3, 1024], P('section', None, 'tensor'), may hold values from -1.75 to 1.75
- w_proj: float32 [2, 1024, 1024], P('section', ('tensor', 'rows')), may hold values from -1.5 to 1.5
- w_fc: float32 [2, 1024, 4096], P('section', 'rows', 'tensor'), may hold values from -0.1875 to 0.1875
- fc_bias: float32 [2, 4096], P('section', 'tensor'), may hold values from -1.75 to 1.75
- w_fc2: float32 [2, 4096, 1024], P('section', ('tensor', 'rows')), may hold values from -0.09375 to 0.09375
- out_bias: float32 [2, 2, 1024], P('section'), may hold values from -1.75 to 1.75
- prefix_embed: float32 [10, 1024], replicated, may hold values from -6 to 6
- rep_w1: float32 [1024, 512], replicated, may hold values from -0.1875 to 0.1875
- rep_b1: float32 [512], replicated, may hold values from -1.75 to 1.75
- rep_w2: float32 [512, 2, 2, 1024], P(None, 'section', None, 'tensor'), may hold values from -0.5 to 0.5
- rep_b2: float32 [2, 2, 1024], P('section', None, 'tensor'), may hold values from -1.75 to 1.75
Outputs:
- acts: float32 [2, 2, 8192, 1024], P('section', None, ('rows', 'tensor'))
- in_grads: float32 [2, 2, 8192, 1024], P('section', None, ('rows', 'tensor'))
- grad_embed: float32 [10, 1024], P(None, 'rows')
- grad_w1: float32 [1024, 512], P('rows')
- grad_b1: float32 [512], replicated
- grad_w2: float32 [512, 2, 2, 1024], P('rows', 'section', None, 'tensor')
- grad_b2: float32 [2, 2, 1024], P('section', None, 'tensor')
The draws below stay inside these ranges and needn't reach their ends.
Inputs may be any that keep to these rules, and one draw needn't show every extreme that they name: `segment_ids`: within each packed row of 1024 tokens the ids never fall; each id's run holds 1 to 256 positions and some run holds exactly 256.
All inputs are finite; a program needn't handle non-finite values.
Results may differ from the reference program's by a relative error of at most 0.025.
Values may be sent and summed in bfloat16 or wider, within the bound.
No kernel may reach another device: no remote copies, remote signals or barrier semaphores. Data moves between devices by JAX's collectives and lax.ppermute only.
A program may use at most 384 MiB of HBM per device.

```python
import math
import jax
import jax.numpy as jnp
import numpy as np
from jax import lax

D = 1024
HEADS = 16
HEAD = 64
FF = 4096
MID = 512
PREF = 10
SEQ = 1024
SEGS = 8
MICRO = 2
LAYERS = 2
SEG_MOST = 256
PACKED = 8
ROW_TOKENS = 8192


def block_scale(stream_key, dims, split, low, high):
    def one(position, parts):
        heights = jax.random.uniform(jax.random.fold_in(jax.random.fold_in(stream_key, 6), position), (parts,), jnp.float32, low / len(split), high / len(split))
        return jnp.repeat(jnp.exp(heights), dims[position] // parts).reshape((-1,) + (1,) * (len(dims) - position - 1))

    gain = one(*split[0])
    for cut in split[1:]:
        gain = gain * one(*cut)
    return gain


def profile(amount, total, most, lean):
    weights = [(1 << 20) // math.isqrt(grade ** lean) + 1 for grade in range(2, amount + 1)]
    spare, given = total - most - (amount - 1), [1] * (amount - 1)
    while spare > 0:
        movable = [i for i in range(amount - 1) if given[i] < most]
        mass, left = sum([weights[i] for i in movable]), spare
        for i in movable:
            more = min(most - given[i], max(1, left * weights[i] // mass), spare)
            given[i] = given[i] + more
            spare = spare - more
    return np.array([most] + given)


def ragged(own_key, number_of, total, limit, lean):
    if number_of == 2:
        one = jax.random.randint(own_key, (), max(1, total - limit), min(limit, total - 1) + 1)
        return jnp.stack([one, total - one])
    tallies = jnp.asarray(profile(number_of, total, limit, lean), jnp.int32)
    twos = (number_of - 1) // 2
    source_of, sink = tallies[1:1 + 2 * twos:2], tallies[2:2 + 2 * twos:2]
    margin = jnp.minimum(source_of - 1, limit - sink)
    passed = jax.random.randint(jax.random.fold_in(own_key, 1), (twos,), 0, 1 << 20) % (margin + 1)
    tallies = tallies.at[1:1 + 2 * twos:2].set(source_of - passed).at[2:2 + 2 * twos:2].set(sink + passed)
    return tallies[jax.random.permutation(jax.random.fold_in(own_key, 2), number_of)]


def gaussian(stream_key, dims, scale, reach, split=(), kind=jnp.bfloat16):
    drawn = jax.random.normal(stream_key, dims, jnp.float32) * scale
    if len(split) > 0:
        drawn = block_scale(stream_key, dims, split, -0.22, 0.18) * drawn
    return jnp.clip(drawn, min=-reach, max=reach).astype(kind)


def setup_inputs(seed: int = 0) -> dict:
    arg_keys = jax.random.split(jax.random.key(seed), 18)
    tokens = gaussian(arg_keys[0], (MICRO, ROW_TOKENS, D), 1.0, 6.0, ((1, 16),))
    segment_ids = jax.vmap(lambda own: jnp.searchsorted(jnp.cumsum(ragged(own, SEGS, SEQ, SEG_MOST, 1)), jnp.arange(SEQ), side="right"))(jax.random.split(arg_keys[1], MICRO * PACKED)).reshape((MICRO, PACKED, SEQ)).astype(jnp.int32)
    cotangent = gaussian(arg_keys[2], (MICRO, ROW_TOKENS, D), 1.0, 6.0, ((1, 16),))
    ln_gain = jnp.clip(1.0 + 0.1 * jax.random.normal(arg_keys[3], (LAYERS, 2, D), jnp.float32), 0.5, 1.5)
    ln_bias = gaussian(arg_keys[4], (LAYERS, 2, D), 0.3, 1.75, ((0, 2),), jnp.float32)
    w_qkv = gaussian(arg_keys[5], (LAYERS, D, 3, D), D ** -0.5, 0.1875, ((0, 2), (1, 8), (3, 2)), jnp.float32)
    query_key_value_bias = gaussian(arg_keys[6], (LAYERS, 3, D), 0.3, 1.75, ((0, 2), (2, 2)), jnp.float32)
    w_proj = gaussian(arg_keys[7], (LAYERS, D, D), (D // 64) ** -0.5, 1.5, ((0, 2), (1, 16)), jnp.float32)
    w_fc = gaussian(arg_keys[8], (LAYERS, D, FF), D ** -0.5, 0.1875, ((0, 2), (1, 8), (2, 2)), jnp.float32)
    fc_bias = gaussian(arg_keys[9], (LAYERS, FF), 0.3, 1.75, ((0, 2), (1, 2)), jnp.float32)
    w_fc2 = gaussian(arg_keys[10], (LAYERS, FF, D), FF ** -0.5, 0.09375, ((0, 2), (1, 16)), jnp.float32)
    out_bias = gaussian(arg_keys[11], (LAYERS, 2, D), 0.3, 1.75, ((0, 2),), jnp.float32)
    prefix_embed = gaussian(arg_keys[12], (PREF, D), 1.0, 6.0, (), jnp.float32)
    rep_w1 = gaussian(arg_keys[13], (D, MID), D ** -0.5, 0.1875, (), jnp.float32)
    rep_b1 = gaussian(arg_keys[14], (MID,), 0.3, 1.75, (), jnp.float32)
    rep_w2 = gaussian(arg_keys[15], (MID, LAYERS, 2, D), (MID // 4) ** -0.5, 0.5, ((1, 2), (3, 2)), jnp.float32)
    rep_b2 = gaussian(arg_keys[16], (LAYERS, 2, D), 0.3, 1.75, ((0, 2), (2, 2)), jnp.float32)
    return {"tokens": tokens, "segment_ids": segment_ids, "cotangent": cotangent, "ln_gain": ln_gain, "ln_bias": ln_bias, "w_qkv": w_qkv, "query_key_value_bias": query_key_value_bias, "w_proj": w_proj, "w_fc": w_fc, "fc_bias": fc_bias, "w_fc2": w_fc2, "out_bias": out_bias, "prefix_embed": prefix_embed, "rep_w1": rep_w1, "rep_b1": rep_b1, "rep_w2": rep_w2, "rep_b2": rep_b2}


EPSILON = 1e-05
NEGATIVE = -1000000000.0
HIGHEST = lax.Precision.HIGHEST

@jax.custom_vjp
def low(v):
    return lax.optimization_barrier(v.astype(jnp.bfloat16)).astype(jnp.float32)

@jax.custom_vjp
def low_back(v):
    return v

def low_keep(v):
    return (low(v), None)

def low_pass(kept, grad):
    return (grad,)

def back_keep(v):
    return (v, None)

def back_low(kept, grad):
    return (low(grad),)
low.defvjp(low_keep, low_pass)
low_back.defvjp(back_keep, back_low)

def layer_norm(values, norm_gain, norm_shift):
    centre = values - lax.optimization_barrier(jnp.mean(values, axis=-1, keepdims=True))
    spread = lax.optimization_barrier(jnp.mean(centre * centre, axis=-1, keepdims=True))
    return centre * lax.rsqrt(spread + EPSILON) * norm_gain + norm_shift

def allowed_of(segments):
    places = jnp.arange(segments.shape[0])
    return (segments[:, None] == segments[None, :]) & (places[:, None] >= places[None, :])

def block(inputs, allowed, model_parameters, prefix_key, prefix_val):
    norm_gains, shifts, w_joined, b_joined, w_out, w_up, b_up, w_down, b_both = model_parameters
    seq_len = inputs.shape[0]
    normed = low(layer_norm(inputs, norm_gains[0], shifts[0]))
    joined = jnp.einsum('sd,dce->sce', normed, w_joined, precision=HIGHEST) + b_joined
    queries = low_back(low(joined[:, 0])).reshape(seq_len, HEADS, HEAD)
    keys_tok = low_back(low(joined[:, 1])).reshape(seq_len, HEADS, HEAD)
    values_tok = low_back(low(joined[:, 2])).reshape(seq_len, HEADS, HEAD)
    keys_all = jnp.concatenate([prefix_key, keys_tok], axis=0)
    values_all = jnp.concatenate([prefix_val, values_tok], axis=0)
    scores = low_back(jnp.einsum('qhe,khe->hqk', queries, keys_all, precision=HIGHEST) * HEAD ** (-0.5))
    scores = jnp.where(allowed[None], scores, NEGATIVE)
    soft_probs = low(jax.nn.softmax(scores, axis=-1))
    context = jnp.einsum('hqk,khe->qhe', soft_probs, values_all, precision=HIGHEST).reshape(seq_len, D)
    context = low_back(low(context))
    attended = jnp.dot(context, w_out, precision=HIGHEST) + b_both[0]
    middle = inputs + low_back(attended)
    normed_two = low(layer_norm(middle, norm_gains[1], shifts[1]))
    hidden = low_back(jnp.dot(normed_two, w_up, precision=HIGHEST) + b_up)
    activated = low(jax.nn.gelu(hidden, approximate=True))
    branch_out = jnp.dot(activated, w_down, precision=HIGHEST) + b_both[1]
    return middle + low_back(branch_out)

def reference(tokens, segment_ids, cotangent, ln_gain, ln_bias, w_qkv, query_key_value_bias, w_proj, w_fc, fc_bias, w_fc2, out_bias, prefix_embed, rep_w1, rep_b1, rep_w2, rep_b2):
    layers = [(ln_gain[index], ln_bias[index], low(w_qkv[index]), query_key_value_bias[index], low(w_proj[index]), low(w_fc[index]), fc_bias[index], low(w_fc2[index]), out_bias[index]) for index in range(LAYERS)]
    row_count = MICRO * PACKED
    flat_tokens = tokens.astype(jnp.float32).reshape(row_count, SEQ, D)
    flat_segments = segment_ids.reshape(row_count, SEQ).astype(jnp.int32)
    flattened_cotangent = cotangent.astype(jnp.float32).reshape(row_count, SEQ, D)
    probes = jnp.zeros((LAYERS - 1, row_count, SEQ, D), jnp.float32)

    def forward(inputs, probe_all, embed_rows, weight_one, bias_one, weight_two, bias_two):
        rep_hidden = jnp.tanh(jnp.dot(embed_rows, weight_one, precision=HIGHEST) + bias_one)
        prefix = low(jnp.einsum('pm,mlcd->plcd', rep_hidden, weight_two, precision=HIGHEST) + bias_two)
        prefix = prefix.reshape(PREF, LAYERS, 2, HEADS, HEAD)

        def one_row(carried, operands):
            row_tokens, probe_rows, segments = operands
            allowed = jnp.concatenate([jnp.ones((SEQ, PREF), dtype=jnp.bool_), allowed_of(segments)], axis=1)
            current = row_tokens
            results = []
            for layer_index in range(LAYERS):
                if layer_index > 0:
                    current = low_back(low(current)) + probe_rows[layer_index - 1]
                current = block(current, allowed, layers[layer_index], carried[:, layer_index, 0], carried[:, layer_index, 1])
                results.append(current)
            return (carried, jnp.stack(results))
        _, stacked = lax.scan(jax.checkpoint(one_row), prefix, (inputs, jnp.moveaxis(probe_all, 1, 0), flat_segments))
        return stacked
    stacked, pull_back = jax.vjp(forward, flat_tokens, probes, prefix_embed, rep_w1, rep_b1, rep_w2, rep_b2)
    seed_grad = jnp.zeros_like(stacked).at[:, LAYERS - 1].set(flattened_cotangent)
    grads = pull_back(seed_grad)
    acts = jnp.moveaxis(stacked, 1, 0).reshape(LAYERS, MICRO, ROW_TOKENS, D)
    in_grads = jnp.concatenate([grads[0][None], grads[1]], axis=0).reshape(LAYERS, MICRO, ROW_TOKENS, D)
    return (acts, in_grads, grads[2], grads[3], grads[4], grads[5], grads[6])
```

```python
import functools

import jax
import jax.numpy as jnp
from jax import lax
from jax.experimental import pallas as pl
from jax.experimental.pallas import tpu as pltpu
from jax.sharding import PartitionSpec as P

HEAD = 64
EPSILON = 1e-05
NEGATIVE = -1000000000.0
HIGHEST = lax.Precision.HIGHEST
LOW = jnp.bfloat16
WIDE = jnp.float32
QB = 128
BAND = 256
KB = QB + BAND
PREP = 16


def swap(block, axis):
    return lax.ppermute(block, axis, [(0, 1), (1, 0)])


def layer_norm(values, gain, shift):
    centre = values - jnp.mean(values, axis=-1, keepdims=True)
    spread = jnp.mean(centre * centre, axis=-1, keepdims=True)
    return centre * lax.rsqrt(spread + EPSILON) * gain + shift


def norm_back(values, gain, grad):
    centre = values - jnp.mean(values, axis=-1, keepdims=True)
    inverse = lax.rsqrt(jnp.mean(centre * centre, axis=-1, keepdims=True) + EPSILON)
    normal = centre * inverse
    scaled = grad * gain
    return inverse * (
        scaled
        - jnp.mean(scaled, axis=-1, keepdims=True)
        - normal * jnp.mean(scaled * normal, axis=-1, keepdims=True)
    )


def gelu_parts(values):
    root = 0.7978845608028654
    square = values * values
    inner = jnp.tanh(root * values * (1.0 + 0.044715 * square))
    half = 0.5 * (1.0 + inner)
    slope = half + 0.5 * values * (1.0 - inner * inner) * root * (1.0 + 3 * 0.044715 * square)
    return values * half, slope


def dot_nn(left, right):
    return jnp.dot(left, right, preferred_element_type=WIDE)


def dot_nt(left, right):
    return lax.dot_general(left, right, (((1,), (1,)), ((), ())), preferred_element_type=WIDE)


def stacked(pair):
    lane = lax.broadcasted_iota(jnp.int32, pair.shape, 1)
    zero = jnp.zeros_like(pair)
    return jnp.concatenate(
        [jnp.where(lane < HEAD, pair, zero), jnp.where(lane >= HEAD, pair, zero)], axis=0
    )


def unstacked(both):
    row = lax.broadcasted_iota(jnp.int32, (2 * HEAD, QB), 0)
    return jnp.where(row < HEAD, both[:, :QB], both[:, QB:]).T


def fill_keys(scratch, prefix_ref, halo_ref, own_ref):
    scratch[:PREP] = prefix_ref[...]
    scratch[PREP : PREP + BAND] = halo_ref[...]
    scratch[PREP + BAND :] = own_ref[...]


def fill_turned(scratch, prefix_ref, halo_ref, own_ref):
    tokens = own_ref.shape[0]
    scratch[:, :BAND] = halo_ref[...].astype(WIDE).T.astype(LOW)
    scratch[:, BAND : BAND + tokens] = own_ref[...].astype(WIDE).T.astype(LOW)
    padded = jnp.concatenate(
        [prefix_ref[...].astype(WIDE), jnp.zeros((128 - PREP, 2 * HEAD), WIDE)], axis=0
    )
    scratch[:, BAND + tokens :] = padded.T.astype(LOW)


def masked_scores(queries, keys, start_ref, block, pref_count):
    pre = dot_nt(keys[:PREP], queries)
    pre = jnp.where(
        lax.broadcasted_iota(jnp.int32, pre.shape, 0) < pref_count, pre, NEGATIVE
    )
    band = dot_nt(keys[pl.ds(PREP + block * QB, KB)], queries)
    first = start_ref[:, block * QB : (block + 1) * QB] - block * QB
    first = jnp.concatenate([first, first], axis=1)
    last = lax.broadcasted_iota(jnp.int32, (1, 2 * QB), 1) % QB + BAND
    place = lax.broadcasted_iota(jnp.int32, band.shape, 0)
    band = jnp.where((place >= first) & (place <= last), band, NEGATIVE)
    return pre, band


def attend_kernel(pref_count, q_ref, k_ref, v_ref, hk_ref, hv_ref, pk_ref, pv_ref, start_ref,
                  c_ref, lse_ref, keys, turned):
    tokens = q_ref.shape[0]
    fill_keys(keys, pk_ref, hk_ref, k_ref)
    fill_turned(turned, pv_ref, hv_ref, v_ref)
    for block in range(tokens // QB):
        span = slice(block * QB, (block + 1) * QB)
        queries = stacked(q_ref[span, :] * jnp.asarray(HEAD ** (-0.5), LOW))
        pre, band = masked_scores(queries, keys, start_ref, block, pref_count)
        top = jnp.maximum(jnp.max(pre, axis=0, keepdims=True), jnp.max(band, axis=0, keepdims=True))
        pre = jnp.exp(pre - top)
        band = jnp.exp(band - top)
        total = jnp.sum(pre, axis=0, keepdims=True) + jnp.sum(band, axis=0, keepdims=True)
        lse_ref[0, block : block + 1, :] = top + jnp.log(total)
        inverse = 1.0 / total
        out = dot_nn(turned[:, block * QB : block * QB + KB], (band * inverse).astype(LOW))
        out = out + dot_nn(turned[:, BAND + tokens : BAND + tokens + PREP], (pre * inverse).astype(LOW))
        c_ref[span, :] = unstacked(out).astype(LOW)


def attend_back_kernel(pref_count, q_ref, k_ref, v_ref, hk_ref, hv_ref, pk_ref, pv_ref, start_ref,
                       lse_ref, dc_ref, dq_ref, dk_ref, dv_ref, dhk_ref, dhv_ref, dpk_ref, dpv_ref,
                       keys, vals, turned, dkeys, dvals):
    tokens = q_ref.shape[0]
    fill_keys(keys, pk_ref, hk_ref, k_ref)
    fill_keys(vals, pv_ref, hv_ref, v_ref)
    fill_turned(turned, pk_ref, hk_ref, k_ref)
    dkeys[...] = jnp.zeros_like(dkeys)
    dvals[...] = jnp.zeros_like(dvals)
    scaling = HEAD ** (-0.5)
    for block in range(tokens // QB):
        span = slice(block * QB, (block + 1) * QB)
        seen = pl.ds(PREP + block * QB, KB)
        queries = stacked(q_ref[span, :] * jnp.asarray(scaling, LOW))
        grads = stacked(dc_ref[span, :])
        pre, band = masked_scores(queries, keys, start_ref, block, pref_count)
        lse = lse_ref[0, block : block + 1, :]
        pre = jnp.exp(pre - lse)
        band = jnp.exp(band - lse)
        dpre = dot_nt(vals[:PREP], grads)
        dband = dot_nt(vals[seen], grads)
        inside = jnp.sum(pre * dpre, axis=0, keepdims=True) + jnp.sum(
            band * dband, axis=0, keepdims=True
        )
        dvals[:PREP] += dot_nn(pre.astype(LOW), grads)
        dvals[seen] += dot_nn(band.astype(LOW), grads)
        pre = (pre * (dpre - inside)).astype(LOW)
        band = (band * (dband - inside)).astype(LOW)
        dkeys[:PREP] += dot_nn(pre, queries)
        dkeys[seen] += dot_nn(band, queries)
        out = dot_nn(turned[:, block * QB : block * QB + KB], band)
        out = out + dot_nn(turned[:, BAND + tokens : BAND + tokens + PREP], pre)
        dq_ref[span, :] = (unstacked(out) * scaling).astype(LOW)
    dk_ref[...] = dkeys[PREP + BAND :].astype(LOW)
    dv_ref[...] = dvals[PREP + BAND :].astype(LOW)
    dhk_ref[...] = dkeys[PREP : PREP + BAND].astype(LOW)
    dhv_ref[...] = dvals[PREP : PREP + BAND].astype(LOW)
    dpk_ref[...] = dkeys[:PREP]
    dpv_ref[...] = dvals[:PREP]


def column(rows, offset):
    return pl.BlockSpec((rows, 2 * HEAD), lambda i: (0, offset + i))


def attention_specs(tokens, pairs):
    return [
        column(tokens, 0),
        column(tokens, pairs),
        column(tokens, 2 * pairs),
        column(BAND, 0),
        column(BAND, pairs),
        column(PREP, 0),
        column(PREP, pairs),
        pl.BlockSpec((1, tokens), lambda i: (0, 0)),
    ]


def attend(pref_count, qkv, halo, prefix, start):
    tokens, width = qkv.shape[0], qkv.shape[1] // 3
    pairs, blocks = width // (2 * HEAD), tokens // QB
    return pl.pallas_call(
        functools.partial(attend_kernel, pref_count),
        grid=(pairs,),
        in_specs=attention_specs(tokens, pairs),
        out_specs=[column(tokens, 0), pl.BlockSpec((1, blocks, 2 * QB), lambda i: (i, 0, 0))],
        out_shape=[
            jax.ShapeDtypeStruct((tokens, width), LOW),
            jax.ShapeDtypeStruct((pairs, blocks, 2 * QB), WIDE),
        ],
        scratch_shapes=[
            pltpu.VMEM((PREP + BAND + tokens, 2 * HEAD), LOW),
            pltpu.VMEM((2 * HEAD, BAND + tokens + 128), LOW),
        ],
        name="attend",
    )(qkv, qkv, qkv, halo, halo, prefix, prefix, start)


def attend_back(pref_count, qkv, halo, prefix, start, lse, grad):
    tokens, width = qkv.shape[0], qkv.shape[1] // 3
    pairs, blocks = width // (2 * HEAD), tokens // QB
    keys = PREP + BAND + tokens
    sizes = [(tokens, LOW)] * 3 + [(BAND, LOW)] * 2 + [(PREP, WIDE)] * 2
    return pl.pallas_call(
        functools.partial(attend_back_kernel, pref_count),
        grid=(pairs,),
        in_specs=attention_specs(tokens, pairs)
        + [pl.BlockSpec((1, blocks, 2 * QB), lambda i: (i, 0, 0)), column(tokens, 0)],
        out_specs=[column(rows, 0) for rows, _ in sizes],
        out_shape=[jax.ShapeDtypeStruct((rows, width), kind) for rows, kind in sizes],
        scratch_shapes=[
            pltpu.VMEM((keys, 2 * HEAD), LOW),
            pltpu.VMEM((keys, 2 * HEAD), LOW),
            pltpu.VMEM((2 * HEAD, BAND + tokens + 128), LOW),
            pltpu.VMEM((keys, 2 * HEAD), WIDE),
            pltpu.VMEM((keys, 2 * HEAD), WIDE),
        ],
        name="attend_back",
    )(qkv, qkv, qkv, halo, halo, prefix, prefix, start, lse, grad)


def block_forward(x, start, weights, small, pref_count):
    gains, shifts, biases = small["gain"], small["shift"], small["out"]
    normed = layer_norm(x, gains[0], shifts[0]).astype(LOW)
    qkv = [
        (dot_nn(normed, weights["qkv"][h]) + small["qkv"][h]).astype(LOW) for h in range(2)
    ]
    width = qkv[0].shape[1] // 3
    sent = [lax.ppermute(qkv[h][-BAND:, width:], "tensor", [(0, 1)]) for h in range(2)]
    halo = [sent[1], sent[0]]
    out = [attend(pref_count, qkv[h], halo[h], small["prefix"][h], start) for h in range(2)]
    middle = x + (
        dot_nn(out[0][0], weights["proj"][0]) + dot_nn(out[1][0], weights["proj"][1]) + biases[0]
    )
    normed_two = layer_norm(middle, gains[1], shifts[1]).astype(LOW)
    hidden, active = [], []
    for h in range(2):
        u = dot_nn(normed_two, weights["fc"][h]) + small["fc"][h]
        hidden.append(u.astype(LOW))
        active.append(gelu_parts(u)[0].astype(LOW))
    y = middle + (
        dot_nn(active[0], weights["fc2"][0]) + dot_nn(active[1], weights["fc2"][1]) + biases[1]
    )
    return y, (x, middle, qkv, halo, [o[1] for o in out], hidden)


def block_backward(stored, start, dy, weights, small, pref_count):
    x, middle, qkv, halo, lse, hidden = stored
    gains = small["gain"]
    low = dy.astype(LOW)
    dm = 0.0
    for h in range(2):
        slope = gelu_parts(hidden[h].astype(WIDE))[1]
        du = (dot_nt(low, weights["fc2"][h]) * slope).astype(LOW)
        dm = dm + dot_nt(du, weights["fc"][h])
    dh = dy + norm_back(middle, gains[1], dm)
    low = dh.astype(LOW)
    grads = []
    for h in range(2):
        dc = dot_nt(low, weights["proj"][h]).astype(LOW)
        grads.append(
            attend_back(pref_count, qkv[h], halo[h], small["prefix"][h], start, lse[h], dc)
        )
    sent = [
        [lax.ppermute(g, "tensor", [(1, 0)]) for g in grads[h][3:5]] for h in range(2)
    ]
    da = 0.0
    for h in range(2):
        dq, dk, dv = grads[h][:3]
        dk = dk.at[-BAND:].add(sent[1 - h][0])
        dv = dv.at[-BAND:].add(sent[1 - h][1])
        da = da + dot_nt(jnp.concatenate([dq, dk, dv], axis=1), weights["qkv"][h])
    dx = dh + norm_back(x, gains[0], da)
    return dx, [jnp.stack([grads[h][5], grads[h][6]]) for h in range(2)]


def gather_weights(shards):
    result = [{}, {}]
    for name, shard in shards.items():
        whole = lax.all_gather(shard, ("section", "rows"), axis=0, tiled=True)
        whole = whole.reshape(2, -1, shard.shape[1])
        far = swap(whole, "tensor")
        for layer in range(2):
            result[layer][name] = (whole[layer], far[layer])
    return result


def on_device(
    tokens,
    segment_ids,
    cotangent,
    ln_gain,
    ln_bias,
    w_qkv,
    query_key_value_bias,
    w_proj,
    w_fc,
    fc_bias,
    w_fc2,
    out_bias,
    prefix_embed,
    rep_w1,
    rep_b1,
    rep_w2,
    rep_b2,
):
    share, width = tokens.shape[1:]
    section, core = lax.axis_index("section"), lax.axis_index("tensor")
    rows_index, rows = lax.axis_index("rows"), lax.axis_size("rows")
    half = rep_w2.shape[-1]
    pref_count = prefix_embed.shape[0]

    shards = {
        "qkv": w_qkv[0].astype(LOW).reshape(w_qkv.shape[1], -1),
        "proj": w_proj[0].astype(LOW),
        "fc": w_fc[0].astype(LOW),
        "fc2": w_fc2[0].astype(LOW),
    }
    weights = gather_weights(shards)

    rep_hidden = jnp.tanh(jnp.dot(prefix_embed, rep_w1, precision=HIGHEST) + rep_b1)
    prefix = jnp.einsum("pm,mcd->pcd", rep_hidden, rep_w2[:, 0], precision=HIGHEST) + rep_b2[0]
    prefix = prefix.astype(LOW).astype(WIDE)
    prefix = jnp.pad(prefix, ((0, PREP - pref_count), (0, 0), (0, 0)))
    parts = [ln_gain[0], ln_bias[0], out_bias[0], query_key_value_bias[0], fc_bias[0], prefix]
    packed = jnp.concatenate([part.reshape(-1) for part in parts])
    packed = lax.all_gather(packed, ("section", "tensor"), axis=0).reshape(2, 2, -1)
    packed = jnp.where(core == 0, packed, packed[:, ::-1])
    smalls = []
    for layer in range(2):
        cut, place = [], 0
        for part in parts:
            cut.append([packed[layer, h, place : place + part.size].reshape(part.shape) for h in range(2)])
            place += part.size
        smalls.append(
            {
                "gain": cut[0][0],
                "shift": cut[1][0],
                "out": cut[2][0],
                "qkv": [cut[3][h].reshape(-1) for h in range(2)],
                "fc": cut[4],
                "prefix": [cut[5][h].reshape(PREP, -1).astype(LOW) for h in range(2)],
            }
        )

    own = section
    segments = lax.dynamic_index_in_dim(segment_ids, own, 0, keepdims=False).reshape(-1)
    mine = lax.dynamic_slice_in_dim(segments, core * share, share)
    start = jnp.sum(segments[:, None] < mine[None, :], axis=0, dtype=jnp.int32)
    start = (start - core * share + BAND)[None]

    x = lax.dynamic_index_in_dim(tokens, own, 0, keepdims=False).astype(WIDE)
    y0, kept0 = block_forward(x, start, weights[0], smalls[0], pref_count)
    x1 = y0.astype(LOW).astype(WIDE)
    y1, kept1 = block_forward(x1, start, weights[1], smalls[1], pref_count)
    dy = lax.dynamic_index_in_dim(cotangent, own, 0, keepdims=False).astype(WIDE)
    g1, pre1 = block_backward(kept1, start, dy, weights[1], smalls[1], pref_count)
    g0, pre0 = block_backward(
        kept0, start, g1.astype(LOW).astype(WIDE), weights[0], smalls[0], pref_count
    )

    def settle(first, second):
        keep = jnp.where(section == 0, first, second)
        send = jnp.where(section == 0, second, first).astype(LOW)
        got = swap(send, "section").astype(WIDE)
        return jnp.where(section == 0, jnp.stack([keep, got]), jnp.stack([got, keep]))[None]

    acts = settle(y0, y1)
    in_grads = settle(g0, g1)

    terms = jnp.stack([jnp.stack(pre0), jnp.stack(pre1)])
    keep = lax.dynamic_index_in_dim(terms, section, 0, keepdims=False)
    send = lax.dynamic_index_in_dim(terms, 1 - section, 0, keepdims=False)
    layer_terms = keep + swap(send, "section")
    total = layer_terms[0] + swap(layer_terms[1], "tensor")
    total = lax.psum(total[:, :pref_count], "rows")
    total = jnp.swapaxes(total, 0, 1)
    grad_b2 = jnp.sum(total, axis=0)
    mid_part = rep_w1.shape[1] // rows
    width_part = width // rows
    hidden_part = lax.dynamic_slice_in_dim(rep_hidden, rows_index * mid_part, mid_part, 1)
    grad_w2 = jnp.einsum("pm,pcd->mcd", hidden_part, total, precision=HIGHEST)
    hidden_term = jnp.einsum("pcd,mcd->pm", total, rep_w2[:, 0], precision=HIGHEST)
    grad_hidden = lax.psum(hidden_term, ("section", "tensor"))
    grad_pre = grad_hidden * (1.0 - rep_hidden * rep_hidden)
    grad_b1 = jnp.sum(grad_pre, axis=0)
    embed_part = lax.dynamic_slice_in_dim(prefix_embed, rows_index * width_part, width_part, 1)
    grad_w1 = jnp.einsum("pd,pm->dm", embed_part, grad_pre, precision=HIGHEST)
    weight_part = lax.dynamic_slice_in_dim(rep_w1, rows_index * width_part, width_part, 0)
    grad_embed = jnp.einsum("pm,dm->pd", grad_pre, weight_part, precision=HIGHEST)
    return (acts, in_grads, grad_embed, grad_w1, grad_b1, grad_w2[:, None], grad_b2[None])


def solution(mesh):
    return jax.shard_map(
        on_device,
        mesh=mesh,
        in_specs=(
            P(None, ("rows", "tensor"), None),
            P(None, "rows", None),
            P(None, ("rows", "tensor"), None),
            P("section", None, None),
            P("section", None, None),
            P("section", "rows", None, "tensor"),
            P("section", None, "tensor"),
            P("section", ("tensor", "rows"), None),
            P("section", "rows", "tensor"),
            P("section", "tensor"),
            P("section", ("tensor", "rows"), None),
            P("section", None, None),
            P(),
            P(),
            P(),
            P(None, "section", None, "tensor"),
            P("section", None, "tensor"),
        ),
        out_specs=(
            P("section", None, ("rows", "tensor"), None),
            P("section", None, ("rows", "tensor"), None),
            P(None, "rows"),
            P("rows", None),
            P(),
            P("rows", "section", None, "tensor"),
            P("section", None, "tensor"),
        ),
        check_vma=False,
    )
```

```python
import functools

import jax
import jax.numpy as jnp
from jax import lax
from jax.experimental import pallas as pl
from jax.experimental.pallas import tpu as pltpu
from jax.sharding import PartitionSpec as P

HEAD = 64
EPSILON = 1e-05
NEGATIVE = -1000000000.0
HIGHEST = lax.Precision.HIGHEST
LOW = jnp.bfloat16
WIDE = jnp.float32
QB = 128
BAND = 256
KB = QB + BAND
PREP = 16


def swap(block, axis):
    return lax.ppermute(block, axis, [(0, 1), (1, 0)])


def layer_norm(values, gain, shift):
    centre = values - jnp.mean(values, axis=-1, keepdims=True)
    spread = jnp.mean(centre * centre, axis=-1, keepdims=True)
    return centre * lax.rsqrt(spread + EPSILON) * gain + shift


def norm_back(values, gain, grad):
    centre = values - jnp.mean(values, axis=-1, keepdims=True)
    inverse = lax.rsqrt(jnp.mean(centre * centre, axis=-1, keepdims=True) + EPSILON)
    normal = centre * inverse
    scaled = grad * gain
    return inverse * (
        scaled
        - jnp.mean(scaled, axis=-1, keepdims=True)
        - normal * jnp.mean(scaled * normal, axis=-1, keepdims=True)
    )


def gelu_parts(values):
    root = 0.7978845608028654
    square = values * values
    inner = jnp.tanh(root * values * (1.0 + 0.044715 * square))
    half = 0.5 * (1.0 + inner)
    slope = half + 0.5 * values * (1.0 - inner * inner) * root * (1.0 + 3 * 0.044715 * square)
    return values * half, slope


def dot_nn(left, right):
    return jnp.dot(left, right, preferred_element_type=WIDE)


def dot_nt(left, right):
    return lax.dot_general(left, right, (((1,), (1,)), ((), ())), preferred_element_type=WIDE)


def stacked(pair):
    lane = lax.broadcasted_iota(jnp.int32, pair.shape, 1)
    zero = jnp.zeros_like(pair)
    return jnp.concatenate(
        [jnp.where(lane < HEAD, pair, zero), jnp.where(lane >= HEAD, pair, zero)], axis=0
    )


def unstacked(both):
    row = lax.broadcasted_iota(jnp.int32, (2 * HEAD, QB), 0)
    return jnp.where(row < HEAD, both[:, :QB], both[:, QB:]).T


def fill_keys(scratch, prefix_ref, halo_ref, own_ref):
    scratch[:PREP] = prefix_ref[...]
    scratch[PREP : PREP + BAND] = halo_ref[...]
    scratch[PREP + BAND :] = own_ref[...]


def fill_turned(scratch, prefix_ref, halo_ref, own_ref):
    tokens = own_ref.shape[0]
    scratch[:, :BAND] = halo_ref[...].astype(WIDE).T.astype(LOW)
    scratch[:, BAND : BAND + tokens] = own_ref[...].astype(WIDE).T.astype(LOW)
    padded = jnp.concatenate(
        [prefix_ref[...].astype(WIDE), jnp.zeros((128 - PREP, 2 * HEAD), WIDE)], axis=0
    )
    scratch[:, BAND + tokens :] = padded.T.astype(LOW)


def masked_scores(queries, keys, start_ref, block, pref_count):
    pre = dot_nt(keys[:PREP], queries)
    pre = jnp.where(
        lax.broadcasted_iota(jnp.int32, pre.shape, 0) < pref_count, pre, NEGATIVE
    )
    band = dot_nt(keys[pl.ds(PREP + block * QB, KB)], queries)
    first = start_ref[:, block * QB : (block + 1) * QB] - block * QB
    first = jnp.concatenate([first, first], axis=1)
    last = lax.broadcasted_iota(jnp.int32, (1, 2 * QB), 1) % QB + BAND
    place = lax.broadcasted_iota(jnp.int32, band.shape, 0)
    band = jnp.where((place >= first) & (place <= last), band, NEGATIVE)
    return pre, band


def attend_kernel(pref_count, q_ref, k_ref, v_ref, hk_ref, hv_ref, pk_ref, pv_ref, start_ref,
                  c_ref, lse_ref, keys, turned):
    tokens = q_ref.shape[0]
    fill_keys(keys, pk_ref, hk_ref, k_ref)
    fill_turned(turned, pv_ref, hv_ref, v_ref)
    for block in range(tokens // QB):
        span = slice(block * QB, (block + 1) * QB)
        queries = stacked(q_ref[span, :] * jnp.asarray(HEAD ** (-0.5), LOW))
        pre, band = masked_scores(queries, keys, start_ref, block, pref_count)
        top = jnp.maximum(jnp.max(pre, axis=0, keepdims=True), jnp.max(band, axis=0, keepdims=True))
        pre = jnp.exp(pre - top)
        band = jnp.exp(band - top)
        total = jnp.sum(pre, axis=0, keepdims=True) + jnp.sum(band, axis=0, keepdims=True)
        lse_ref[0, block : block + 1, :] = top + jnp.log(total)
        inverse = 1.0 / total
        out = dot_nn(turned[:, block * QB : block * QB + KB], (band * inverse).astype(LOW))
        out = out + dot_nn(turned[:, BAND + tokens : BAND + tokens + PREP], (pre * inverse).astype(LOW))
        c_ref[span, :] = unstacked(out).astype(LOW)


def attend_back_kernel(pref_count, q_ref, k_ref, v_ref, hk_ref, hv_ref, pk_ref, pv_ref, start_ref,
                       lse_ref, dc_ref, dq_ref, dk_ref, dv_ref, dhk_ref, dhv_ref, dpk_ref, dpv_ref,
                       keys, vals, turned, dkeys, dvals):
    tokens = q_ref.shape[0]
    fill_keys(keys, pk_ref, hk_ref, k_ref)
    fill_keys(vals, pv_ref, hv_ref, v_ref)
    fill_turned(turned, pk_ref, hk_ref, k_ref)
    dkeys[...] = jnp.zeros_like(dkeys)
    dvals[...] = jnp.zeros_like(dvals)
    scaling = HEAD ** (-0.5)
    for block in range(tokens // QB):
        span = slice(block * QB, (block + 1) * QB)
        seen = pl.ds(PREP + block * QB, KB)
        queries = stacked(q_ref[span, :] * jnp.asarray(scaling, LOW))
        grads = stacked(dc_ref[span, :])
        pre, band = masked_scores(queries, keys, start_ref, block, pref_count)
        lse = lse_ref[0, block : block + 1, :]
        pre = jnp.exp(pre - lse)
        band = jnp.exp(band - lse)
        dpre = dot_nt(vals[:PREP], grads)
        dband = dot_nt(vals[seen], grads)
        inside = jnp.sum(pre * dpre, axis=0, keepdims=True) + jnp.sum(
            band * dband, axis=0, keepdims=True
        )
        dvals[:PREP] += dot_nn(pre.astype(LOW), grads)
        dvals[seen] += dot_nn(band.astype(LOW), grads)
        pre = (pre * (dpre - inside)).astype(LOW)
        band = (band * (dband - inside)).astype(LOW)
        dkeys[:PREP] += dot_nn(pre, queries)
        dkeys[seen] += dot_nn(band, queries)
        out = dot_nn(turned[:, block * QB : block * QB + KB], band)
        out = out + dot_nn(turned[:, BAND + tokens : BAND + tokens + PREP], pre)
        dq_ref[span, :] = (unstacked(out) * scaling).astype(LOW)
    dk_ref[...] = dkeys[PREP + BAND :].astype(LOW)
    dv_ref[...] = dvals[PREP + BAND :].astype(LOW)
    dhk_ref[...] = dkeys[PREP : PREP + BAND].astype(LOW)
    dhv_ref[...] = dvals[PREP : PREP + BAND].astype(LOW)
    dpk_ref[...] = dkeys[:PREP]
    dpv_ref[...] = dvals[:PREP]


def column(rows, offset):
    return pl.BlockSpec((rows, 2 * HEAD), lambda i: (0, offset + i))


def attention_specs(tokens, pairs):
    return [
        column(tokens, 0),
        column(tokens, pairs),
        column(tokens, 2 * pairs),
        column(BAND, 0),
        column(BAND, pairs),
        column(PREP, 0),
        column(PREP, pairs),
        pl.BlockSpec((1, tokens), lambda i: (0, 0)),
    ]


def attend(pref_count, qkv, halo, prefix, start):
    tokens, width = qkv.shape[0], qkv.shape[1] // 3
    pairs, blocks = width // (2 * HEAD), tokens // QB
    return pl.pallas_call(
        functools.partial(attend_kernel, pref_count),
        grid=(pairs,),
        in_specs=attention_specs(tokens, pairs),
        out_specs=[column(tokens, 0), pl.BlockSpec((1, blocks, 2 * QB), lambda i: (i, 0, 0))],
        out_shape=[
            jax.ShapeDtypeStruct((tokens, width), LOW),
            jax.ShapeDtypeStruct((pairs, blocks, 2 * QB), WIDE),
        ],
        scratch_shapes=[
            pltpu.VMEM((PREP + BAND + tokens, 2 * HEAD), LOW),
            pltpu.VMEM((2 * HEAD, BAND + tokens + 128), LOW),
        ],
        name="attend",
    )(qkv, qkv, qkv, halo, halo, prefix, prefix, start)


def attend_back(pref_count, qkv, halo, prefix, start, lse, grad):
    tokens, width = qkv.shape[0], qkv.shape[1] // 3
    pairs, blocks = width // (2 * HEAD), tokens // QB
    keys = PREP + BAND + tokens
    sizes = [(tokens, LOW)] * 3 + [(BAND, LOW)] * 2 + [(PREP, WIDE)] * 2
    return pl.pallas_call(
        functools.partial(attend_back_kernel, pref_count),
        grid=(pairs,),
        in_specs=attention_specs(tokens, pairs)
        + [pl.BlockSpec((1, blocks, 2 * QB), lambda i: (i, 0, 0)), column(tokens, 0)],
        out_specs=[column(rows, 0) for rows, _ in sizes],
        out_shape=[jax.ShapeDtypeStruct((rows, width), kind) for rows, kind in sizes],
        scratch_shapes=[
            pltpu.VMEM((keys, 2 * HEAD), LOW),
            pltpu.VMEM((keys, 2 * HEAD), LOW),
            pltpu.VMEM((2 * HEAD, BAND + tokens + 128), LOW),
            pltpu.VMEM((keys, 2 * HEAD), WIDE),
            pltpu.VMEM((keys, 2 * HEAD), WIDE),
        ],
        name="attend_back",
    )(qkv, qkv, qkv, halo, halo, prefix, prefix, start, lse, grad)


def block_forward(x, start, weights, small, pref_count):
    gains, shifts, biases = small["gain"], small["shift"], small["out"]
    normed = layer_norm(x, gains[0], shifts[0]).astype(LOW)
    qkv = [
        (dot_nn(normed, weights["qkv"][h]) + small["qkv"][h]).astype(LOW) for h in range(2)
    ]
    width = qkv[0].shape[1] // 3
    sent = [lax.ppermute(qkv[h][-BAND:, width:], "tensor", [(0, 1)]) for h in range(2)]
    halo = [sent[1], sent[0]]
    out = [attend(pref_count, qkv[h], halo[h], small["prefix"][h], start) for h in range(2)]
    middle = x + (
        dot_nn(out[0][0], weights["proj"][0]) + dot_nn(out[1][0], weights["proj"][1]) + biases[0]
    )
    normed_two = layer_norm(middle, gains[1], shifts[1]).astype(LOW)
    hidden, active = [], []
    for h in range(2):
        u = dot_nn(normed_two, weights["fc"][h]) + small["fc"][h]
        hidden.append(u.astype(LOW))
        active.append(gelu_parts(u)[0].astype(LOW))
    y = middle + (
        dot_nn(active[0], weights["fc2"][0]) + dot_nn(active[1], weights["fc2"][1]) + biases[1]
    )
    return y, (x, middle, qkv, halo, [o[1] for o in out], hidden)


def block_backward(stored, start, dy, weights, small, pref_count):
    x, middle, qkv, halo, lse, hidden = stored
    gains = small["gain"]
    low = dy.astype(LOW)
    dm = 0.0
    for h in range(2):
        slope = gelu_parts(hidden[h].astype(WIDE))[1]
        du = (dot_nt(low, weights["fc2"][h]) * slope).astype(LOW)
        dm = dm + dot_nt(du, weights["fc"][h])
    dh = dy + norm_back(middle, gains[1], dm)
    low = dh.astype(LOW)
    grads = []
    for h in range(2):
        dc = dot_nt(low, weights["proj"][h]).astype(LOW)
        grads.append(
            attend_back(pref_count, qkv[h], halo[h], small["prefix"][h], start, lse[h], dc)
        )
    sent = [
        [lax.ppermute(g, "tensor", [(1, 0)]) for g in grads[h][3:5]] for h in range(2)
    ]
    da = 0.0
    for h in range(2):
        dq, dk, dv = grads[h][:3]
        dk = dk.at[-BAND:].add(sent[1 - h][0])
        dv = dv.at[-BAND:].add(sent[1 - h][1])
        da = da + dot_nt(jnp.concatenate([dq, dk, dv], axis=1), weights["qkv"][h])
    dx = dh + norm_back(x, gains[0], da)
    return dx, [jnp.stack([grads[h][5], grads[h][6]]) for h in range(2)]


ORDER = (
    ("x", "qkv", "qkvx"),
    ("y", "proj", "projy"),
    ("z", "qkv", "qkvz"),
    ("y", "fc", "fcy"),
    ("x", "fc2", "fc2x"),
    ("z", "fc2", "fc2z"),
    ("x", "proj&", "proj&x"),
    ("y", "qkv&", "qkv&y"),
    ("z", "qkvz", "qkvzz"),
    ("x", "qkvz", "qkvzx"),
    ("y", "fc2&", "fc2&y"),
    ("x", "fcL0", "fcL0x"),
    ("z", "proj&&", "proj&&z"),
    ("z", "qkvzz", "qkvzzz"),
    ("x", "qkvzz", "qkvzzx"),
    ("y", "qkvz&", "qkvz&y"),
    ("x", "fcL1", "fcL1x"),
    ("z", "proj&&z", "proj&&zz"),
    ("x", "qkvzzz", "qkvzzzx"),
    ("y", "qkvzz&", "qkvzz&y"),
    ("z", "fc2z", "fc2zz"),
    ("z", "fcL0", "fcL0z"),
    ("x", "fc2z", "fc2zx"),
    ("y", "qkvzzz&", "qkvzzz&y"),
    ("x", "fc2zz", "fc2zzx"),
    ("z", "fc2zz", "fc2zzz"),
    ("y", "fc2z&", "fc2z&y"),
    ("x", "fcL0z", "fcL0zx"),
    ("z", "fcL0z", "fcL0zz"),
    ("x", "fc2zzz", "fc2zzzx"),
    ("z", "fcL1", "fcL1z"),
    ("y", "fc2zz&", "fc2zz&y"),
    ("x", "fcL0zz", "fcL0zzx"),
    ("z", "fcL0zz", "fcL0zzz"),
    ("x", "fcL1z", "fcL1zx"),
    ("z", "fcL1z", "fcL1zz"),
    ("y", "fc2zzz&", "fc2zzz&y"),
    ("x", "fcL0zzz", "fcL0zzzx"),
    ("z", "proj&&zz", "proj&&zzz"),
    ("z", "fcL1zz", "fcL1zzz"),
    ("x", "fcL1zz", "fcL1zzx"),
    ("x", "fcL1zzz", "fcL1zzzx"),
)
JOINED = {"proj&": ("proj", "projy"), "proj&&": ("proj&", "proj&x")}
DEEP = 2


def move(block, link):
    if link == "y":
        return swap(block, "section")
    count = lax.axis_size("rows")
    if link == "x":
        return lax.ppermute(block, "rows", [(i, i ^ 1) for i in range(count)])
    return lax.ppermute(block, "rows", [(i, (i + 2) % count) for i in range(count)])


def spread(shards, section):
    held, sent = dict(shards), {}

    def get(name):
        if name not in held:
            if name in JOINED:
                parts = JOINED[name]
            elif name.endswith("&"):
                parts = (name[:-1], name[:-1] + "x")
            else:
                held[name] = jnp.where(section == int(name[-1]), held["fc"], held["fcy"])
                return held[name]
            held[name] = jnp.concatenate([get(part) for part in parts], axis=0)
        return held[name]

    for link, source, target in ORDER:
        block, ahead = get(source), sent.setdefault(link, [])
        if len(ahead) >= DEEP:
            block, _ = lax.optimization_barrier((block, ahead[-DEEP]))
        held[target] = move(block, link)
        ahead.append(held[target])
    return get, held


def pieces(name, layer):
    result = []
    for steps in range(4):
        moved = "z" * steps
        for other in range(2):
            if name == "proj":
                base = "proj&&" + moved
                result.append((steps, other, (base, 2 * other), (base, 2 * other + 1)))
            elif name == "fc":
                base = "fcL%d%s%s" % (layer, moved, "x" * other)
                result.append((steps, other, (base, 0), (base, 0)))
            else:
                base = name + moved + "&"
                result.append((steps, other, (base, other), (base + "y", other)))
    return result


def join_kernel(plan, layer, rows, place_ref, *refs):
    buffers, (out_ref, sems) = refs[:-2], refs[-2:]
    section, z, x = place_ref[0], place_ref[1], place_ref[2]

    def copy(index, source):
        steps, other = plan[index][:2]
        slot = ((z + 4 - steps) % 4) * 2 + (x + other) % 2
        buffer, block = source
        return pltpu.make_async_copy(
            buffers[buffer].at[block * rows : (block + 1) * rows], out_ref.at[slot], sems.at[index]
        )

    @pl.when(section == layer)
    def _():
        for index, entry in enumerate(plan):
            copy(index, entry[2]).start()

    @pl.when(section != layer)
    def _():
        for index, entry in enumerate(plan):
            copy(index, entry[3]).start()

    for index, entry in enumerate(plan):
        copy(index, entry[2]).wait()


def joined(name, layer, get, shape, place):
    rows, columns = shape
    names, plan = [], []
    for steps, other, *sources in pieces(name, layer):
        spots = []
        for buffer, block in sources:
            if buffer not in names:
                names.append(buffer)
            spots.append((names.index(buffer), block))
        plan.append((steps, other, *spots))
    anywhere = pl.BlockSpec(memory_space=pl.ANY)
    whole = pl.pallas_call(
        functools.partial(join_kernel, plan, layer, rows),
        in_specs=[pl.BlockSpec(memory_space=pltpu.SMEM)] + [anywhere] * len(names),
        out_specs=anywhere,
        out_shape=jax.ShapeDtypeStruct((8, rows, columns), LOW),
        scratch_shapes=[pltpu.SemaphoreType.DMA((8,))],
        name="join_" + name,
    )(place, *[get(buffer) for buffer in names])
    return whole.reshape(8 * rows, columns)


def gather_weights(shards):
    result = [{}, {}]
    section, rows = lax.axis_index("section"), lax.axis_index("rows")
    if lax.axis_size("rows") == 8:
        get, _ = spread(shards, section)
        place = jnp.stack([section, rows // 2, rows % 2]).astype(jnp.int32)
        for layer in range(2):
            for name, shard in shards.items():
                whole = joined(name, layer, get, shard.shape, place)
                result[layer][name] = (whole, swap(whole, "tensor"))
        return result
    for name, shard in shards.items():
        whole = lax.all_gather(shard, ("section", "rows"), axis=0, tiled=True)
        whole = whole.reshape(2, -1, shard.shape[1])
        far = swap(whole, "tensor")
        for layer in range(2):
            result[layer][name] = (whole[layer], far[layer])
    return result


def on_device(
    tokens,
    segment_ids,
    cotangent,
    ln_gain,
    ln_bias,
    w_qkv,
    query_key_value_bias,
    w_proj,
    w_fc,
    fc_bias,
    w_fc2,
    out_bias,
    prefix_embed,
    rep_w1,
    rep_b1,
    rep_w2,
    rep_b2,
):
    share, width = tokens.shape[1:]
    section, core = lax.axis_index("section"), lax.axis_index("tensor")
    rows_index, rows = lax.axis_index("rows"), lax.axis_size("rows")
    half = rep_w2.shape[-1]
    pref_count = prefix_embed.shape[0]

    shards = {
        "qkv": w_qkv[0].astype(LOW).reshape(w_qkv.shape[1], -1),
        "proj": w_proj[0].astype(LOW),
        "fc": w_fc[0].astype(LOW),
        "fc2": w_fc2[0].astype(LOW),
    }
    weights = gather_weights(shards)

    rep_hidden = jnp.tanh(jnp.dot(prefix_embed, rep_w1, precision=HIGHEST) + rep_b1)
    prefix = jnp.einsum("pm,mcd->pcd", rep_hidden, rep_w2[:, 0], precision=HIGHEST) + rep_b2[0]
    prefix = prefix.astype(LOW).astype(WIDE)
    prefix = jnp.pad(prefix, ((0, PREP - pref_count), (0, 0), (0, 0)))
    parts = [ln_gain[0], ln_bias[0], out_bias[0], query_key_value_bias[0], fc_bias[0], prefix]
    packed = jnp.concatenate([part.reshape(-1) for part in parts])
    packed = lax.all_gather(packed, ("section", "tensor"), axis=0).reshape(2, 2, -1)
    packed = jnp.where(core == 0, packed, packed[:, ::-1])
    smalls = []
    for layer in range(2):
        cut, place = [], 0
        for part in parts:
            cut.append([packed[layer, h, place : place + part.size].reshape(part.shape) for h in range(2)])
            place += part.size
        smalls.append(
            {
                "gain": cut[0][0],
                "shift": cut[1][0],
                "out": cut[2][0],
                "qkv": [cut[3][h].reshape(-1) for h in range(2)],
                "fc": cut[4],
                "prefix": [cut[5][h].reshape(PREP, -1).astype(LOW) for h in range(2)],
            }
        )

    own = section
    segments = lax.dynamic_index_in_dim(segment_ids, own, 0, keepdims=False).reshape(-1)
    mine = lax.dynamic_slice_in_dim(segments, core * share, share)
    start = jnp.sum(segments[:, None] < mine[None, :], axis=0, dtype=jnp.int32)
    start = (start - core * share + BAND)[None]

    x = lax.dynamic_index_in_dim(tokens, own, 0, keepdims=False).astype(WIDE)
    y0, kept0 = block_forward(x, start, weights[0], smalls[0], pref_count)
    x1 = y0.astype(LOW).astype(WIDE)
    y1, kept1 = block_forward(x1, start, weights[1], smalls[1], pref_count)
    dy = lax.dynamic_index_in_dim(cotangent, own, 0, keepdims=False).astype(WIDE)
    g1, pre1 = block_backward(kept1, start, dy, weights[1], smalls[1], pref_count)
    g0, pre0 = block_backward(
        kept0, start, g1.astype(LOW).astype(WIDE), weights[0], smalls[0], pref_count
    )

    def settle(first, second):
        keep = jnp.where(section == 0, first, second)
        send = jnp.where(section == 0, second, first).astype(LOW)
        got = swap(send, "section").astype(WIDE)
        return jnp.where(section == 0, jnp.stack([keep, got]), jnp.stack([got, keep]))[None]

    acts = settle(y0, y1)
    in_grads = settle(g0, g1)

    terms = jnp.stack([jnp.stack(pre0), jnp.stack(pre1)])
    keep = lax.dynamic_index_in_dim(terms, section, 0, keepdims=False)
    send = lax.dynamic_index_in_dim(terms, 1 - section, 0, keepdims=False)
    layer_terms = keep + swap(send, "section")
    total = layer_terms[0] + swap(layer_terms[1], "tensor")
    total = lax.psum(total[:, :pref_count], "rows")
    total = jnp.swapaxes(total, 0, 1)
    grad_b2 = jnp.sum(total, axis=0)
    mid_part = rep_w1.shape[1] // rows
    width_part = width // rows
    hidden_part = lax.dynamic_slice_in_dim(rep_hidden, rows_index * mid_part, mid_part, 1)
    grad_w2 = jnp.einsum("pm,pcd->mcd", hidden_part, total, precision=HIGHEST)
    hidden_term = jnp.einsum("pcd,mcd->pm", total, rep_w2[:, 0], precision=HIGHEST)
    grad_hidden = lax.psum(hidden_term, ("section", "tensor"))
    grad_pre = grad_hidden * (1.0 - rep_hidden * rep_hidden)
    grad_b1 = jnp.sum(grad_pre, axis=0)
    embed_part = lax.dynamic_slice_in_dim(prefix_embed, rows_index * width_part, width_part, 1)
    grad_w1 = jnp.einsum("pd,pm->dm", embed_part, grad_pre, precision=HIGHEST)
    weight_part = lax.dynamic_slice_in_dim(rep_w1, rows_index * width_part, width_part, 0)
    grad_embed = jnp.einsum("pm,dm->pd", grad_pre, weight_part, precision=HIGHEST)
    return (acts, in_grads, grad_embed, grad_w1, grad_b1, grad_w2[:, None], grad_b2[None])


def solution(mesh):
    return jax.shard_map(
        on_device,
        mesh=mesh,
        in_specs=(
            P(None, ("rows", "tensor"), None),
            P(None, "rows", None),
            P(None, ("rows", "tensor"), None),
            P("section", None, None),
            P("section", None, None),
            P("section", "rows", None, "tensor"),
            P("section", None, "tensor"),
            P("section", ("tensor", "rows"), None),
            P("section", "rows", "tensor"),
            P("section", "tensor"),
            P("section", ("tensor", "rows"), None),
            P("section", None, None),
            P(),
            P(),
            P(),
            P(None, "section", None, "tensor"),
            P("section", None, "tensor"),
        ),
        out_specs=(
            P("section", None, ("rows", "tensor"), None),
            P("section", None, ("rows", "tensor"), None),
            P(None, "rows"),
            P("rows", None),
            P(),
            P("rows", "section", None, "tensor"),
            P("section", None, "tensor"),
        ),
        check_vma=False,
    )
```

```python
import functools

import jax
import jax.numpy as jnp
from jax import lax
from jax.experimental import pallas as pl
from jax.experimental.pallas import tpu as pltpu
from jax.sharding import PartitionSpec as P

HEAD = 64
EPSILON = 1e-05
NEGATIVE = -1000000000.0
HIGHEST = lax.Precision.HIGHEST
LOW = jnp.bfloat16
WIDE = jnp.float32
QB = 128
BAND = 256
KB = QB + BAND
PREP = 16


def swap(block, axis):
    return lax.ppermute(block, axis, [(0, 1), (1, 0)])


def all_sum(block, axes):
    for axis in axes:
        count = lax.axis_size(axis)
        if count & (count - 1):
            block = lax.psum(block, axis)
            continue
        bit = 1
        while bit < count:
            block = block + lax.ppermute(block, axis, [(i, i ^ bit) for i in range(count)])
            bit *= 2
    return block


def layer_norm(values, gain, shift):
    centre = values - jnp.mean(values, axis=-1, keepdims=True)
    spread = jnp.mean(centre * centre, axis=-1, keepdims=True)
    return centre * lax.rsqrt(spread + EPSILON) * gain + shift


def norm_back(values, gain, grad):
    centre = values - jnp.mean(values, axis=-1, keepdims=True)
    inverse = lax.rsqrt(jnp.mean(centre * centre, axis=-1, keepdims=True) + EPSILON)
    normal = centre * inverse
    scaled = grad * gain
    return inverse * (
        scaled
        - jnp.mean(scaled, axis=-1, keepdims=True)
        - normal * jnp.mean(scaled * normal, axis=-1, keepdims=True)
    )


def gelu_parts(values):
    root = 0.7978845608028654
    square = values * values
    inner = jnp.tanh(root * values * (1.0 + 0.044715 * square))
    half = 0.5 * (1.0 + inner)
    slope = half + 0.5 * values * (1.0 - inner * inner) * root * (1.0 + 3 * 0.044715 * square)
    return values * half, slope


def dot_nn(left, right):
    return jnp.dot(left, right, preferred_element_type=WIDE)


def dot_nt(left, right):
    return lax.dot_general(left, right, (((1,), (1,)), ((), ())), preferred_element_type=WIDE)


def stacked(pair):
    lane = lax.broadcasted_iota(jnp.int32, pair.shape, 1)
    zero = jnp.zeros_like(pair)
    return jnp.concatenate(
        [jnp.where(lane < HEAD, pair, zero), jnp.where(lane >= HEAD, pair, zero)], axis=0
    )


def unstacked(both):
    row = lax.broadcasted_iota(jnp.int32, (2 * HEAD, QB), 0)
    return jnp.where(row < HEAD, both[:, :QB], both[:, QB:]).T


def fill_keys(scratch, prefix_ref, halo_ref, own_ref):
    scratch[:PREP] = prefix_ref[...]
    scratch[PREP : PREP + BAND] = halo_ref[...]
    scratch[PREP + BAND :] = own_ref[...]


def fill_turned(scratch, prefix_ref, halo_ref, own_ref):
    tokens = own_ref.shape[0]
    scratch[:, :BAND] = halo_ref[...].astype(WIDE).T.astype(LOW)
    scratch[:, BAND : BAND + tokens] = own_ref[...].astype(WIDE).T.astype(LOW)
    padded = jnp.concatenate(
        [prefix_ref[...].astype(WIDE), jnp.zeros((128 - PREP, 2 * HEAD), WIDE)], axis=0
    )
    scratch[:, BAND + tokens :] = padded.T.astype(LOW)


def masked_scores(queries, keys, start_ref, block, pref_count):
    pre = dot_nt(keys[:PREP], queries)
    pre = jnp.where(
        lax.broadcasted_iota(jnp.int32, pre.shape, 0) < pref_count, pre, NEGATIVE
    )
    band = dot_nt(keys[pl.ds(PREP + block * QB, KB)], queries)
    first = start_ref[:, block * QB : (block + 1) * QB] - block * QB
    first = jnp.concatenate([first, first], axis=1)
    last = lax.broadcasted_iota(jnp.int32, (1, 2 * QB), 1) % QB + BAND
    place = lax.broadcasted_iota(jnp.int32, band.shape, 0)
    band = jnp.where((place >= first) & (place <= last), band, NEGATIVE)
    return pre, band


def attend_kernel(pref_count, q_ref, k_ref, v_ref, hk_ref, hv_ref, pk_ref, pv_ref, start_ref,
                  c_ref, lse_ref, keys, turned):
    tokens = q_ref.shape[0]
    fill_keys(keys, pk_ref, hk_ref, k_ref)
    fill_turned(turned, pv_ref, hv_ref, v_ref)
    for block in range(tokens // QB):
        span = slice(block * QB, (block + 1) * QB)
        queries = stacked(q_ref[span, :] * jnp.asarray(HEAD ** (-0.5), LOW))
        pre, band = masked_scores(queries, keys, start_ref, block, pref_count)
        top = jnp.maximum(jnp.max(pre, axis=0, keepdims=True), jnp.max(band, axis=0, keepdims=True))
        pre = jnp.exp(pre - top)
        band = jnp.exp(band - top)
        total = jnp.sum(pre, axis=0, keepdims=True) + jnp.sum(band, axis=0, keepdims=True)
        lse_ref[0, block : block + 1, :] = top + jnp.log(total)
        inverse = 1.0 / total
        out = dot_nn(turned[:, block * QB : block * QB + KB], (band * inverse).astype(LOW))
        out = out + dot_nn(turned[:, BAND + tokens : BAND + tokens + PREP], (pre * inverse).astype(LOW))
        c_ref[span, :] = unstacked(out).astype(LOW)


def attend_back_kernel(pref_count, q_ref, k_ref, v_ref, hk_ref, hv_ref, pk_ref, pv_ref, start_ref,
                       lse_ref, dc_ref, dq_ref, dk_ref, dv_ref, dhk_ref, dhv_ref, dpk_ref, dpv_ref,
                       keys, vals, turned, dkeys, dvals):
    tokens = q_ref.shape[0]
    fill_keys(keys, pk_ref, hk_ref, k_ref)
    fill_keys(vals, pv_ref, hv_ref, v_ref)
    fill_turned(turned, pk_ref, hk_ref, k_ref)
    dkeys[...] = jnp.zeros_like(dkeys)
    dvals[...] = jnp.zeros_like(dvals)
    scaling = HEAD ** (-0.5)
    for block in range(tokens // QB):
        span = slice(block * QB, (block + 1) * QB)
        seen = pl.ds(PREP + block * QB, KB)
        queries = stacked(q_ref[span, :] * jnp.asarray(scaling, LOW))
        grads = stacked(dc_ref[span, :])
        pre, band = masked_scores(queries, keys, start_ref, block, pref_count)
        lse = lse_ref[0, block : block + 1, :]
        pre = jnp.exp(pre - lse)
        band = jnp.exp(band - lse)
        dpre = dot_nt(vals[:PREP], grads)
        dband = dot_nt(vals[seen], grads)
        inside = jnp.sum(pre * dpre, axis=0, keepdims=True) + jnp.sum(
            band * dband, axis=0, keepdims=True
        )
        dvals[:PREP] += dot_nn(pre.astype(LOW), grads)
        dvals[seen] += dot_nn(band.astype(LOW), grads)
        pre = (pre * (dpre - inside)).astype(LOW)
        band = (band * (dband - inside)).astype(LOW)
        dkeys[:PREP] += dot_nn(pre, queries)
        dkeys[seen] += dot_nn(band, queries)
        out = dot_nn(turned[:, block * QB : block * QB + KB], band)
        out = out + dot_nn(turned[:, BAND + tokens : BAND + tokens + PREP], pre)
        dq_ref[span, :] = (unstacked(out) * scaling).astype(LOW)
    dk_ref[...] = dkeys[PREP + BAND :].astype(LOW)
    dv_ref[...] = dvals[PREP + BAND :].astype(LOW)
    dhk_ref[...] = dkeys[PREP : PREP + BAND].astype(LOW)
    dhv_ref[...] = dvals[PREP : PREP + BAND].astype(LOW)
    dpk_ref[...] = dkeys[:PREP]
    dpv_ref[...] = dvals[:PREP]


def column(rows, place=lambda half, pair: 0, per=0):
    if per == 0:
        return pl.BlockSpec((rows, 2 * HEAD), lambda i: (0, i))
    return pl.BlockSpec((rows, 2 * HEAD), lambda i: (0, place(i // per) + i % per))


def attention_specs(tokens, per):
    return [
        column(tokens, lambda half: 3 * per * half, per),
        column(tokens, lambda half: 3 * per * half + per, per),
        column(tokens, lambda half: 3 * per * half + 2 * per, per),
        column(BAND, lambda half: 2 * per * (1 - half), per),
        column(BAND, lambda half: 2 * per * (1 - half) + per, per),
        column(PREP, lambda half: 2 * per * half, per),
        column(PREP, lambda half: 2 * per * half + per, per),
        pl.BlockSpec((1, tokens), lambda i: (0, 0)),
    ]


def attend(pref_count, qkv, halo, prefix, start):
    tokens, width = qkv.shape[0], qkv.shape[1] // 3
    pairs, blocks = width // (2 * HEAD), tokens // QB
    return pl.pallas_call(
        functools.partial(attend_kernel, pref_count),
        grid=(pairs,),
        in_specs=attention_specs(tokens, pairs // 2),
        out_specs=[column(tokens), pl.BlockSpec((1, blocks, 2 * QB), lambda i: (i, 0, 0))],
        out_shape=[
            jax.ShapeDtypeStruct((tokens, width), LOW),
            jax.ShapeDtypeStruct((pairs, blocks, 2 * QB), WIDE),
        ],
        scratch_shapes=[
            pltpu.VMEM((PREP + BAND + tokens, 2 * HEAD), LOW),
            pltpu.VMEM((2 * HEAD, BAND + tokens + 128), LOW),
        ],
        name="attend",
    )(qkv, qkv, qkv, halo, halo, prefix, prefix, start)


def attend_back(pref_count, qkv, halo, prefix, start, lse, grad):
    tokens, width = qkv.shape[0], qkv.shape[1] // 3
    pairs, blocks = width // (2 * HEAD), tokens // QB
    keys = PREP + BAND + tokens
    sizes = [(tokens, LOW)] * 3 + [(BAND, LOW)] * 2 + [(PREP, WIDE)] * 2
    return pl.pallas_call(
        functools.partial(attend_back_kernel, pref_count),
        grid=(pairs,),
        in_specs=attention_specs(tokens, pairs // 2)
        + [pl.BlockSpec((1, blocks, 2 * QB), lambda i: (i, 0, 0)), column(tokens)],
        out_specs=[column(rows) for rows, _ in sizes],
        out_shape=[jax.ShapeDtypeStruct((rows, width), kind) for rows, kind in sizes],
        scratch_shapes=[
            pltpu.VMEM((keys, 2 * HEAD), LOW),
            pltpu.VMEM((keys, 2 * HEAD), LOW),
            pltpu.VMEM((2 * HEAD, BAND + tokens + 128), LOW),
            pltpu.VMEM((keys, 2 * HEAD), WIDE),
            pltpu.VMEM((keys, 2 * HEAD), WIDE),
        ],
        name="attend_back",
    )(qkv, qkv, qkv, halo, halo, prefix, prefix, start, lse, grad)


CHUNK = 512
ROWS = 128


def by_rows(total, body, step=ROWS):
    @pl.loop(0, total // step)
    def _(index):
        body(pl.ds(pl.multiple_of(index * step, step), step))


def of_half(step, count, own_ref, far_ref, body):
    @pl.when(step < count)
    def _():
        body(own_ref)

    @pl.when(step >= count)
    def _():
        body(far_ref)


def halves(shape, count, across):
    def spec(place):
        return pl.BlockSpec(shape, lambda j: (0, place(j)) if across else (place(j), 0))

    return [spec(lambda j: jnp.minimum(j, count - 1)), spec(lambda j: jnp.maximum(j - count, 0))]


def whole(shape):
    return pl.BlockSpec(shape, lambda j: (0,) * len(shape))


def call(kernel, grid, in_specs, out_specs, out_shape, scratch, name, flops, operands):
    size = sum(o.size * o.dtype.itemsize for o in operands)
    return pl.pallas_call(
        kernel,
        grid=(grid,),
        in_specs=in_specs,
        out_specs=out_specs,
        out_shape=out_shape,
        scratch_shapes=scratch,
        name=name,
        compiler_params=pltpu.CompilerParams(vmem_limit_bytes=56 * 2**20),
        cost_estimate=pl.CostEstimate(flops=flops, bytes_accessed=size, transcendentals=0),
    )(*operands)


def qkv_kernel(x_ref, gain_ref, shift_ref, own_ref, far_ref, bias_ref, out_ref, halo_ref, normed):
    step = pl.program_id(0)

    @pl.when(step == 0)
    def _():
        def body(span):
            normed[span] = layer_norm(
                x_ref[span].astype(WIDE), gain_ref[...], shift_ref[...]
            ).astype(LOW)

        by_rows(x_ref.shape[0], body)

    def body(weight_ref):
        out_ref[...] = (dot_nn(normed[...], weight_ref[...]) + bias_ref[...]).astype(LOW)

    of_half(step, 3, own_ref, far_ref, body)

    @pl.when(step % 3 != 0)
    def _():
        halo_ref[...] = out_ref[out_ref.shape[0] - BAND :]


def qkv_forward(x, gain, shift, weights, bias):
    tokens, width = x.shape
    half = weights[0].shape[1] // 3
    return call(
        qkv_kernel,
        6,
        [whole(x.shape), whole((1, width)), whole((1, width))]
        + halves((width, half), 3, True)
        + [pl.BlockSpec((1, half), lambda j: (0, j))],
        [
            pl.BlockSpec((tokens, half), lambda j: (0, j)),
            pl.BlockSpec((BAND, half), lambda j: (0, 2 * (j // 3) + jnp.maximum(j % 3 - 1, 0))),
        ],
        [
            jax.ShapeDtypeStruct((tokens, 6 * half), LOW),
            jax.ShapeDtypeStruct((BAND, 4 * half), LOW),
        ],
        [pltpu.VMEM(x.shape, LOW)],
        "qkv",
        12 * tokens * width * half,
        (x, gain, shift, *weights, bias),
    )


def mlp_kernel(count, x_ref, c_ref, po_ref, pf_ref, b0_ref, gain_ref, shift_ref, fo_ref, ff_ref, bias_ref, wo_ref,
               wf_ref, b1_ref, h_ref, slope_ref, y_ref, low_ref, normed):
    step = pl.program_id(0)
    half = po_ref.shape[0]

    @pl.when(step == 0)
    def _():
        def body(span):
            h = x_ref[span].astype(WIDE) + (
                dot_nn(c_ref[span, :half], po_ref[...])
                + dot_nn(c_ref[span, half:], pf_ref[...])
                + b0_ref[...]
            )
            h_ref[span] = h
            normed[span] = layer_norm(h, gain_ref[...], shift_ref[...]).astype(LOW)
            y_ref[span] = h + b1_ref[...]

        by_rows(x_ref.shape[0], body)

    def half_body(up_ref, down_ref):
        def body(span):
            active, slope = gelu_parts(dot_nn(normed[span], up_ref[...]) + bias_ref[...])
            slope_ref[span] = slope.astype(LOW)
            y_ref[span] += dot_nn(active.astype(LOW), down_ref[...])

        by_rows(x_ref.shape[0], body, 256)

    of_half(step, count, (fo_ref, wo_ref), (ff_ref, wf_ref), lambda refs: half_body(*refs))

    @pl.when(step == 2 * count - 1)
    def _():
        low_ref[...] = y_ref[...].astype(LOW)


def mlp_forward(x, c, weights, biases, gain, shift, fc_bias):
    tokens, width = x.shape
    half, count = width // 2, weights["fc"][0].shape[1] // CHUNK
    row = whole((1, width))
    return call(
        functools.partial(mlp_kernel, count),
        2 * count,
        [whole(x.shape), whole(c.shape), whole((half, width)), whole((half, width)), row, row, row]
        + halves((width, CHUNK), count, True)
        + [pl.BlockSpec((1, CHUNK), lambda j: (0, j))]
        + halves((CHUNK, width), count, False)
        + [row],
        [whole(x.shape), pl.BlockSpec((tokens, CHUNK), lambda j: (0, j)), whole(x.shape), whole(x.shape)],
        [
            jax.ShapeDtypeStruct(x.shape, WIDE),
            jax.ShapeDtypeStruct((tokens, 2 * count * CHUNK), LOW),
            jax.ShapeDtypeStruct(x.shape, WIDE),
            jax.ShapeDtypeStruct(x.shape, LOW),
        ],
        [pltpu.VMEM(x.shape, LOW)],
        "mlp",
        2 * tokens * width * (width + 4 * count * CHUNK),
        (x, c, *weights["proj"], biases[0], gain, shift, *weights["fc"], fc_bias, *weights["fc2"], biases[1]),
    )


def mlp_back_kernel(count, dy_ref, h_ref, gain_ref, slope_ref, wo_ref, wf_ref, fo_ref, ff_ref, po_ref, pf_ref,
                    dh_ref, dc_ref, total):
    step = pl.program_id(0)
    half = po_ref.shape[0]

    def half_body(first, up_ref, down_ref):
        def body(span):
            du = (dot_nt(dy_ref[span], down_ref[...]) * slope_ref[span].astype(WIDE)).astype(LOW)
            dm = dot_nt(du, up_ref[...])
            total[span] = dm if first else total[span] + dm

        by_rows(dy_ref.shape[0], body, 256)

    @pl.when(step == 0)
    def _():
        half_body(True, fo_ref, wo_ref)

    @pl.when((step > 0) & (step < count))
    def _():
        half_body(False, fo_ref, wo_ref)

    @pl.when(step >= count)
    def _():
        half_body(False, ff_ref, wf_ref)

    @pl.when(step == 2 * count - 1)
    def _():
        def body(span):
            dh = dy_ref[span].astype(WIDE) + norm_back(h_ref[span], gain_ref[...], total[span])
            dh_ref[span] = dh
            low = dh.astype(LOW)
            dc_ref[span, :half] = dot_nt(low, po_ref[...]).astype(LOW)
            dc_ref[span, half:] = dot_nt(low, pf_ref[...]).astype(LOW)

        by_rows(dy_ref.shape[0], body)


def mlp_back(dy, h, gain, slope, weights):
    tokens, width = dy.shape
    half, count = width // 2, weights["fc"][0].shape[1] // CHUNK
    return call(
        functools.partial(mlp_back_kernel, count),
        2 * count,
        [whole(dy.shape), whole(dy.shape), whole((1, width)), pl.BlockSpec((tokens, CHUNK), lambda j: (0, j))]
        + halves((CHUNK, width), count, False)
        + halves((width, CHUNK), count, True)
        + [whole((half, width)), whole((half, width))],
        [whole(dy.shape), whole(dy.shape)],
        [jax.ShapeDtypeStruct(dy.shape, WIDE), jax.ShapeDtypeStruct(dy.shape, LOW)],
        [pltpu.VMEM(dy.shape, WIDE)],
        "mlp_back",
        2 * tokens * width * (width + 4 * count * CHUNK),
        (dy, h, gain, slope, *weights["fc2"], *weights["fc"], *weights["proj"]),
    )


def qkv_back_kernel(dq_ref, dk_ref, dv_ref, hk_ref, hv_ref, own_ref, far_ref, x_ref, dh_ref, gain_ref, dx_ref, low_ref,
                    total):
    step = pl.program_id(0)

    def chunk(grad_ref, halo_ref, kind):
        grad = grad_ref[...]
        if halo_ref is not None:
            early = grad.shape[0] - BAND
            late = (grad[early:].astype(WIDE) + halo_ref[...].astype(WIDE)).astype(LOW)
            grad = jnp.concatenate([grad[:early], late], axis=0)

        def body(weight_ref):
            total[...] += dot_nt(grad, weight_ref[...])

        @pl.when(step % 3 == kind)
        def _():
            of_half(step, 3, own_ref, far_ref, body)

    @pl.when(step == 0)
    def _():
        total[...] = jnp.zeros_like(total)

    chunk(dq_ref, None, 0)
    chunk(dk_ref, hk_ref, 1)
    chunk(dv_ref, hv_ref, 2)

    @pl.when(step == 5)
    def _():
        def body(span):
            dx = dh_ref[span] + norm_back(x_ref[span].astype(WIDE), gain_ref[...], total[span])
            dx_ref[span] = dx
            low_ref[span] = dx.astype(LOW)

        by_rows(x_ref.shape[0], body)


def qkv_back(grads, halo, weights, x, dh, gain):
    tokens, width = x.shape
    half = width // 2
    part = pl.BlockSpec((tokens, half), lambda j: (0, j // 3))
    edge = pl.BlockSpec((BAND, half), lambda j: (0, 1 - j // 3))
    return call(
        qkv_back_kernel,
        6,
        [part, part, part, edge, edge]
        + halves((width, half), 3, True)
        + [whole(x.shape), whole(x.shape), whole((1, width))],
        [whole(x.shape), whole(x.shape)],
        [jax.ShapeDtypeStruct(x.shape, WIDE), jax.ShapeDtypeStruct(x.shape, LOW)],
        [pltpu.VMEM(x.shape, WIDE)],
        "qkv_back",
        12 * tokens * width * half,
        (*grads, *halo, *weights, x, dh, gain),
    )


def block_forward(x, start, weights, small, pref_count):
    qkv, edge = qkv_forward(x, small["gain"][0:1], small["shift"][0:1], weights["qkv"], small["qkv"])
    halo = lax.ppermute(edge, "tensor", [(0, 1)])
    c, lse = attend(pref_count, qkv, halo, small["prefix"], start)
    h, slope, y, low = mlp_forward(
        x, c, weights, (small["out"][0:1], small["out"][1:2]), small["gain"][1:2], small["shift"][1:2], small["fc"]
    )
    return y, low, (x, h, qkv, halo, lse, slope)


def block_backward(stored, start, dy, weights, small, pref_count):
    x, h, qkv, halo, lse, slope = stored
    dh, dc = mlp_back(dy, h, small["gain"][1:2], slope, weights)
    *grads, hk, hv, pk, pv = attend_back(pref_count, qkv, halo, small["prefix"], start, lse, dc)
    edges = [lax.ppermute(edge, "tensor", [(1, 0)]) for edge in (hk, hv)]
    dx, low = qkv_back(grads, edges, weights["qkv"], x, dh, small["gain"][0:1])
    return dx, low, jnp.stack([pk, pv])


ORDER = (
    ("x", "qkv", "qkvx"),
    ("y", "proj", "projy"),
    ("z", "qkv", "qkvz"),
    ("y", "fc", "fcy"),
    ("x", "fc2", "fc2x"),
    ("z", "fc2", "fc2z"),
    ("x", "proj&", "proj&x"),
    ("y", "qkv&", "qkv&y"),
    ("z", "qkvz", "qkvzz"),
    ("x", "qkvz", "qkvzx"),
    ("y", "fc2&", "fc2&y"),
    ("x", "fcL0", "fcL0x"),
    ("z", "proj&&", "proj&&z"),
    ("z", "qkvzz", "qkvzzz"),
    ("x", "qkvzz", "qkvzzx"),
    ("y", "qkvz&", "qkvz&y"),
    ("x", "fcL1", "fcL1x"),
    ("z", "proj&&z", "proj&&zz"),
    ("x", "qkvzzz", "qkvzzzx"),
    ("y", "qkvzz&", "qkvzz&y"),
    ("z", "fc2z", "fc2zz"),
    ("z", "fcL0", "fcL0z"),
    ("x", "fc2z", "fc2zx"),
    ("y", "qkvzzz&", "qkvzzz&y"),
    ("x", "fc2zz", "fc2zzx"),
    ("z", "fc2zz", "fc2zzz"),
    ("y", "fc2z&", "fc2z&y"),
    ("x", "fcL0z", "fcL0zx"),
    ("z", "fcL0z", "fcL0zz"),
    ("x", "fc2zzz", "fc2zzzx"),
    ("z", "fcL1", "fcL1z"),
    ("y", "fc2zz&", "fc2zz&y"),
    ("x", "fcL0zz", "fcL0zzx"),
    ("z", "fcL0zz", "fcL0zzz"),
    ("x", "fcL1z", "fcL1zx"),
    ("z", "fcL1z", "fcL1zz"),
    ("y", "fc2zzz&", "fc2zzz&y"),
    ("x", "fcL0zzz", "fcL0zzzx"),
    ("z", "proj&&zz", "proj&&zzz"),
    ("z", "fcL1zz", "fcL1zzz"),
    ("x", "fcL1zz", "fcL1zzx"),
    ("x", "fcL1zzz", "fcL1zzzx"),
)
JOINED = {"proj&": ("proj", "projy"), "proj&&": ("proj&", "proj&x")}
DEEP = 2


def move(block, link):
    if link == "y":
        return swap(block, "section")
    count = lax.axis_size("rows")
    if link == "x":
        return lax.ppermute(block, "rows", [(i, i ^ 1) for i in range(count)])
    return lax.ppermute(block, "rows", [(i, (i + 2) % count) for i in range(count)])


def spread(shards, section):
    held, sent = dict(shards), {}

    def get(name):
        if name not in held:
            if name in JOINED:
                parts = JOINED[name]
            elif name.endswith("&"):
                parts = (name[:-1], name[:-1] + "x")
            else:
                held[name] = jnp.where(section == int(name[-1]), held["fc"], held["fcy"])
                return held[name]
            held[name] = jnp.concatenate([get(part) for part in parts], axis=0)
        return held[name]

    for link, source, target in ORDER:
        block, ahead = get(source), sent.setdefault(link, [])
        if len(ahead) >= DEEP:
            block, _ = lax.optimization_barrier((block, ahead[-DEEP]))
        held[target] = move(block, link)
        ahead.append(held[target])
    return get, held


def pieces(name, layer):
    result = []
    for steps in range(4):
        moved = "z" * steps
        for other in range(2):
            if name == "proj":
                base = "proj&&" + moved
                result.append((steps, other, (base, 2 * other), (base, 2 * other + 1)))
            elif name == "fc":
                base = "fcL%d%s%s" % (layer, moved, "x" * other)
                result.append((steps, other, (base, 0), (base, 0)))
            else:
                base = name + moved + "&"
                result.append((steps, other, (base, other), (base + "y", other)))
    return result


def join_kernel(plan, layer, rows, place_ref, *refs):
    buffers, (out_ref, sems) = refs[:-2], refs[-2:]
    section, z, x = place_ref[0], place_ref[1], place_ref[2]

    def copy(index, source):
        steps, other = plan[index][:2]
        slot = ((z + 4 - steps) % 4) * 2 + (x + other) % 2
        buffer, block = source
        return pltpu.make_async_copy(
            buffers[buffer].at[block * rows : (block + 1) * rows], out_ref.at[slot], sems.at[index]
        )

    @pl.when(section == layer)
    def _():
        for index, entry in enumerate(plan):
            copy(index, entry[2]).start()

    @pl.when(section != layer)
    def _():
        for index, entry in enumerate(plan):
            copy(index, entry[3]).start()

    for index, entry in enumerate(plan):
        copy(index, entry[2]).wait()


def joined(name, layer, get, shape, place):
    rows, columns = shape
    names, plan = [], []
    for steps, other, *sources in pieces(name, layer):
        spots = []
        for buffer, block in sources:
            if buffer not in names:
                names.append(buffer)
            spots.append((names.index(buffer), block))
        plan.append((steps, other, *spots))
    anywhere = pl.BlockSpec(memory_space=pl.ANY)
    whole = pl.pallas_call(
        functools.partial(join_kernel, plan, layer, rows),
        in_specs=[pl.BlockSpec(memory_space=pltpu.SMEM)] + [anywhere] * len(names),
        out_specs=pl.BlockSpec(memory_space=pltpu.VMEM),
        out_shape=jax.ShapeDtypeStruct((8, rows, columns), LOW),
        scratch_shapes=[pltpu.SemaphoreType.DMA((8,))],
        name="join_" + name,
    )(place, *[get(buffer) for buffer in names])
    return whole.reshape(8 * rows, columns)


def gather_weights(shards):
    result = [{}, {}]
    section, rows = lax.axis_index("section"), lax.axis_index("rows")
    if lax.axis_size("rows") == 8:
        get, _ = spread(shards, section)
        place = jnp.stack([section, rows // 2, rows % 2]).astype(jnp.int32)
        for layer in range(2):
            for name, shard in shards.items():
                whole = joined(name, layer, get, shard.shape, place)
                result[layer][name] = (whole, swap(whole, "tensor"))
        return result
    for name, shard in shards.items():
        whole = lax.all_gather(shard, ("section", "rows"), axis=0, tiled=True)
        whole = whole.reshape(2, -1, shard.shape[1])
        far = swap(whole, "tensor")
        for layer in range(2):
            result[layer][name] = (whole[layer], far[layer])
    return result


def on_device(
    tokens,
    segment_ids,
    cotangent,
    ln_gain,
    ln_bias,
    w_qkv,
    query_key_value_bias,
    w_proj,
    w_fc,
    fc_bias,
    w_fc2,
    out_bias,
    prefix_embed,
    rep_w1,
    rep_b1,
    rep_w2,
    rep_b2,
):
    share, width = tokens.shape[1:]
    section, core = lax.axis_index("section"), lax.axis_index("tensor")
    rows_index, rows = lax.axis_index("rows"), lax.axis_size("rows")
    half = rep_w2.shape[-1]
    pref_count = prefix_embed.shape[0]

    shards = {
        "qkv": w_qkv[0].astype(LOW).reshape(w_qkv.shape[1], -1),
        "proj": w_proj[0].astype(LOW),
        "fc": w_fc[0].astype(LOW),
        "fc2": w_fc2[0].astype(LOW),
    }
    weights = gather_weights(shards)

    rep_hidden = jnp.tanh(jnp.dot(prefix_embed, rep_w1, precision=HIGHEST) + rep_b1)
    prefix = jnp.einsum("pm,mcd->pcd", rep_hidden, rep_w2[:, 0], precision=HIGHEST) + rep_b2[0]
    prefix = prefix.astype(LOW).astype(WIDE)
    prefix = jnp.pad(prefix, ((0, PREP - pref_count), (0, 0), (0, 0)))
    parts = [ln_gain[0], ln_bias[0], out_bias[0], query_key_value_bias[0], fc_bias[0], prefix]
    packed = jnp.concatenate([part.reshape(-1) for part in parts])
    near = jnp.stack([packed, swap(packed, "tensor")])
    away = swap(near, "section")
    smalls = []
    for layer in range(2):
        cut, place = [], 0
        chosen = jnp.where(section == layer, near, away)
        for part in parts:
            cut.append([chosen[h, place : place + part.size].reshape(part.shape) for h in range(2)])
            place += part.size
        smalls.append(
            {
                "gain": cut[0][0],
                "shift": cut[1][0],
                "out": cut[2][0],
                "qkv": jnp.concatenate([cut[3][h].reshape(1, -1) for h in range(2)], axis=1),
                "fc": jnp.concatenate([cut[4][h].reshape(1, -1) for h in range(2)], axis=1),
                "prefix": jnp.concatenate(
                    [cut[5][h].reshape(PREP, -1).astype(LOW) for h in range(2)], axis=1
                ),
            }
        )

    own = section
    segments = lax.dynamic_index_in_dim(segment_ids, own, 0, keepdims=False).reshape(-1)
    mine = lax.dynamic_slice_in_dim(segments, core * share, share)
    start = jnp.sum(segments[:, None] < mine[None, :], axis=0, dtype=jnp.int32)
    start = (start - core * share + BAND)[None]

    x = lax.dynamic_index_in_dim(tokens, own, 0, keepdims=False)
    y0, low0, kept0 = block_forward(x, start, weights[0], smalls[0], pref_count)
    y1, low1, kept1 = block_forward(low0, start, weights[1], smalls[1], pref_count)
    dy = lax.dynamic_index_in_dim(cotangent, own, 0, keepdims=False)
    g1, down1, pre1 = block_backward(kept1, start, dy, weights[1], smalls[1], pref_count)
    g0, down0, pre0 = block_backward(kept0, start, down1, weights[0], smalls[0], pref_count)

    def settle(first, second, first_low, second_low):
        keep = jnp.where(section == 0, first, second)
        got = swap(jnp.where(section == 0, second_low, first_low), "section").astype(WIDE)
        return jnp.where(section == 0, jnp.stack([keep, got]), jnp.stack([got, keep]))[None]

    acts = settle(y0, y1, low0, low1)
    in_grads = settle(g0, g1, down0, down1)

    pre0, pre1 = [pre.reshape(2, PREP, 2, half) for pre in (pre0, pre1)]
    keep = jnp.where(section == 0, pre0, pre1)
    layer_terms = keep + swap(jnp.where(section == 0, pre1, pre0), "section")
    total = layer_terms[:, :, 0] + swap(layer_terms[:, :, 1], "tensor")
    total = all_sum(total[:, :pref_count], ("rows",))
    grad_b2 = jnp.sum(total, axis=1)
    mid_part = rep_w1.shape[1] // rows
    width_part = width // rows
    hidden_part = lax.dynamic_slice_in_dim(rep_hidden, rows_index * mid_part, mid_part, 1)
    grad_w2 = jnp.einsum("pm,cpd->mcd", hidden_part, total, precision=HIGHEST)
    hidden_term = jnp.einsum("cpd,mcd->pm", total, rep_w2[:, 0], precision=HIGHEST)
    grad_hidden = all_sum(hidden_term, ("section", "tensor"))
    grad_pre = grad_hidden * (1.0 - rep_hidden * rep_hidden)
    grad_b1 = jnp.sum(grad_pre, axis=0)
    embed_part = lax.dynamic_slice_in_dim(prefix_embed, rows_index * width_part, width_part, 1)
    grad_w1 = jnp.einsum("pd,pm->dm", embed_part, grad_pre, precision=HIGHEST)
    weight_part = lax.dynamic_slice_in_dim(rep_w1, rows_index * width_part, width_part, 0)
    grad_embed = jnp.einsum("pm,dm->pd", grad_pre, weight_part, precision=HIGHEST)
    return (acts, in_grads, grad_embed, grad_w1, grad_b1, grad_w2[:, None], grad_b2[None])


def solution(mesh):
    return jax.shard_map(
        on_device,
        mesh=mesh,
        in_specs=(
            P(None, ("rows", "tensor"), None),
            P(None, "rows", None),
            P(None, ("rows", "tensor"), None),
            P("section", None, None),
            P("section", None, None),
            P("section", "rows", None, "tensor"),
            P("section", None, "tensor"),
            P("section", ("tensor", "rows"), None),
            P("section", "rows", "tensor"),
            P("section", "tensor"),
            P("section", ("tensor", "rows"), None),
            P("section", None, None),
            P(),
            P(),
            P(),
            P(None, "section", None, "tensor"),
            P("section", None, "tensor"),
        ),
        out_specs=(
            P("section", None, ("rows", "tensor"), None),
            P("section", None, ("rows", "tensor"), None),
            P(None, "rows"),
            P("rows", None),
            P(),
            P("rows", "section", None, "tensor"),
            P("section", None, "tensor"),
        ),
        check_vma=False,
    )
```

```python
import functools

import jax
import jax.numpy as jnp
from jax import lax
from jax.experimental import pallas as pl
from jax.experimental.pallas import tpu as pltpu
from jax.sharding import PartitionSpec as P

HEAD = 64
EPSILON = 1e-05
NEGATIVE = -1000000000.0
HIGHEST = lax.Precision.HIGHEST
LOW = jnp.bfloat16
WIDE = jnp.float32
QB = 128
BAND = 256
KB = QB + BAND
PREP = 16


def swap(block, axis):
    return lax.ppermute(block, axis, [(0, 1), (1, 0)])


def all_sum(block, axes):
    for axis in axes:
        count = lax.axis_size(axis)
        if count & (count - 1):
            block = lax.psum(block, axis)
            continue
        bit = 1
        while bit < count:
            block = block + lax.ppermute(block, axis, [(i, i ^ bit) for i in range(count)])
            bit *= 2
    return block


def layer_norm(values, gain, shift):
    centre = values - jnp.mean(values, axis=-1, keepdims=True)
    spread = jnp.mean(centre * centre, axis=-1, keepdims=True)
    return centre * lax.rsqrt(spread + EPSILON) * gain + shift


def norm_back(values, gain, grad):
    centre = values - jnp.mean(values, axis=-1, keepdims=True)
    inverse = lax.rsqrt(jnp.mean(centre * centre, axis=-1, keepdims=True) + EPSILON)
    normal = centre * inverse
    scaled = grad * gain
    return inverse * (
        scaled
        - jnp.mean(scaled, axis=-1, keepdims=True)
        - normal * jnp.mean(scaled * normal, axis=-1, keepdims=True)
    )


def gelu_parts(values):
    root = 0.7978845608028654
    square = values * values
    inner = jnp.tanh(root * values * (1.0 + 0.044715 * square))
    half = 0.5 * (1.0 + inner)
    slope = half + 0.5 * values * (1.0 - inner * inner) * root * (1.0 + 3 * 0.044715 * square)
    return values * half, slope


def dot_nn(left, right):
    return jnp.dot(left, right, preferred_element_type=WIDE)


def dot_nt(left, right):
    return lax.dot_general(left, right, (((1,), (1,)), ((), ())), preferred_element_type=WIDE)


def stacked(pair):
    lane = lax.broadcasted_iota(jnp.int32, pair.shape, 1)
    zero = jnp.zeros_like(pair)
    return jnp.concatenate(
        [jnp.where(lane < HEAD, pair, zero), jnp.where(lane >= HEAD, pair, zero)], axis=0
    )


def unstacked(both):
    lane = lax.broadcasted_iota(jnp.int32, (QB, 2 * HEAD), 1)
    return jnp.where(lane < HEAD, both[:QB], both[QB:])


def dot_tn(left, right):
    return lax.dot_general(left, right, (((0,), (0,)), ((), ())), preferred_element_type=WIDE)


def lower():
    row = lax.broadcasted_iota(jnp.int32, (QB, 2 * QB), 0)
    lane = lax.broadcasted_iota(jnp.int32, (QB, 2 * QB), 1)
    return row <= jnp.where(lane < QB, lane, lane - QB)


def fold(band, near):
    return jnp.concatenate([jnp.where(near, band[BAND:], band[:QB]), band[QB:BAND]], axis=0)


def unfold(folded, near):
    zero = jnp.zeros((QB, 2 * QB), folded.dtype)
    edge = folded[:QB]
    return jnp.concatenate(
        [jnp.where(near, zero, edge), folded[QB:], jnp.where(near, edge, zero)], axis=0
    )


def fill_places(places):
    row = lax.broadcasted_iota(jnp.int32, (QB, 2 * QB), 0)
    places[:QB] = jnp.where(lower(), row + BAND, row)
    places[QB:] = row + QB


def fill_keys(scratch, prefix_ref, halo_ref, own_ref):
    scratch[:PREP] = prefix_ref[...]
    scratch[PREP : PREP + BAND] = halo_ref[...]
    scratch[PREP + BAND :] = own_ref[...]


def masked_scores(queries, keys, start_ref, block, pref_count, places, near):
    pre = dot_nt(keys[:PREP], queries)
    pre = jnp.where(
        lax.broadcasted_iota(jnp.int32, pre.shape, 0) < pref_count, pre, NEGATIVE
    )
    band = fold(dot_nt(keys[pl.ds(PREP + block * QB, KB)], queries), near)
    first = start_ref[:, block * QB : (block + 1) * QB] - block * QB
    first = jnp.concatenate([first, first], axis=1)
    return pre, jnp.where(places[...] >= first, band, NEGATIVE)


def attend_kernel(pref_count, q_ref, k_ref, v_ref, hk_ref, hv_ref, pk_ref, pv_ref, start_ref,
                  c_ref, probs_ref, keys, vals, places):
    fill_keys(keys, pk_ref, hk_ref, k_ref)
    fill_keys(vals, pv_ref, hv_ref, v_ref)
    fill_places(places)
    near = lower()
    for block in range(q_ref.shape[0] // QB):
        span = slice(block * QB, (block + 1) * QB)
        seen = pl.ds(PREP + block * QB, KB)
        queries = stacked(q_ref[span, :] * jnp.asarray(HEAD ** (-0.5), LOW))
        pre, band = masked_scores(queries, keys, start_ref, block, pref_count, places, near)
        top = jnp.maximum(jnp.max(pre, axis=0, keepdims=True), jnp.max(band, axis=0, keepdims=True))
        pre = jnp.exp(pre - top)
        band = jnp.exp(band - top)
        total = jnp.sum(pre, axis=0, keepdims=True) + jnp.sum(band, axis=0, keepdims=True)
        inverse = 1.0 / total
        probs = jnp.concatenate([pre * inverse, unfold(band * inverse, near)], axis=0).astype(LOW)
        probs_ref[0, block] = probs
        out = dot_tn(probs, jnp.concatenate([vals[:PREP], vals[seen]], axis=0))
        c_ref[span, :] = unstacked(out).astype(LOW)


def attend_back_kernel(q_ref, k_ref, v_ref, hk_ref, hv_ref, pk_ref, pv_ref, probs_ref, dc_ref,
                       dq_ref, dk_ref, dv_ref, dhk_ref, dhv_ref, dpk_ref, dpv_ref,
                       keys, vals, dkeys, dvals):
    fill_keys(keys, pk_ref, hk_ref, k_ref)
    fill_keys(vals, pv_ref, hv_ref, v_ref)
    dkeys[...] = jnp.zeros_like(dkeys)
    dvals[...] = jnp.zeros_like(dvals)
    scaling = HEAD ** (-0.5)
    for block in range(q_ref.shape[0] // QB):
        span = slice(block * QB, (block + 1) * QB)
        seen = pl.ds(PREP + block * QB, KB)
        queries = stacked(q_ref[span, :] * jnp.asarray(scaling, LOW))
        grads = stacked(dc_ref[span, :])
        low = probs_ref[0, block]
        probs = low.astype(WIDE)
        dprobs = dot_nt(jnp.concatenate([vals[:PREP], vals[seen]], axis=0), grads)
        inside = jnp.sum(probs * dprobs, axis=0, keepdims=True)
        slope = (probs * (dprobs - inside)).astype(LOW)
        terms = dot_nn(low, grads)
        dvals[:PREP] += terms[:PREP]
        dvals[seen] += terms[PREP:]
        terms = dot_nn(slope, queries)
        dkeys[:PREP] += terms[:PREP]
        dkeys[seen] += terms[PREP:]
        out = dot_tn(slope, jnp.concatenate([keys[:PREP], keys[seen]], axis=0))
        dq_ref[span, :] = (unstacked(out) * scaling).astype(LOW)
    dk_ref[...] = dkeys[PREP + BAND :].astype(LOW)
    dv_ref[...] = dvals[PREP + BAND :].astype(LOW)
    dhk_ref[...] = dkeys[PREP : PREP + BAND].astype(LOW)
    dhv_ref[...] = dvals[PREP : PREP + BAND].astype(LOW)
    dpk_ref[...] = dkeys[:PREP]
    dpv_ref[...] = dvals[:PREP]


def column(rows, place=lambda half, pair: 0, per=0):
    if per == 0:
        return pl.BlockSpec((rows, 2 * HEAD), lambda i: (0, i))
    return pl.BlockSpec((rows, 2 * HEAD), lambda i: (0, place(i // per) + i % per))


def attention_specs(tokens, per):
    return [
        column(tokens, lambda half: 3 * per * half, per),
        column(tokens, lambda half: 3 * per * half + per, per),
        column(tokens, lambda half: 3 * per * half + 2 * per, per),
        column(BAND, lambda half: 2 * per * (1 - half), per),
        column(BAND, lambda half: 2 * per * (1 - half) + per, per),
        column(PREP, lambda half: 2 * per * half, per),
        column(PREP, lambda half: 2 * per * half + per, per),
    ]


def probs_spec(blocks):
    return pl.BlockSpec((1, blocks, PREP + KB, 2 * QB), lambda i: (i, 0, 0, 0))


def attend(pref_count, qkv, halo, prefix, start):
    tokens, width = qkv.shape[0], qkv.shape[1] // 3
    pairs, blocks = width // (2 * HEAD), tokens // QB
    return pl.pallas_call(
        functools.partial(attend_kernel, pref_count),
        grid=(pairs,),
        in_specs=attention_specs(tokens, pairs // 2) + [pl.BlockSpec((1, tokens), lambda i: (0, 0))],
        out_specs=[column(tokens), probs_spec(blocks)],
        out_shape=[
            jax.ShapeDtypeStruct((tokens, width), LOW),
            jax.ShapeDtypeStruct((pairs, blocks, PREP + KB, 2 * QB), LOW),
        ],
        scratch_shapes=[
            pltpu.VMEM((PREP + BAND + tokens, 2 * HEAD), LOW),
            pltpu.VMEM((PREP + BAND + tokens, 2 * HEAD), LOW),
            pltpu.VMEM((2 * QB, 2 * QB), jnp.int32),
        ],
        name="attend",
        cost_estimate=pl.CostEstimate(flops=12 * 10**9, bytes_accessed=2 * qkv.size, transcendentals=0),
    )(qkv, qkv, qkv, halo, halo, prefix, prefix, start)


def attend_back(qkv, halo, prefix, probs, grad):
    tokens, width = qkv.shape[0], qkv.shape[1] // 3
    pairs, blocks = width // (2 * HEAD), tokens // QB
    keys = PREP + BAND + tokens
    sizes = [(tokens, LOW)] * 3 + [(BAND, LOW)] * 2 + [(PREP, WIDE)] * 2
    return pl.pallas_call(
        attend_back_kernel,
        grid=(pairs,),
        in_specs=attention_specs(tokens, pairs // 2) + [probs_spec(blocks), column(tokens)],
        out_specs=[column(rows) for rows, _ in sizes],
        out_shape=[jax.ShapeDtypeStruct((rows, width), kind) for rows, kind in sizes],
        scratch_shapes=[
            pltpu.VMEM((keys, 2 * HEAD), LOW),
            pltpu.VMEM((keys, 2 * HEAD), LOW),
            pltpu.VMEM((keys, 2 * HEAD), WIDE),
            pltpu.VMEM((keys, 2 * HEAD), WIDE),
        ],
        name="attend_back",
        cost_estimate=pl.CostEstimate(flops=16 * 10**9, bytes_accessed=4 * qkv.size, transcendentals=0),
    )(qkv, qkv, qkv, halo, halo, prefix, prefix, probs, grad)


CHUNK = 512
ROWS = 128


def by_rows(total, body, step=ROWS):
    @pl.loop(0, total // step)
    def _(index):
        body(pl.ds(pl.multiple_of(index * step, step), step))


def of_half(step, count, own_ref, far_ref, body):
    @pl.when(step < count)
    def _():
        body(own_ref)

    @pl.when(step >= count)
    def _():
        body(far_ref)


def halves(shape, count, across):
    def spec(place):
        return pl.BlockSpec(shape, lambda j: (0, place(j)) if across else (place(j), 0))

    return [spec(lambda j: jnp.minimum(j, count - 1)), spec(lambda j: jnp.maximum(j - count, 0))]


def whole(shape):
    return pl.BlockSpec(shape, lambda j: (0,) * len(shape))


def call(kernel, grid, in_specs, out_specs, out_shape, scratch, name, flops, operands):
    size = sum(o.size * o.dtype.itemsize for o in operands)
    return pl.pallas_call(
        kernel,
        grid=(grid,),
        in_specs=in_specs,
        out_specs=out_specs,
        out_shape=out_shape,
        scratch_shapes=scratch,
        name=name,
        compiler_params=pltpu.CompilerParams(vmem_limit_bytes=56 * 2**20),
        cost_estimate=pl.CostEstimate(flops=flops, bytes_accessed=size, transcendentals=0),
    )(*operands)


def qkv_kernel(x_ref, gain_ref, shift_ref, own_ref, far_ref, bias_ref, out_ref, halo_ref, normed):
    step = pl.program_id(0)

    @pl.when(step == 0)
    def _():
        def body(span):
            normed[span] = layer_norm(
                x_ref[span].astype(WIDE), gain_ref[...], shift_ref[...]
            ).astype(LOW)

        by_rows(x_ref.shape[0], body)

    def body(weight_ref):
        out_ref[...] = (dot_nn(normed[...], weight_ref[...]) + bias_ref[...]).astype(LOW)

    of_half(step, 3, own_ref, far_ref, body)

    @pl.when(step % 3 != 0)
    def _():
        halo_ref[...] = out_ref[out_ref.shape[0] - BAND :]


def qkv_forward(x, gain, shift, weights, bias):
    tokens, width = x.shape
    half = weights[0].shape[1] // 3
    return call(
        qkv_kernel,
        6,
        [whole(x.shape), whole((1, width)), whole((1, width))]
        + halves((width, half), 3, True)
        + [pl.BlockSpec((1, half), lambda j: (0, j))],
        [
            pl.BlockSpec((tokens, half), lambda j: (0, j)),
            pl.BlockSpec((BAND, half), lambda j: (0, 2 * (j // 3) + jnp.maximum(j % 3 - 1, 0))),
        ],
        [
            jax.ShapeDtypeStruct((tokens, 6 * half), LOW),
            jax.ShapeDtypeStruct((BAND, 4 * half), LOW),
        ],
        [pltpu.VMEM(x.shape, LOW)],
        "qkv",
        12 * tokens * width * half,
        (x, gain, shift, *weights, bias),
    )


def mlp_kernel(count, x_ref, c_ref, po_ref, pf_ref, b0_ref, gain_ref, shift_ref, fo_ref, ff_ref, bias_ref, wo_ref,
               wf_ref, b1_ref, h_ref, slope_ref, y_ref, low_ref, normed):
    step = pl.program_id(0)
    half = po_ref.shape[0]

    @pl.when(step == 0)
    def _():
        def body(span):
            h = x_ref[span].astype(WIDE) + (
                dot_nn(c_ref[span, :half], po_ref[...])
                + dot_nn(c_ref[span, half:], pf_ref[...])
                + b0_ref[...]
            )
            h_ref[span] = h
            normed[span] = layer_norm(h, gain_ref[...], shift_ref[...]).astype(LOW)
            y_ref[span] = h + b1_ref[...]

        by_rows(x_ref.shape[0], body)

    def half_body(up_ref, down_ref):
        def body(span):
            active, slope = gelu_parts(dot_nn(normed[span], up_ref[...]) + bias_ref[...])
            slope_ref[span] = slope.astype(LOW)
            y_ref[span] += dot_nn(active.astype(LOW), down_ref[...])

        by_rows(x_ref.shape[0], body, 256)

    of_half(step, count, (fo_ref, wo_ref), (ff_ref, wf_ref), lambda refs: half_body(*refs))

    @pl.when(step == 2 * count - 1)
    def _():
        low_ref[...] = y_ref[...].astype(LOW)


def mlp_forward(x, c, weights, biases, gain, shift, fc_bias):
    tokens, width = x.shape
    half, count = width // 2, weights["fc"][0].shape[1] // CHUNK
    row = whole((1, width))
    return call(
        functools.partial(mlp_kernel, count),
        2 * count,
        [whole(x.shape), whole(c.shape), whole((half, width)), whole((half, width)), row, row, row]
        + halves((width, CHUNK), count, True)
        + [pl.BlockSpec((1, CHUNK), lambda j: (0, j))]
        + halves((CHUNK, width), count, False)
        + [row],
        [whole(x.shape), pl.BlockSpec((tokens, CHUNK), lambda j: (0, j)), whole(x.shape), whole(x.shape)],
        [
            jax.ShapeDtypeStruct(x.shape, WIDE),
            jax.ShapeDtypeStruct((tokens, 2 * count * CHUNK), LOW),
            jax.ShapeDtypeStruct(x.shape, WIDE),
            jax.ShapeDtypeStruct(x.shape, LOW),
        ],
        [pltpu.VMEM(x.shape, LOW)],
        "mlp",
        2 * tokens * width * (width + 4 * count * CHUNK),
        (x, c, *weights["proj"], biases[0], gain, shift, *weights["fc"], fc_bias, *weights["fc2"], biases[1]),
    )


def mlp_back_kernel(count, dy_ref, h_ref, gain_ref, slope_ref, wo_ref, wf_ref, fo_ref, ff_ref, po_ref, pf_ref,
                    dh_ref, dc_ref, total):
    step = pl.program_id(0)
    half = po_ref.shape[0]

    def half_body(first, up_ref, down_ref):
        def body(span):
            du = (dot_nt(dy_ref[span], down_ref[...]) * slope_ref[span].astype(WIDE)).astype(LOW)
            dm = dot_nt(du, up_ref[...])
            total[span] = dm if first else total[span] + dm

        by_rows(dy_ref.shape[0], body, 256)

    @pl.when(step == 0)
    def _():
        half_body(True, fo_ref, wo_ref)

    @pl.when((step > 0) & (step < count))
    def _():
        half_body(False, fo_ref, wo_ref)

    @pl.when(step >= count)
    def _():
        half_body(False, ff_ref, wf_ref)

    @pl.when(step == 2 * count - 1)
    def _():
        def body(span):
            dh = dy_ref[span].astype(WIDE) + norm_back(h_ref[span], gain_ref[...], total[span])
            dh_ref[span] = dh
            low = dh.astype(LOW)
            dc_ref[span, :half] = dot_nt(low, po_ref[...]).astype(LOW)
            dc_ref[span, half:] = dot_nt(low, pf_ref[...]).astype(LOW)

        by_rows(dy_ref.shape[0], body)


def mlp_back(dy, h, gain, slope, weights):
    tokens, width = dy.shape
    half, count = width // 2, weights["fc"][0].shape[1] // CHUNK
    return call(
        functools.partial(mlp_back_kernel, count),
        2 * count,
        [whole(dy.shape), whole(dy.shape), whole((1, width)), pl.BlockSpec((tokens, CHUNK), lambda j: (0, j))]
        + halves((CHUNK, width), count, False)
        + halves((width, CHUNK), count, True)
        + [whole((half, width)), whole((half, width))],
        [whole(dy.shape), whole(dy.shape)],
        [jax.ShapeDtypeStruct(dy.shape, WIDE), jax.ShapeDtypeStruct(dy.shape, LOW)],
        [pltpu.VMEM(dy.shape, WIDE)],
        "mlp_back",
        2 * tokens * width * (width + 4 * count * CHUNK),
        (dy, h, gain, slope, *weights["fc2"], *weights["fc"], *weights["proj"]),
    )


def qkv_back_kernel(dq_ref, dk_ref, dv_ref, hk_ref, hv_ref, own_ref, far_ref, x_ref, dh_ref, gain_ref, dx_ref, low_ref,
                    total):
    step = pl.program_id(0)

    def chunk(grad_ref, halo_ref, kind):
        grad = grad_ref[...]
        if halo_ref is not None:
            early = grad.shape[0] - BAND
            late = (grad[early:].astype(WIDE) + halo_ref[...].astype(WIDE)).astype(LOW)
            grad = jnp.concatenate([grad[:early], late], axis=0)

        def body(weight_ref):
            total[...] += dot_nt(grad, weight_ref[...])

        @pl.when(step % 3 == kind)
        def _():
            of_half(step, 3, own_ref, far_ref, body)

    @pl.when(step == 0)
    def _():
        total[...] = jnp.zeros_like(total)

    chunk(dq_ref, None, 0)
    chunk(dk_ref, hk_ref, 1)
    chunk(dv_ref, hv_ref, 2)

    @pl.when(step == 5)
    def _():
        def body(span):
            dx = dh_ref[span] + norm_back(x_ref[span].astype(WIDE), gain_ref[...], total[span])
            dx_ref[span] = dx
            low_ref[span] = dx.astype(LOW)

        by_rows(x_ref.shape[0], body)


def qkv_back(grads, halo, weights, x, dh, gain):
    tokens, width = x.shape
    half = width // 2
    part = pl.BlockSpec((tokens, half), lambda j: (0, j // 3))
    edge = pl.BlockSpec((BAND, half), lambda j: (0, 1 - j // 3))
    return call(
        qkv_back_kernel,
        6,
        [part, part, part, edge, edge]
        + halves((width, half), 3, True)
        + [whole(x.shape), whole(x.shape), whole((1, width))],
        [whole(x.shape), whole(x.shape)],
        [jax.ShapeDtypeStruct(x.shape, WIDE), jax.ShapeDtypeStruct(x.shape, LOW)],
        [pltpu.VMEM(x.shape, WIDE)],
        "qkv_back",
        12 * tokens * width * half,
        (*grads, *halo, *weights, x, dh, gain),
    )


def block_backward(stored, dy, weights, small):
    x, h, qkv, halo, probs, slope = stored
    dh, dc = mlp_back(dy, h, small["gain"][1:2], slope, weights)
    *grads, hk, hv, pk, pv = attend_back(qkv, halo, small["prefix"], probs, dc)
    edges = [lax.ppermute(edge, "tensor", [(1, 0)]) for edge in (hk, hv)]
    dx, low = qkv_back(grads, edges, weights["qkv"], x, dh, small["gain"][0:1])
    return dx, low, jnp.stack([pk, pv])


ORDER = (
    ("x", "qkv", "qkvx"),
    ("z", "qkv", "qkvz"),
    ("y", "qkv", "qkvy"),
    ("x", "fc", "fcx"),
    ("y", "proj", "projy"),
    ("z", "fc", "fcz"),
    ("z", "qkvz", "qkvzz"),
    ("y", "qkvz", "qkvzy"),
    ("y", "qkvx", "qkvxy"),
    ("x", "proj&", "proj&x"),
    ("x", "qkvz", "qkvzx"),
    ("y", "fcx", "fcxy"),
    ("z", "fcz", "fczz"),
    ("z", "qkvzz", "qkvzzz"),
    ("x", "qkvzz", "qkvzzx"),
    ("y", "qkvzz", "qkvzzy"),
    ("x", "fcz", "fczx"),
    ("z", "proj&&", "proj&&z"),
    ("y", "qkvzzx", "qkvzzxy"),
    ("x", "fczz", "fczzx"),
    ("y", "fc2", "fc2y"),
    ("x", "qkvzzz", "qkvzzzx"),
    ("y", "fc", "fcy"),
    ("z", "proj&&z", "proj&&zz"),
    ("z", "fczz", "fczzz"),
    ("y", "fczzx", "fczzxy"),
    ("x", "fc2L1", "fc2L1x"),
    ("z", "proj&&zz", "proj&&zzz"),
    ("y", "qkvzzzx", "qkvzzzxy"),
    ("x", "fczzz", "fczzzx"),
    ("z", "fc2L0", "fc2L0z"),
    ("y", "fczzz", "fczzzy"),
    ("x", "fc2L0", "fc2L0x"),
    ("y", "fczz", "fczzy"),
    ("z", "fc2L1", "fc2L1z"),
    ("x", "fc2L0z", "fc2L0zx"),
    ("z", "fc2L0z", "fc2L0zz"),
    ("y", "qkvzx", "qkvzxy"),
    ("x", "fc2L1z", "fc2L1zx"),
    ("y", "qkvzzz", "qkvzzzy"),
    ("z", "fc2L1z", "fc2L1zz"),
    ("y", "fcz", "fczy"),
    ("x", "fc2L0zz", "fc2L0zzx"),
    ("z", "fc2L0zz", "fc2L0zzz"),
    ("y", "fczzzx", "fczzzxy"),
    ("x", "fc2L1zz", "fc2L1zzx"),
    ("z", "fc2L1zz", "fc2L1zzz"),
    ("y", "fczx", "fczxy"),
    ("x", "fc2L0zzz", "fc2L0zzzx"),
    ("x", "fc2L1zzz", "fc2L1zzzx"),
)
STAGES = (
    "join qkv 0",
    "join proj 0",
    "join fc 0",
    "join fc2 0",
    "join qkv 1",
    "join proj 1",
    "join fc 1",
    "join fc2 1",
    "qkv 0",
    "att 0",
    "mlp 0",
    "qkv 1",
    "att 1",
    "mlp 1",
)
JOINED = {"proj&": ("proj", "projy"), "proj&&": ("proj&", "proj&x")}
DEEP = 2


def move(block, link):
    if link == "y":
        return swap(block, "section")
    count = lax.axis_size("rows")
    if link == "x":
        return lax.ppermute(block, "rows", [(i, i ^ 1) for i in range(count)])
    return lax.ppermute(block, "rows", [(i, (i + 2) % count) for i in range(count)])


def spread(shards, section):
    held, sent = dict(shards), {}

    def get(name):
        if name not in held:
            if name in JOINED:
                held[name] = jnp.concatenate([get(part) for part in JOINED[name]], axis=0)
            else:
                held[name] = jnp.where(section == int(name[-1]), get(name[:-2]), get(name[:-2] + "y"))
        return held[name]

    for link, source, target in ORDER:
        block, ahead = get(source), sent.setdefault(link, [])
        if len(ahead) >= DEEP:
            block, _ = lax.optimization_barrier((block, ahead[-DEEP]))
        held[target] = move(block, link)
        ahead.append(held[target])
    names = list(held)
    return dict(zip(names, lax.optimization_barrier(tuple(held.values()))))


def pieces(name, layer):
    result = []
    for steps in range(4):
        moved = "z" * steps
        for other in range(2):
            if name == "proj":
                base = "proj&&" + moved
                result.append((steps, other, (base, 2 * other), (base, 2 * other + 1)))
            elif name == "fc2":
                base = "fc2L%d%s%s" % (layer, moved, "x" * other)
                result.append((steps, other, (base, 0), (base, 0)))
            else:
                base = name + moved + "x" * other
                result.append((steps, other, (base, 0), (base + "y", 0)))
    return result


def join_kernel(plan, layer, rows, place_ref, *refs):
    buffers, (out_ref, sems) = refs[:-2], refs[-2:]
    section, z, x = place_ref[0], place_ref[1], place_ref[2]

    def copy(index, source):
        steps, other = plan[index][:2]
        slot = ((z + 4 - steps) % 4) * 2 + (x + other) % 2
        buffer, block = source
        return pltpu.make_async_copy(
            buffers[buffer].at[block * rows : (block + 1) * rows], out_ref.at[slot], sems.at[index]
        )

    @pl.when(section == layer)
    def _():
        for index, entry in enumerate(plan):
            copy(index, entry[2]).start()

    @pl.when(section != layer)
    def _():
        for index, entry in enumerate(plan):
            copy(index, entry[3]).start()

    for index, entry in enumerate(plan):
        copy(index, entry[2]).wait()


def joined(name, layer, held, shape, place):
    rows, columns = shape
    names, plan = [], []
    for steps, other, *sources in pieces(name, layer):
        spots = []
        for buffer, block in sources:
            if buffer not in names:
                names.append(buffer)
            spots.append((names.index(buffer), block))
        plan.append((steps, other, *spots))
    anywhere = pl.BlockSpec(memory_space=pl.ANY)
    whole = pl.pallas_call(
        functools.partial(join_kernel, plan, layer, rows),
        in_specs=[pl.BlockSpec(memory_space=pltpu.SMEM)] + [anywhere] * len(names),
        out_specs=pl.BlockSpec(memory_space=pltpu.VMEM),
        out_shape=jax.ShapeDtypeStruct((8, rows, columns), LOW),
        scratch_shapes=[pltpu.SemaphoreType.DMA((8,))],
        name="join_" + name,
        cost_estimate=pl.CostEstimate(flops=0, bytes_accessed=4 * 8 * rows * columns, transcendentals=0),
    )(place, *[held[buffer] for buffer in names])
    return whole.reshape(8 * rows, columns)


def forward(shards, x, start, smalls, pref_count):
    section, rows = lax.axis_index("section"), lax.axis_index("rows")
    weights, kept, outputs = [{}, {}], [None, None], [None, None]

    def run(stage, held):
        kind, *name, layer = stage.split()
        layer = int(layer)
        small, mine = smalls[layer], weights[layer]
        if kind == "join":
            shape = shards[name[0]].shape
            place = jnp.stack([section, rows // 2, rows % 2]).astype(jnp.int32)
            near = joined(name[0], layer, held, shape, place)
            mine[name[0]] = (near, swap(near, "tensor"))
            return
        if kind == "qkv":
            source = outputs[0][1] if layer else x
            qkv, edge = qkv_forward(source, small["gain"][0:1], small["shift"][0:1], mine["qkv"], small["qkv"])
            kept[layer] = (source, qkv, lax.ppermute(edge, "tensor", [(0, 1)]))
            return
        if kind == "att":
            source, qkv, halo = kept[layer]
            c, probs = attend(pref_count, qkv, halo, small["prefix"], start)
            kept[layer] = (source, qkv, halo, probs, c)
            return
        source, qkv, halo, probs, c = kept[layer]
        h, slope, *outputs[layer] = mlp_forward(
            source, c, mine, (small["out"][0:1], small["out"][1:2]), small["gain"][1:2], small["shift"][1:2], small["fc"]
        )
        kept[layer] = (source, h, qkv, halo, probs, slope)

    if lax.axis_size("rows") == 8:
        held = spread(shards, section)
        for stage in STAGES:
            run(stage, held)
    else:
        for name, shard in shards.items():
            near = lax.all_gather(shard, ("section", "rows"), axis=0, tiled=True)
            near = near.reshape(2, -1, shard.shape[1])
            far = swap(near, "tensor")
            for layer in range(2):
                weights[layer][name] = (near[layer], far[layer])
        for stage in STAGES:
            if not stage.startswith("join"):
                run(stage, None)
    return weights, kept, outputs


def on_device(
    tokens,
    segment_ids,
    cotangent,
    ln_gain,
    ln_bias,
    w_qkv,
    query_key_value_bias,
    w_proj,
    w_fc,
    fc_bias,
    w_fc2,
    out_bias,
    prefix_embed,
    rep_w1,
    rep_b1,
    rep_w2,
    rep_b2,
):
    share, width = tokens.shape[1:]
    section, core = lax.axis_index("section"), lax.axis_index("tensor")
    rows_index, rows = lax.axis_index("rows"), lax.axis_size("rows")
    half = rep_w2.shape[-1]
    pref_count = prefix_embed.shape[0]

    shards = {
        "qkv": w_qkv[0].astype(LOW).reshape(w_qkv.shape[1], -1),
        "proj": w_proj[0].astype(LOW),
        "fc": w_fc[0].astype(LOW),
        "fc2": w_fc2[0].astype(LOW),
    }
    rep_hidden = jnp.tanh(jnp.dot(prefix_embed, rep_w1, precision=HIGHEST) + rep_b1)
    prefix = jnp.einsum("pm,mcd->pcd", rep_hidden, rep_w2[:, 0], precision=HIGHEST) + rep_b2[0]
    prefix = prefix.astype(LOW).astype(WIDE)
    prefix = jnp.pad(prefix, ((0, PREP - pref_count), (0, 0), (0, 0)))
    parts = [ln_gain[0], ln_bias[0], out_bias[0], query_key_value_bias[0], fc_bias[0], prefix]
    packed = jnp.concatenate([part.reshape(-1) for part in parts])
    near = jnp.stack([packed, swap(packed, "tensor")])
    away = swap(near, "section")
    smalls = []
    for layer in range(2):
        cut, place = [], 0
        chosen = jnp.where(section == layer, near, away)
        for part in parts:
            cut.append([chosen[h, place : place + part.size].reshape(part.shape) for h in range(2)])
            place += part.size
        smalls.append(
            {
                "gain": cut[0][0],
                "shift": cut[1][0],
                "out": cut[2][0],
                "qkv": jnp.concatenate([cut[3][h].reshape(1, -1) for h in range(2)], axis=1),
                "fc": jnp.concatenate([cut[4][h].reshape(1, -1) for h in range(2)], axis=1),
                "prefix": jnp.concatenate(
                    [cut[5][h].reshape(PREP, -1).astype(LOW) for h in range(2)], axis=1
                ),
            }
        )

    own = section
    segments = lax.dynamic_index_in_dim(segment_ids, own, 0, keepdims=False).reshape(-1)
    mine = lax.dynamic_slice_in_dim(segments, core * share, share)
    start = jnp.sum(segments[:, None] < mine[None, :], axis=0, dtype=jnp.int32)
    start = (start - core * share + BAND)[None]

    x = lax.dynamic_index_in_dim(tokens, own, 0, keepdims=False)
    weights, (kept0, kept1), ((y0, low0), (y1, low1)) = forward(shards, x, start, smalls, pref_count)
    dy = lax.dynamic_index_in_dim(cotangent, own, 0, keepdims=False)
    def settle(first, second, first_low, second_low):
        keep = jnp.where(section == 0, first, second)
        got = swap(jnp.where(section == 0, second_low, first_low), "section").astype(WIDE)
        return jnp.where(section == 0, jnp.stack([keep, got]), jnp.stack([got, keep]))[None]

    acts = settle(y0, y1, low0, low1)
    g1, down1, pre1 = block_backward(kept1, dy, weights[1], smalls[1])
    down1, acts = lax.optimization_barrier((down1, acts))
    g0, down0, pre0 = block_backward(kept0, down1, weights[0], smalls[0])
    in_grads = settle(g0, g1, down0, down1)

    pre0, pre1 = [pre.reshape(2, PREP, 2, half) for pre in (pre0, pre1)]
    keep = jnp.where(section == 0, pre0, pre1)
    layer_terms = keep + swap(jnp.where(section == 0, pre1, pre0), "section")
    layer_terms, _ = lax.optimization_barrier((layer_terms, down0))
    total = layer_terms[:, :, 0] + swap(layer_terms[:, :, 1], "tensor")
    total = all_sum(total[:, :pref_count], ("rows",))
    grad_b2 = jnp.sum(total, axis=1)
    mid_part = rep_w1.shape[1] // rows
    width_part = width // rows
    hidden_part = lax.dynamic_slice_in_dim(rep_hidden, rows_index * mid_part, mid_part, 1)
    grad_w2 = jnp.einsum("pm,cpd->mcd", hidden_part, total, precision=HIGHEST)
    hidden_term = jnp.einsum("cpd,mcd->pm", total, rep_w2[:, 0], precision=HIGHEST)
    grad_hidden = all_sum(hidden_term, ("section", "tensor"))
    grad_pre = grad_hidden * (1.0 - rep_hidden * rep_hidden)
    grad_b1 = jnp.sum(grad_pre, axis=0)
    embed_part = lax.dynamic_slice_in_dim(prefix_embed, rows_index * width_part, width_part, 1)
    grad_w1 = jnp.einsum("pd,pm->dm", embed_part, grad_pre, precision=HIGHEST)
    weight_part = lax.dynamic_slice_in_dim(rep_w1, rows_index * width_part, width_part, 0)
    grad_embed = jnp.einsum("pm,dm->pd", grad_pre, weight_part, precision=HIGHEST)
    return (acts, in_grads, grad_embed, grad_w1, grad_b1, grad_w2[:, None], grad_b2[None])


def solution(mesh):
    return jax.shard_map(
        on_device,
        mesh=mesh,
        in_specs=(
            P(None, ("rows", "tensor"), None),
            P(None, "rows", None),
            P(None, ("rows", "tensor"), None),
            P("section", None, None),
            P("section", None, None),
            P("section", "rows", None, "tensor"),
            P("section", None, "tensor"),
            P("section", ("tensor", "rows"), None),
            P("section", "rows", "tensor"),
            P("section", "tensor"),
            P("section", ("tensor", "rows"), None),
            P("section", None, None),
            P(),
            P(),
            P(),
            P(None, "section", None, "tensor"),
            P("section", None, "tensor"),
        ),
        out_specs=(
            P("section", None, ("rows", "tensor"), None),
            P("section", None, ("rows", "tensor"), None),
            P(None, "rows"),
            P("rows", None),
            P(),
            P("rows", "section", None, "tensor"),
            P("section", None, "tensor"),
        ),
        check_vma=False,
    )
```

```python
import functools

import jax
import jax.numpy as jnp
from jax import lax
from jax.experimental import pallas as pl
from jax.experimental.pallas import tpu as pltpu
from jax.sharding import PartitionSpec as P

HEAD = 64
EPSILON = 1e-05
NEGATIVE = -1000000000.0
HIGHEST = lax.Precision.HIGHEST
LOW = jnp.bfloat16
WIDE = jnp.float32
QB = 128
BAND = 256
KB = QB + BAND
PREP = 16


def swap(block, axis):
    return lax.ppermute(block, axis, [(0, 1), (1, 0)])


def all_sum(block, axes):
    for axis in axes:
        count = lax.axis_size(axis)
        if count & (count - 1):
            block = lax.psum(block, axis)
            continue
        bit = 1
        while bit < count:
            block = block + lax.ppermute(block, axis, [(i, i ^ bit) for i in range(count)])
            bit *= 2
    return block


def layer_norm(values, gain, shift):
    centre = values - jnp.mean(values, axis=-1, keepdims=True)
    spread = jnp.mean(centre * centre, axis=-1, keepdims=True)
    return centre * lax.rsqrt(spread + EPSILON) * gain + shift


def norm_back(values, gain, grad):
    centre = values - jnp.mean(values, axis=-1, keepdims=True)
    inverse = lax.rsqrt(jnp.mean(centre * centre, axis=-1, keepdims=True) + EPSILON)
    normal = centre * inverse
    scaled = grad * gain
    return inverse * (
        scaled
        - jnp.mean(scaled, axis=-1, keepdims=True)
        - normal * jnp.mean(scaled * normal, axis=-1, keepdims=True)
    )


def gelu_parts(values):
    root = 0.7978845608028654
    square = values * values
    inner = jnp.tanh(root * values * (1.0 + 0.044715 * square))
    half = 0.5 * (1.0 + inner)
    slope = half + 0.5 * values * (1.0 - inner * inner) * root * (1.0 + 3 * 0.044715 * square)
    return values * half, slope


def dot_nn(left, right):
    return jnp.dot(left, right, preferred_element_type=WIDE)


def dot_nt(left, right):
    return lax.dot_general(left, right, (((1,), (1,)), ((), ())), preferred_element_type=WIDE)


def stacked(pair):
    lane = lax.broadcasted_iota(jnp.int32, pair.shape, 1)
    zero = jnp.zeros_like(pair)
    return jnp.concatenate(
        [jnp.where(lane < HEAD, pair, zero), jnp.where(lane >= HEAD, pair, zero)], axis=0
    )


def unstacked(both):
    lane = lax.broadcasted_iota(jnp.int32, (QB, 2 * HEAD), 1)
    return jnp.where(lane < HEAD, both[:QB], both[QB:])


def dot_tn(left, right):
    return lax.dot_general(left, right, (((0,), (0,)), ((), ())), preferred_element_type=WIDE)


def lower():
    row = lax.broadcasted_iota(jnp.int32, (QB, 2 * QB), 0)
    lane = lax.broadcasted_iota(jnp.int32, (QB, 2 * QB), 1)
    return row <= jnp.where(lane < QB, lane, lane - QB)


def fold(band, near):
    return jnp.concatenate([jnp.where(near, band[BAND:], band[:QB]), band[QB:BAND]], axis=0)


def unfold(folded, near):
    zero = jnp.zeros((QB, 2 * QB), folded.dtype)
    edge = folded[:QB]
    return jnp.concatenate(
        [jnp.where(near, zero, edge), folded[QB:], jnp.where(near, edge, zero)], axis=0
    )


def fill_places(places):
    row = lax.broadcasted_iota(jnp.int32, (QB, 2 * QB), 0)
    places[:QB] = jnp.where(lower(), row + BAND, row)
    places[QB:] = row + QB


def fill_keys(scratch, prefix_ref, halo_ref, own_ref):
    scratch[:PREP] = prefix_ref[...]
    scratch[PREP : PREP + BAND] = halo_ref[...]
    scratch[PREP + BAND :] = own_ref[...]


def masked_scores(queries, keys, start_ref, block, pref_count, places, near):
    pre = dot_nt(keys[:PREP], queries)
    pre = jnp.where(
        lax.broadcasted_iota(jnp.int32, pre.shape, 0) < pref_count, pre, NEGATIVE
    )
    band = fold(dot_nt(keys[pl.ds(PREP + block * QB, KB)], queries), near)
    first = start_ref[:, block * QB : (block + 1) * QB] - block * QB
    first = jnp.concatenate([first, first], axis=1)
    return pre, jnp.where(places[...] >= first, band, NEGATIVE)


def attend_kernel(pref_count, q_ref, k_ref, v_ref, hk_ref, hv_ref, pk_ref, pv_ref, start_ref,
                  c_ref, probs_ref, keys, vals, places):
    fill_keys(keys, pk_ref, hk_ref, k_ref)
    fill_keys(vals, pv_ref, hv_ref, v_ref)
    fill_places(places)
    near = lower()
    for block in range(q_ref.shape[0] // QB):
        span = slice(block * QB, (block + 1) * QB)
        seen = pl.ds(PREP + block * QB, KB)
        queries = stacked(q_ref[span, :] * jnp.asarray(HEAD ** (-0.5), LOW))
        pre, band = masked_scores(queries, keys, start_ref, block, pref_count, places, near)
        top = jnp.maximum(jnp.max(pre, axis=0, keepdims=True), jnp.max(band, axis=0, keepdims=True))
        pre = jnp.exp(pre - top)
        band = jnp.exp(band - top)
        total = jnp.sum(pre, axis=0, keepdims=True) + jnp.sum(band, axis=0, keepdims=True)
        inverse = 1.0 / total
        probs = jnp.concatenate([pre * inverse, unfold(band * inverse, near)], axis=0).astype(LOW)
        probs_ref[0, block] = probs
        out = dot_tn(probs, jnp.concatenate([vals[:PREP], vals[seen]], axis=0))
        c_ref[span, :] = unstacked(out).astype(LOW)


def attend_back_kernel(q_ref, k_ref, v_ref, hk_ref, hv_ref, pk_ref, pv_ref, probs_ref, dc_ref,
                       dq_ref, dk_ref, dv_ref, edge_ref, prefix_ref, keys, vals, dkeys, dvals):
    fill_keys(keys, pk_ref, hk_ref, k_ref)
    fill_keys(vals, pv_ref, hv_ref, v_ref)
    dkeys[...] = jnp.zeros_like(dkeys)
    dvals[...] = jnp.zeros_like(dvals)
    scaling = HEAD ** (-0.5)
    for block in range(q_ref.shape[0] // QB):
        span = slice(block * QB, (block + 1) * QB)
        seen = pl.ds(PREP + block * QB, KB)
        queries = stacked(q_ref[span, :] * jnp.asarray(scaling, LOW))
        grads = stacked(dc_ref[span, :])
        low = probs_ref[0, block]
        probs = low.astype(WIDE)
        dprobs = dot_nt(jnp.concatenate([vals[:PREP], vals[seen]], axis=0), grads)
        inside = jnp.sum(probs * dprobs, axis=0, keepdims=True)
        slope = (probs * (dprobs - inside)).astype(LOW)
        terms = dot_nn(low, grads)
        dvals[:PREP] += terms[:PREP]
        dvals[seen] += terms[PREP:]
        terms = dot_nn(slope, queries)
        dkeys[:PREP] += terms[:PREP]
        dkeys[seen] += terms[PREP:]
        out = dot_tn(slope, jnp.concatenate([keys[:PREP], keys[seen]], axis=0))
        dq_ref[span, :] = (unstacked(out) * scaling).astype(LOW)
    dk_ref[...] = dkeys[PREP + BAND :].astype(LOW)
    dv_ref[...] = dvals[PREP + BAND :].astype(LOW)
    edge_ref[:BAND] = dkeys[PREP : PREP + BAND].astype(LOW)
    edge_ref[BAND:] = dvals[PREP : PREP + BAND].astype(LOW)
    prefix_ref[:PREP] = dkeys[:PREP]
    prefix_ref[PREP:] = dvals[:PREP]


def column(rows, place=lambda half, pair: 0, per=0):
    if per == 0:
        return pl.BlockSpec((rows, 2 * HEAD), lambda i: (0, i))
    return pl.BlockSpec((rows, 2 * HEAD), lambda i: (0, place(i // per) + i % per))


def attention_specs(tokens, per):
    return [
        column(tokens, lambda half: 3 * per * half, per),
        column(tokens, lambda half: 3 * per * half + per, per),
        column(tokens, lambda half: 3 * per * half + 2 * per, per),
        column(BAND, lambda half: 2 * per * (1 - half), per),
        column(BAND, lambda half: 2 * per * (1 - half) + per, per),
        column(PREP, lambda half: 2 * per * half, per),
        column(PREP, lambda half: 2 * per * half + per, per),
    ]


def probs_spec(blocks):
    return pl.BlockSpec((1, blocks, PREP + KB, 2 * QB), lambda i: (i, 0, 0, 0))


def attend(pref_count, qkv, halo, prefix, start):
    tokens, width = qkv.shape[0], qkv.shape[1] // 3
    pairs, blocks = width // (2 * HEAD), tokens // QB
    return pl.pallas_call(
        functools.partial(attend_kernel, pref_count),
        grid=(pairs,),
        in_specs=attention_specs(tokens, pairs // 2) + [pl.BlockSpec((1, tokens), lambda i: (0, 0))],
        out_specs=[column(tokens), probs_spec(blocks)],
        out_shape=[
            jax.ShapeDtypeStruct((tokens, width), LOW),
            jax.ShapeDtypeStruct((pairs, blocks, PREP + KB, 2 * QB), LOW),
        ],
        scratch_shapes=[
            pltpu.VMEM((PREP + BAND + tokens, 2 * HEAD), LOW),
            pltpu.VMEM((PREP + BAND + tokens, 2 * HEAD), LOW),
            pltpu.VMEM((2 * QB, 2 * QB), jnp.int32),
        ],
        name="attend",
        cost_estimate=pl.CostEstimate(flops=12 * 10**9, bytes_accessed=2 * qkv.size, transcendentals=0),
    )(qkv, qkv, qkv, halo, halo, prefix, prefix, start)


def attend_back(qkv, halo, prefix, probs, grad):
    tokens, width = qkv.shape[0], qkv.shape[1] // 3
    pairs, blocks = width // (2 * HEAD), tokens // QB
    keys = PREP + BAND + tokens
    sizes = [(tokens, LOW)] * 3 + [(2 * BAND, LOW), (2 * PREP, WIDE)]
    return pl.pallas_call(
        attend_back_kernel,
        grid=(pairs,),
        in_specs=attention_specs(tokens, pairs // 2) + [probs_spec(blocks), column(tokens)],
        out_specs=[column(rows) for rows, _ in sizes],
        out_shape=[jax.ShapeDtypeStruct((rows, width), kind) for rows, kind in sizes],
        scratch_shapes=[
            pltpu.VMEM((keys, 2 * HEAD), LOW),
            pltpu.VMEM((keys, 2 * HEAD), LOW),
            pltpu.VMEM((keys, 2 * HEAD), WIDE),
            pltpu.VMEM((keys, 2 * HEAD), WIDE),
        ],
        name="attend_back",
        cost_estimate=pl.CostEstimate(flops=16 * 10**9, bytes_accessed=4 * qkv.size, transcendentals=0),
    )(qkv, qkv, qkv, halo, halo, prefix, prefix, probs, grad)


CHUNK = 512
ROWS = 128


def by_rows(total, body, step=ROWS):
    @pl.loop(0, total // step)
    def _(index):
        body(pl.ds(pl.multiple_of(index * step, step), step))


def of_half(step, count, own_ref, far_ref, body):
    @pl.when(step < count)
    def _():
        body(own_ref)

    @pl.when(step >= count)
    def _():
        body(far_ref)


def halves(shape, count, across):
    def spec(place):
        return pl.BlockSpec(shape, lambda j: (0, place(j)) if across else (place(j), 0))

    return [spec(lambda j: jnp.minimum(j, count - 1)), spec(lambda j: jnp.maximum(j - count, 0))]


def whole(shape):
    return pl.BlockSpec(shape, lambda j: (0,) * len(shape))


def call(kernel, grid, in_specs, out_specs, out_shape, scratch, name, flops, operands):
    size = sum(o.size * o.dtype.itemsize for o in operands)
    return pl.pallas_call(
        kernel,
        grid=(grid,),
        in_specs=in_specs,
        out_specs=out_specs,
        out_shape=out_shape,
        scratch_shapes=scratch,
        name=name,
        compiler_params=pltpu.CompilerParams(vmem_limit_bytes=56 * 2**20),
        cost_estimate=pl.CostEstimate(flops=flops, bytes_accessed=size, transcendentals=0),
    )(*operands)


def qkv_kernel(x_ref, gain_ref, shift_ref, own_ref, far_ref, bias_ref, out_ref, halo_ref, normed):
    step = pl.program_id(0)

    @pl.when(step == 0)
    def _():
        def body(span):
            normed[span] = layer_norm(
                x_ref[span].astype(WIDE), gain_ref[...], shift_ref[...]
            ).astype(LOW)

        by_rows(x_ref.shape[0], body)

    def body(weight_ref):
        out_ref[...] = (dot_nn(normed[...], weight_ref[...]) + bias_ref[...]).astype(LOW)

    of_half(step, 3, own_ref, far_ref, body)

    @pl.when(step % 3 != 0)
    def _():
        halo_ref[...] = out_ref[out_ref.shape[0] - BAND :]


def qkv_forward(x, gain, shift, weights, bias):
    tokens, width = x.shape
    half = weights[0].shape[1] // 3
    return call(
        qkv_kernel,
        6,
        [whole(x.shape), whole((1, width)), whole((1, width))]
        + halves((width, half), 3, True)
        + [pl.BlockSpec((1, half), lambda j: (0, j))],
        [
            pl.BlockSpec((tokens, half), lambda j: (0, j)),
            pl.BlockSpec((BAND, half), lambda j: (0, 2 * (j // 3) + jnp.maximum(j % 3 - 1, 0))),
        ],
        [
            jax.ShapeDtypeStruct((tokens, 6 * half), LOW),
            jax.ShapeDtypeStruct((BAND, 4 * half), LOW),
        ],
        [pltpu.VMEM(x.shape, LOW)],
        "qkv",
        12 * tokens * width * half,
        (x, gain, shift, *weights, bias),
    )


def mlp_kernel(count, x_ref, c_ref, po_ref, pf_ref, b0_ref, gain_ref, shift_ref, fo_ref, ff_ref, bias_ref, wo_ref,
               wf_ref, b1_ref, h_ref, slope_ref, y_ref, low_ref, normed):
    step = pl.program_id(0)
    half = po_ref.shape[0]

    @pl.when(step == 0)
    def _():
        def body(span):
            h = x_ref[span].astype(WIDE) + (
                dot_nn(c_ref[span, :half], po_ref[...])
                + dot_nn(c_ref[span, half:], pf_ref[...])
                + b0_ref[...]
            )
            h_ref[span] = h
            normed[span] = layer_norm(h, gain_ref[...], shift_ref[...]).astype(LOW)
            y_ref[span] = h + b1_ref[...]

        by_rows(x_ref.shape[0], body)

    def half_body(up_ref, down_ref):
        def body(span):
            active, slope = gelu_parts(dot_nn(normed[span], up_ref[...]) + bias_ref[...])
            slope_ref[span] = slope.astype(LOW)
            y_ref[span] += dot_nn(active.astype(LOW), down_ref[...])

        by_rows(x_ref.shape[0], body, 256)

    of_half(step, count, (fo_ref, wo_ref), (ff_ref, wf_ref), lambda refs: half_body(*refs))

    @pl.when(step == 2 * count - 1)
    def _():
        low_ref[...] = y_ref[...].astype(LOW)


def mlp_forward(x, c, weights, biases, gain, shift, fc_bias):
    tokens, width = x.shape
    half, count = width // 2, weights["fc"][0].shape[1] // CHUNK
    row = whole((1, width))
    return call(
        functools.partial(mlp_kernel, count),
        2 * count,
        [whole(x.shape), whole(c.shape), whole((half, width)), whole((half, width)), row, row, row]
        + halves((width, CHUNK), count, True)
        + [pl.BlockSpec((1, CHUNK), lambda j: (0, j))]
        + halves((CHUNK, width), count, False)
        + [row],
        [whole(x.shape), pl.BlockSpec((tokens, CHUNK), lambda j: (0, j)), whole(x.shape), whole(x.shape)],
        [
            jax.ShapeDtypeStruct(x.shape, WIDE),
            jax.ShapeDtypeStruct((tokens, 2 * count * CHUNK), LOW),
            jax.ShapeDtypeStruct(x.shape, WIDE),
            jax.ShapeDtypeStruct(x.shape, LOW),
        ],
        [pltpu.VMEM(x.shape, LOW)],
        "mlp",
        2 * tokens * width * (width + 4 * count * CHUNK),
        (x, c, *weights["proj"], biases[0], gain, shift, *weights["fc"], fc_bias, *weights["fc2"], biases[1]),
    )


def mlp_back_kernel(count, dy_ref, h_ref, gain_ref, slope_ref, wo_ref, wf_ref, fo_ref, ff_ref, po_ref, pf_ref,
                    dh_ref, dc_ref, total):
    step = pl.program_id(0)
    half = po_ref.shape[0]

    def half_body(first, up_ref, down_ref):
        def body(span):
            du = (dot_nt(dy_ref[span], down_ref[...]) * slope_ref[span].astype(WIDE)).astype(LOW)
            dm = dot_nt(du, up_ref[...])
            total[span] = dm if first else total[span] + dm

        by_rows(dy_ref.shape[0], body, 256)

    @pl.when(step == 0)
    def _():
        half_body(True, fo_ref, wo_ref)

    @pl.when((step > 0) & (step < count))
    def _():
        half_body(False, fo_ref, wo_ref)

    @pl.when(step >= count)
    def _():
        half_body(False, ff_ref, wf_ref)

    @pl.when(step == 2 * count - 1)
    def _():
        def body(span):
            dh = dy_ref[span].astype(WIDE) + norm_back(h_ref[span], gain_ref[...], total[span])
            dh_ref[span] = dh
            low = dh.astype(LOW)
            dc_ref[span, :half] = dot_nt(low, po_ref[...]).astype(LOW)
            dc_ref[span, half:] = dot_nt(low, pf_ref[...]).astype(LOW)

        by_rows(dy_ref.shape[0], body)


def mlp_back(dy, h, gain, slope, weights):
    tokens, width = dy.shape
    half, count = width // 2, weights["fc"][0].shape[1] // CHUNK
    return call(
        functools.partial(mlp_back_kernel, count),
        2 * count,
        [whole(dy.shape), whole(dy.shape), whole((1, width)), pl.BlockSpec((tokens, CHUNK), lambda j: (0, j))]
        + halves((CHUNK, width), count, False)
        + halves((width, CHUNK), count, True)
        + [whole((half, width)), whole((half, width))],
        [whole(dy.shape), whole(dy.shape)],
        [jax.ShapeDtypeStruct(dy.shape, WIDE), jax.ShapeDtypeStruct(dy.shape, LOW)],
        [pltpu.VMEM(dy.shape, WIDE)],
        "mlp_back",
        2 * tokens * width * (width + 4 * count * CHUNK),
        (dy, h, gain, slope, *weights["fc2"], *weights["fc"], *weights["proj"]),
    )


def mlp_both_kernel(count, x_ref, c_ref, dy_ref, po_ref, pf_ref, b0_ref, gain_ref, shift_ref, fo_ref, ff_ref, bias_ref,
                    wo_ref, wf_ref, b1_ref, y_ref, low_ref, dh_ref, dc_ref, h_ref, normed, total):
    step = pl.program_id(0)
    half = po_ref.shape[0]

    @pl.when(step == 0)
    def _():
        def body(span):
            h = x_ref[span].astype(WIDE) + (
                dot_nn(c_ref[span, :half], po_ref[...])
                + dot_nn(c_ref[span, half:], pf_ref[...])
                + b0_ref[...]
            )
            h_ref[span] = h
            normed[span] = layer_norm(h, gain_ref[...], shift_ref[...]).astype(LOW)
            y_ref[span] = h + b1_ref[...]
            total[span] = jnp.zeros_like(h)

        by_rows(x_ref.shape[0], body)

    def half_body(up_ref, down_ref):
        def body(span):
            active, slope = gelu_parts(dot_nn(normed[span], up_ref[...]) + bias_ref[...])
            du = (dot_nt(dy_ref[span], down_ref[...]) * slope).astype(LOW)
            y_ref[span] += dot_nn(active.astype(LOW), down_ref[...])
            total[span] += dot_nt(du, up_ref[...])

        by_rows(x_ref.shape[0], body, 256)

    of_half(step, count, (fo_ref, wo_ref), (ff_ref, wf_ref), lambda refs: half_body(*refs))

    @pl.when(step == 2 * count - 1)
    def _():
        def body(span):
            low_ref[span] = y_ref[span].astype(LOW)
            dh = dy_ref[span].astype(WIDE) + norm_back(h_ref[span], gain_ref[...], total[span])
            dh_ref[span] = dh
            low = dh.astype(LOW)
            dc_ref[span, :half] = dot_nt(low, po_ref[...]).astype(LOW)
            dc_ref[span, half:] = dot_nt(low, pf_ref[...]).astype(LOW)

        by_rows(x_ref.shape[0], body)


def mlp_both(x, c, dy, weights, biases, gain, shift, fc_bias):
    tokens, width = x.shape
    half, count = width // 2, weights["fc"][0].shape[1] // CHUNK
    row, full = whole((1, width)), whole(x.shape)
    return call(
        functools.partial(mlp_both_kernel, count),
        2 * count,
        [full, full, full, whole((half, width)), whole((half, width)), row, row, row]
        + halves((width, CHUNK), count, True)
        + [pl.BlockSpec((1, CHUNK), lambda j: (0, j))]
        + halves((CHUNK, width), count, False)
        + [row],
        [full] * 4,
        [jax.ShapeDtypeStruct(x.shape, kind) for kind in (WIDE, LOW, WIDE, LOW)],
        [pltpu.VMEM(x.shape, WIDE), pltpu.VMEM(x.shape, LOW), pltpu.VMEM(x.shape, WIDE)],
        "mlp_both",
        4 * tokens * width * (width + 4 * count * CHUNK),
        (x, c, dy, *weights["proj"], biases[0], gain, shift, *weights["fc"], fc_bias, *weights["fc2"], biases[1]),
    )


def qkv_back_kernel(dq_ref, dk_ref, dv_ref, hk_ref, hv_ref, own_ref, far_ref, x_ref, dh_ref, gain_ref, dx_ref, low_ref,
                    total):
    step = pl.program_id(0)

    def chunk(grad_ref, halo_ref, kind):
        def body(weight_ref):
            grad = grad_ref[...]
            if halo_ref is not None:
                early = grad.shape[0] - BAND
                late = (grad[early:].astype(WIDE) + halo_ref[...].astype(WIDE)).astype(LOW)
                grad = jnp.concatenate([grad[:early], late], axis=0)
            total[...] += dot_nt(grad, weight_ref[...])

        @pl.when(step % 3 == kind)
        def _():
            of_half(step, 3, own_ref, far_ref, body)

    @pl.when(step == 0)
    def _():
        total[...] = jnp.zeros_like(total)

    chunk(dq_ref, None, 0)
    chunk(dk_ref, hk_ref, 1)
    chunk(dv_ref, hv_ref, 2)

    @pl.when(step == 5)
    def _():
        def body(span):
            dx = dh_ref[span] + norm_back(x_ref[span].astype(WIDE), gain_ref[...], total[span])
            dx_ref[span] = dx
            low_ref[span] = dx.astype(LOW)

        by_rows(x_ref.shape[0], body)


def qkv_back(grads, halo, weights, x, dh, gain):
    tokens, width = x.shape
    half = width // 2
    part = pl.BlockSpec((tokens, half), lambda j: (0, j // 3))
    edges = [pl.BlockSpec((BAND, half), lambda j, i=i: (i, 1 - j // 3)) for i in range(2)]
    return call(
        qkv_back_kernel,
        6,
        [part, part, part, *edges]
        + halves((width, half), 3, True)
        + [whole(x.shape), whole(x.shape), whole((1, width))],
        [whole(x.shape), whole(x.shape)],
        [jax.ShapeDtypeStruct(x.shape, WIDE), jax.ShapeDtypeStruct(x.shape, LOW)],
        [pltpu.VMEM(x.shape, WIDE)],
        "qkv_back",
        12 * tokens * width * half,
        (*grads, halo, halo, *weights, x, dh, gain),
    )


def attention_backward(stored, dh, dc, weights, small):
    x, qkv, halo, probs = stored
    *grads, edge, prefix_term = attend_back(qkv, halo, small["prefix"], probs, dc)
    dx, low = qkv_back(
        grads, lax.ppermute(edge, "tensor", [(1, 0)]), weights["qkv"], x, dh, small["gain"][0:1]
    )
    return dx, low, prefix_term


NAMES = ("qkv", "proj", "fc", "fc2")
JOIN, QKV, ATTEND, MLP = range(4)
ORDER = (
    (0, 0, 0, 0, 0), (2, 0, 0, 0, 0), (1, 0, 0, 0, 0), (0, 2, 0, 0, 0), (1, 1, 0, 0, 0),
    (2, 2, 0, 0, 0), (2, 0, 1, 0, 0), (1, 0, 1, 0, 0), (1, 0, 0, 1, 0), (0, 8, 0, 0, 0),
    (0, 0, 1, 0, 0), (1, 2, 0, 1, 0), (2, 2, 1, 0, 0), (2, 0, 2, 0, 0), (0, 0, 2, 0, 0),
    (1, 0, 2, 0, 0), (0, 2, 1, 0, 0), (2, 9, 0, 0, 0), (1, 0, 2, 1, 0), (0, 2, 2, 0, 0),
    (1, 3, 0, 0, 0), (0, 0, 3, 0, 0), (1, 2, 0, 0, 0), (2, 9, 1, 0, 0), (2, 2, 2, 0, 0),
    (1, 2, 2, 1, 0), (0, 7, 0, 0, 0), (2, 9, 2, 0, 0), (1, 0, 3, 1, 0), (0, 2, 3, 0, 0),
    (2, 6, 0, 0, 0), (1, 2, 3, 0, 0), (0, 6, 0, 0, 0), (1, 2, 2, 0, 0), (2, 7, 0, 0, 0),
    (0, 6, 1, 0, 0), (2, 6, 1, 0, 0), (1, 0, 1, 1, 0), (0, 7, 1, 0, 0), (1, 0, 3, 0, 0),
    (2, 7, 1, 0, 0), (1, 2, 1, 0, 0), (0, 6, 2, 0, 0), (2, 6, 2, 0, 0), (1, 2, 3, 1, 0),
    (0, 7, 2, 0, 0), (2, 7, 2, 0, 0), (1, 2, 1, 1, 0), (0, 6, 3, 0, 0), (0, 7, 3, 0, 0),
    (3, 0, 0, 0, 0), (3, 0, 1, 0, 0), (3, 0, 2, 0, 0), (3, 0, 3, 0, 0), (3, 0, 0, 1, 0),
    (3, 0, 1, 1, 0), (3, 0, 2, 1, 0), (3, 0, 3, 1, 0), (3, 1, 0, 0, 0), (3, 2, 0, 0, 0),
    (3, 3, 0, 0, 0), (3, 1, 0, 1, 0), (3, 2, 0, 1, 0), (3, 3, 0, 1, 0),
)
JOINED = {8: ((1, 0, 0, 0), (1, 0, 0, 1)), 9: ((8, 0, 0, 0), (8, 0, 1, 0))}
DEEP = 2
LATE = 3


def move(block, link):
    if link == 1:
        return swap(block, "section")
    count = lax.axis_size("rows")
    if link == 0:
        return lax.ppermute(block, "rows", [(i, i ^ 1) for i in range(count)])
    return lax.ppermute(block, "rows", [(i, (i + 2) % count) for i in range(count)])


def spread(shards, section, run):
    held = {(base, 0, 0, 0): shards[name] for base, name in enumerate(NAMES)}
    sent, passed, awaited = {}, [], []

    def get(key):
        if key not in held:
            base = key[0]
            if base in JOINED:
                held[key] = jnp.concatenate([get(part) for part in JOINED[base]], axis=0)
            else:
                raw = base // 2
                held[key] = jnp.where(section == base % 2, get((raw, 0, 0, 0)), get((raw, 0, 0, 1)))
        return held[key]

    for link, *key in ORDER:
        if link == 3:
            now, later = run(*key[:3], get)
            passed = [now]
            if later is not None:
                awaited.append([LATE, later])
            continue
        block, ahead = get(tuple(key)), sent.setdefault(link, [])
        behind = list(passed)
        if len(ahead) >= DEEP:
            behind.append(ahead[-DEEP])
        for entry in awaited:
            entry[0] -= 1
            if entry[0] == 0:
                behind.append(entry[1])
        if behind:
            block, *_ = lax.optimization_barrier((block, *behind))
        base, steps, over_x, over_y = key
        target = (base, steps + (link == 2), over_x + (link == 0), over_y + (link == 1))
        held[target] = move(block, link)
        ahead.append(held[target])


def pieces(matrix, layer, resolved):
    result = []
    for steps in range(4):
        for over_x in range(2):
            if matrix == 1:
                key = (9, steps, 0, 0)
                near, away = (key, 2 * over_x), (key, 2 * over_x + 1)
            elif resolved:
                near = away = ((2 * matrix + layer, steps, over_x, 0), 0)
            else:
                near, away = ((matrix, steps, over_x, 0), 0), ((matrix, steps, over_x, 1), 0)
            result.append((steps, over_x, near, away))
    return result


def join_kernel(plan, layer, rows, place_ref, *refs):
    buffers, (out_ref, sems) = refs[:-2], refs[-2:]
    section, z, x = place_ref[0], place_ref[1], place_ref[2]

    def copy(index, source):
        steps, other = plan[index][:2]
        slot = ((z + 4 - steps) % 4) * 2 + (x + other) % 2
        buffer, block = source
        return pltpu.make_async_copy(
            buffers[buffer].at[block * rows : (block + 1) * rows], out_ref.at[slot], sems.at[index]
        )

    @pl.when(section == layer)
    def _():
        for index, entry in enumerate(plan):
            copy(index, entry[2]).start()

    @pl.when(section != layer)
    def _():
        for index, entry in enumerate(plan):
            copy(index, entry[3]).start()

    for index, entry in enumerate(plan):
        copy(index, entry[2]).wait()


def joined(matrix, layer, get, shape, place):
    rows, columns = shape
    keys, plan = [], []
    resolved = any(link < 3 and base == 2 * matrix for link, base, *_ in ORDER if matrix > 1)
    for steps, over_x, *sources in pieces(matrix, layer, resolved):
        spots = []
        for key, block in sources:
            if key not in keys:
                keys.append(key)
            spots.append((keys.index(key), block))
        plan.append((steps, over_x, *spots))
    anywhere = pl.BlockSpec(memory_space=pl.ANY)
    whole = pl.pallas_call(
        functools.partial(join_kernel, plan, layer, rows),
        in_specs=[pl.BlockSpec(memory_space=pltpu.SMEM)] + [anywhere] * len(keys),
        out_specs=pl.BlockSpec(memory_space=pltpu.VMEM),
        out_shape=jax.ShapeDtypeStruct((8, rows, columns), LOW),
        scratch_shapes=[pltpu.SemaphoreType.DMA((8,))],
        name="join",
        cost_estimate=pl.CostEstimate(flops=0, bytes_accessed=4 * 8 * rows * columns, transcendentals=0),
    )(place, *[get(key) for key in keys])
    return whole.reshape(8 * rows, columns)


def forward(shards, x, dy, start, smalls, pref_count):
    section, rows = lax.axis_index("section"), lax.axis_index("rows")
    weights, kept, outputs, slopes = [{}, {}], [None, None], [None, None], []

    def run(kind, matrix, layer, get):
        small, mine = smalls[layer], weights[layer]
        if kind == JOIN:
            name = NAMES[matrix]
            place = jnp.stack([section, rows // 2, rows % 2]).astype(jnp.int32)
            near = joined(matrix, layer, get, shards[name].shape, place)
            mine[name] = (near, swap(near, "tensor"))
            return mine[name]
        if kind == QKV:
            source = outputs[0][1] if layer else x
            qkv, edge = qkv_forward(source, small["gain"][0:1], small["shift"][0:1], mine["qkv"], small["qkv"])
            kept[layer] = (source, qkv, lax.ppermute(edge, "tensor", [(0, 1)]))
            return qkv, kept[layer][2]
        if kind == ATTEND:
            source, qkv, halo = kept[layer]
            c, probs = attend(pref_count, qkv, halo, small["prefix"], start)
            kept[layer] = (source, qkv, halo, probs, c)
            return c, None
        source, qkv, halo, probs, c = kept[layer]
        kept[layer] = (source, qkv, halo, probs)
        biases = (small["out"][0:1], small["out"][1:2])
        norm = (small["gain"][1:2], small["shift"][1:2])
        if layer:
            *outputs[1], dh, dc = mlp_both(source, c, dy, mine, biases, *norm, small["fc"])
            slopes.extend((dh, dc))
        else:
            h, slope, *outputs[0] = mlp_forward(source, c, mine, biases, *norm, small["fc"])
            slopes.extend((h, slope))
        return slopes[-1], None

    if lax.axis_size("rows") == 8:
        spread(shards, section, run)
    else:
        for name in NAMES:
            near = lax.all_gather(shards[name], ("section", "rows"), axis=0, tiled=True)
            near = near.reshape(2, -1, near.shape[1])
            far = swap(near, "tensor")
            for layer in range(2):
                weights[layer][name] = (near[layer], far[layer])
        for link, *stage in ORDER:
            if link == 3 and stage[0] != JOIN:
                run(*stage[:3], None)
    return weights, kept, outputs, slopes


def on_device(
    tokens,
    segment_ids,
    cotangent,
    ln_gain,
    ln_bias,
    w_qkv,
    query_key_value_bias,
    w_proj,
    w_fc,
    fc_bias,
    w_fc2,
    out_bias,
    prefix_embed,
    rep_w1,
    rep_b1,
    rep_w2,
    rep_b2,
):
    share, width = tokens.shape[1:]
    section, core = lax.axis_index("section"), lax.axis_index("tensor")
    rows_index, rows = lax.axis_index("rows"), lax.axis_size("rows")
    half = rep_w2.shape[-1]
    pref_count = prefix_embed.shape[0]

    shards = {
        "qkv": w_qkv[0].astype(LOW).reshape(w_qkv.shape[1], -1),
        "proj": w_proj[0].astype(LOW),
        "fc": w_fc[0].astype(LOW),
        "fc2": w_fc2[0].astype(LOW),
    }
    rep_hidden = jnp.tanh(jnp.dot(prefix_embed, rep_w1, precision=HIGHEST) + rep_b1)
    prefix = jnp.einsum("pm,mcd->pcd", rep_hidden, rep_w2[:, 0], precision=HIGHEST) + rep_b2[0]
    prefix = prefix.astype(LOW).astype(WIDE)
    prefix = jnp.pad(prefix, ((0, PREP - pref_count), (0, 0), (0, 0)))
    parts = [ln_gain[0], ln_bias[0], out_bias[0], query_key_value_bias[0], fc_bias[0], prefix]
    packed = jnp.concatenate([part.reshape(-1) for part in parts])
    near = jnp.stack([packed, swap(packed, "tensor")])
    away = swap(near, "section")
    smalls = []
    for layer in range(2):
        cut, place = [], 0
        chosen = jnp.where(section == layer, near, away)
        for part in parts:
            cut.append([chosen[h, place : place + part.size].reshape(part.shape) for h in range(2)])
            place += part.size
        smalls.append(
            {
                "gain": cut[0][0],
                "shift": cut[1][0],
                "out": cut[2][0],
                "qkv": jnp.concatenate([cut[3][h].reshape(1, -1) for h in range(2)], axis=1),
                "fc": jnp.concatenate([cut[4][h].reshape(1, -1) for h in range(2)], axis=1),
                "prefix": jnp.concatenate(
                    [cut[5][h].reshape(PREP, -1).astype(LOW) for h in range(2)], axis=1
                ),
            }
        )

    own = section
    segments = lax.dynamic_index_in_dim(segment_ids, own, 0, keepdims=False).reshape(-1)
    mine = lax.dynamic_slice_in_dim(segments, core * share, share)
    start = jnp.sum(segments[:, None] < mine[None, :], axis=0, dtype=jnp.int32)
    start = (start - core * share + BAND)[None]

    x = lax.dynamic_index_in_dim(tokens, own, 0, keepdims=False)
    dy = lax.dynamic_index_in_dim(cotangent, own, 0, keepdims=False)
    weights, (kept0, kept1), ((y0, low0), (y1, low1)), (h, slope, dh, dc) = forward(
        shards, x, dy, start, smalls, pref_count
    )
    dy = lax.dynamic_index_in_dim(cotangent, own, 0, keepdims=False)
    def settle(first, second, first_low, second_low):
        keep = jnp.where(section == 0, first, second)
        got = swap(jnp.where(section == 0, second_low, first_low), "section").astype(WIDE)
        return jnp.where(section == 0, jnp.stack([keep, got]), jnp.stack([got, keep]))[None]

    acts = settle(y0, y1, low0, low1)
    g1, down1, pre1 = attention_backward(kept1, dh, dc, weights[1], smalls[1])
    down1, acts = lax.optimization_barrier((down1, acts))
    dh, dc = mlp_back(down1, h, smalls[0]["gain"][1:2], slope, weights[0])
    g0, down0, pre0 = attention_backward(kept0, dh, dc, weights[0], smalls[0])
    in_grads = settle(g0, g1, down0, down1)

    pre0, pre1 = [pre.reshape(2, PREP, 2, half) for pre in (pre0, pre1)]
    keep = jnp.where(section == 0, pre0, pre1)
    layer_terms = keep + swap(jnp.where(section == 0, pre1, pre0), "section")
    layer_terms, _ = lax.optimization_barrier((layer_terms, down0))
    total = layer_terms[:, :, 0] + swap(layer_terms[:, :, 1], "tensor")
    total = all_sum(total[:, :pref_count], ("rows",))
    grad_b2 = jnp.sum(total, axis=1)
    mid_part = rep_w1.shape[1] // rows
    width_part = width // rows
    hidden_part = lax.dynamic_slice_in_dim(rep_hidden, rows_index * mid_part, mid_part, 1)
    grad_w2 = jnp.einsum("pm,cpd->mcd", hidden_part, total, precision=HIGHEST)
    hidden_term = jnp.einsum("cpd,mcd->pm", total, rep_w2[:, 0], precision=HIGHEST)
    grad_hidden = all_sum(hidden_term, ("section", "tensor"))
    grad_pre = grad_hidden * (1.0 - rep_hidden * rep_hidden)
    grad_b1 = jnp.sum(grad_pre, axis=0)
    embed_part = lax.dynamic_slice_in_dim(prefix_embed, rows_index * width_part, width_part, 1)
    grad_w1 = jnp.einsum("pd,pm->dm", embed_part, grad_pre, precision=HIGHEST)
    weight_part = lax.dynamic_slice_in_dim(rep_w1, rows_index * width_part, width_part, 0)
    grad_embed = jnp.einsum("pm,dm->pd", grad_pre, weight_part, precision=HIGHEST)
    return (acts, in_grads, grad_embed, grad_w1, grad_b1, grad_w2[:, None], grad_b2[None])


def solution(mesh):
    return jax.shard_map(
        on_device,
        mesh=mesh,
        in_specs=(
            P(None, ("rows", "tensor"), None),
            P(None, "rows", None),
            P(None, ("rows", "tensor"), None),
            P("section", None, None),
            P("section", None, None),
            P("section", "rows", None, "tensor"),
            P("section", None, "tensor"),
            P("section", ("tensor", "rows"), None),
            P("section", "rows", "tensor"),
            P("section", "tensor"),
            P("section", ("tensor", "rows"), None),
            P("section", None, None),
            P(),
            P(),
            P(),
            P(None, "section", None, "tensor"),
            P("section", None, "tensor"),
        ),
        out_specs=(
            P("section", None, ("rows", "tensor"), None),
            P("section", None, ("rows", "tensor"), None),
            P(None, "rows"),
            P("rows", None),
            P(),
            P("rows", "section", None, "tensor"),
            P("section", None, "tensor"),
        ),
        check_vma=False,
    )
```

```python
import functools

import jax
import jax.numpy as jnp
from jax import lax
from jax.experimental import pallas as pl
from jax.experimental.pallas import tpu as pltpu
from jax.sharding import PartitionSpec as P

HEAD = 64
EPSILON = 1e-05
NEGATIVE = -1000000000.0
HIGHEST = lax.Precision.HIGHEST
LOW = jnp.bfloat16
WIDE = jnp.float32
QB = 128
BAND = 256
KB = QB + BAND
PREP = 16


def swap(block, axis):
    return lax.ppermute(block, axis, [(0, 1), (1, 0)])


def all_sum(block, axes):
    for axis in axes:
        count = lax.axis_size(axis)
        if count & (count - 1):
            block = lax.psum(block, axis)
            continue
        bit = 1
        while bit < count:
            block = block + lax.ppermute(block, axis, [(i, i ^ bit) for i in range(count)])
            bit *= 2
    return block


def layer_norm(values, gain, shift):
    centre = values - jnp.mean(values, axis=-1, keepdims=True)
    spread = jnp.mean(centre * centre, axis=-1, keepdims=True)
    return centre * lax.rsqrt(spread + EPSILON) * gain + shift


def norm_back(values, gain, grad):
    centre = values - jnp.mean(values, axis=-1, keepdims=True)
    inverse = lax.rsqrt(jnp.mean(centre * centre, axis=-1, keepdims=True) + EPSILON)
    normal = centre * inverse
    scaled = grad * gain
    return inverse * (
        scaled
        - jnp.mean(scaled, axis=-1, keepdims=True)
        - normal * jnp.mean(scaled * normal, axis=-1, keepdims=True)
    )


def gelu_parts(values):
    root = 0.7978845608028654
    square = values * values
    inner = jnp.tanh(root * values * (1.0 + 0.044715 * square))
    half = 0.5 * (1.0 + inner)
    slope = half + 0.5 * values * (1.0 - inner * inner) * root * (1.0 + 3 * 0.044715 * square)
    return values * half, slope


def dot_nn(left, right):
    return jnp.dot(left, right, preferred_element_type=WIDE)


def dot_nt(left, right):
    return lax.dot_general(left, right, (((1,), (1,)), ((), ())), preferred_element_type=WIDE)


def stacked(pair):
    lane = lax.broadcasted_iota(jnp.int32, pair.shape, 1)
    zero = jnp.zeros_like(pair)
    return jnp.concatenate(
        [jnp.where(lane < HEAD, pair, zero), jnp.where(lane >= HEAD, pair, zero)], axis=0
    )


def unstacked(both):
    lane = lax.broadcasted_iota(jnp.int32, (QB, 2 * HEAD), 1)
    return jnp.where(lane < HEAD, both[:QB], both[QB:])


def dot_tn(left, right):
    return lax.dot_general(left, right, (((0,), (0,)), ((), ())), preferred_element_type=WIDE)


def lower():
    row = lax.broadcasted_iota(jnp.int32, (QB, 2 * QB), 0)
    lane = lax.broadcasted_iota(jnp.int32, (QB, 2 * QB), 1)
    return row <= jnp.where(lane < QB, lane, lane - QB)


def fold(band, near):
    return jnp.concatenate([jnp.where(near, band[BAND:], band[:QB]), band[QB:BAND]], axis=0)


def unfold(folded, near):
    zero = jnp.zeros((QB, 2 * QB), folded.dtype)
    edge = folded[:QB]
    return jnp.concatenate(
        [jnp.where(near, zero, edge), folded[QB:], jnp.where(near, edge, zero)], axis=0
    )


def fill_places(places):
    row = lax.broadcasted_iota(jnp.int32, (QB, 2 * QB), 0)
    places[:QB] = jnp.where(lower(), row + BAND, row)
    places[QB:] = row + QB


def fill_keys(scratch, prefix_ref, halo_ref, own_ref):
    scratch[:PREP] = prefix_ref[...]
    scratch[PREP : PREP + BAND] = halo_ref[...]
    scratch[PREP + BAND :] = own_ref[...]


def masked_scores(queries, keys, start_ref, block, pref_count, places, near):
    pre = dot_nt(keys[:PREP], queries)
    pre = jnp.where(
        lax.broadcasted_iota(jnp.int32, pre.shape, 0) < pref_count, pre, NEGATIVE
    )
    band = fold(dot_nt(keys[pl.ds(PREP + block * QB, KB)], queries), near)
    first = start_ref[:, block * QB : (block + 1) * QB] - block * QB
    first = jnp.concatenate([first, first], axis=1)
    return pre, jnp.where(places[...] >= first, band, NEGATIVE)


def attend_kernel(pref_count, q_ref, k_ref, v_ref, hk_ref, hv_ref, pk_ref, pv_ref, start_ref,
                  c_ref, probs_ref, keys, vals, places):
    fill_keys(keys, pk_ref, hk_ref, k_ref)
    fill_keys(vals, pv_ref, hv_ref, v_ref)
    fill_places(places)
    near = lower()
    for block in range(q_ref.shape[0] // QB):
        span = slice(block * QB, (block + 1) * QB)
        seen = pl.ds(PREP + block * QB, KB)
        queries = stacked(q_ref[span, :] * jnp.asarray(HEAD ** (-0.5), LOW))
        pre, band = masked_scores(queries, keys, start_ref, block, pref_count, places, near)
        top = jnp.maximum(jnp.max(pre, axis=0, keepdims=True), jnp.max(band, axis=0, keepdims=True))
        pre = jnp.exp(pre - top)
        band = jnp.exp(band - top)
        total = jnp.sum(pre, axis=0, keepdims=True) + jnp.sum(band, axis=0, keepdims=True)
        inverse = 1.0 / total
        probs = jnp.concatenate([pre * inverse, unfold(band * inverse, near)], axis=0).astype(LOW)
        probs_ref[0, block] = probs
        out = dot_tn(probs, jnp.concatenate([vals[:PREP], vals[seen]], axis=0))
        c_ref[span, :] = unstacked(out).astype(LOW)


def attend_back_kernel(q_ref, k_ref, v_ref, hk_ref, hv_ref, pk_ref, pv_ref, probs_ref, dc_ref,
                       dq_ref, dk_ref, dv_ref, edge_ref, prefix_ref, keys, vals, dkeys, dvals):
    fill_keys(keys, pk_ref, hk_ref, k_ref)
    fill_keys(vals, pv_ref, hv_ref, v_ref)
    dkeys[...] = jnp.zeros_like(dkeys)
    dvals[...] = jnp.zeros_like(dvals)
    scaling = HEAD ** (-0.5)
    for block in range(q_ref.shape[0] // QB):
        span = slice(block * QB, (block + 1) * QB)
        seen = pl.ds(PREP + block * QB, KB)
        queries = stacked(q_ref[span, :] * jnp.asarray(scaling, LOW))
        grads = stacked(dc_ref[span, :])
        low = probs_ref[0, block]
        probs = low.astype(WIDE)
        dprobs = dot_nt(jnp.concatenate([vals[:PREP], vals[seen]], axis=0), grads)
        inside = jnp.sum(probs * dprobs, axis=0, keepdims=True)
        slope = (probs * (dprobs - inside)).astype(LOW)
        terms = dot_nn(low, grads)
        dvals[:PREP] += terms[:PREP]
        dvals[seen] += terms[PREP:]
        terms = dot_nn(slope, queries)
        dkeys[:PREP] += terms[:PREP]
        dkeys[seen] += terms[PREP:]
        out = dot_tn(slope, jnp.concatenate([keys[:PREP], keys[seen]], axis=0))
        dq_ref[span, :] = (unstacked(out) * scaling).astype(LOW)
    dk_ref[...] = dkeys[PREP + BAND :].astype(LOW)
    dv_ref[...] = dvals[PREP + BAND :].astype(LOW)
    edge_ref[:BAND] = dkeys[PREP : PREP + BAND].astype(LOW)
    edge_ref[BAND:] = dvals[PREP : PREP + BAND].astype(LOW)
    prefix_ref[:PREP] = dkeys[:PREP]
    prefix_ref[PREP:] = dvals[:PREP]


def column(rows, place=lambda half, pair: 0, per=0):
    if per == 0:
        return pl.BlockSpec((rows, 2 * HEAD), lambda i: (0, i))
    return pl.BlockSpec((rows, 2 * HEAD), lambda i: (0, place(i // per) + i % per))


def attention_specs(tokens, per):
    return [
        column(tokens, lambda half: 3 * per * half, per),
        column(tokens, lambda half: 3 * per * half + per, per),
        column(tokens, lambda half: 3 * per * half + 2 * per, per),
        column(BAND, lambda half: 2 * per * (1 - half), per),
        column(BAND, lambda half: 2 * per * (1 - half) + per, per),
        column(PREP, lambda half: 2 * per * half, per),
        column(PREP, lambda half: 2 * per * half + per, per),
    ]


def probs_spec(blocks):
    return pl.BlockSpec((1, blocks, PREP + KB, 2 * QB), lambda i: (i, 0, 0, 0))


def attend(pref_count, qkv, halo, prefix, start):
    tokens, width = qkv.shape[0], qkv.shape[1] // 3
    pairs, blocks = width // (2 * HEAD), tokens // QB
    return pl.pallas_call(
        functools.partial(attend_kernel, pref_count),
        grid=(pairs,),
        in_specs=attention_specs(tokens, pairs // 2) + [pl.BlockSpec((1, tokens), lambda i: (0, 0))],
        out_specs=[column(tokens), probs_spec(blocks)],
        out_shape=[
            jax.ShapeDtypeStruct((tokens, width), LOW),
            jax.ShapeDtypeStruct((pairs, blocks, PREP + KB, 2 * QB), LOW),
        ],
        scratch_shapes=[
            pltpu.VMEM((PREP + BAND + tokens, 2 * HEAD), LOW),
            pltpu.VMEM((PREP + BAND + tokens, 2 * HEAD), LOW),
            pltpu.VMEM((2 * QB, 2 * QB), jnp.int32),
        ],
        name="attend",
        cost_estimate=pl.CostEstimate(flops=12 * 10**9, bytes_accessed=2 * qkv.size, transcendentals=0),
    )(qkv, qkv, qkv, halo, halo, prefix, prefix, start)


def attend_back(qkv, halo, prefix, probs, grad):
    tokens, width = qkv.shape[0], qkv.shape[1] // 3
    pairs, blocks = width // (2 * HEAD), tokens // QB
    keys = PREP + BAND + tokens
    sizes = [(tokens, LOW)] * 3 + [(2 * BAND, LOW), (2 * PREP, WIDE)]
    return pl.pallas_call(
        attend_back_kernel,
        grid=(pairs,),
        in_specs=attention_specs(tokens, pairs // 2) + [probs_spec(blocks), column(tokens)],
        out_specs=[column(rows) for rows, _ in sizes],
        out_shape=[jax.ShapeDtypeStruct((rows, width), kind) for rows, kind in sizes],
        scratch_shapes=[
            pltpu.VMEM((keys, 2 * HEAD), LOW),
            pltpu.VMEM((keys, 2 * HEAD), LOW),
            pltpu.VMEM((keys, 2 * HEAD), WIDE),
            pltpu.VMEM((keys, 2 * HEAD), WIDE),
        ],
        name="attend_back",
        cost_estimate=pl.CostEstimate(flops=16 * 10**9, bytes_accessed=4 * qkv.size, transcendentals=0),
    )(qkv, qkv, qkv, halo, halo, prefix, prefix, probs, grad)


CHUNK = 512
ROWS = 128


def by_rows(total, body, step=ROWS):
    @pl.loop(0, total // step)
    def _(index):
        body(pl.ds(pl.multiple_of(index * step, step), step))


def of_half(step, count, own_ref, far_ref, body):
    @pl.when(step < count)
    def _():
        body(own_ref)

    @pl.when(step >= count)
    def _():
        body(far_ref)


def halves(shape, count, across):
    def spec(place):
        return pl.BlockSpec(shape, lambda j: (0, place(j)) if across else (place(j), 0))

    return [spec(lambda j: jnp.minimum(j, count - 1)), spec(lambda j: jnp.maximum(j - count, 0))]


def whole(shape):
    return pl.BlockSpec(shape, lambda j: (0,) * len(shape))


def slab(index, tokens, width, part=0):
    return pl.BlockSpec((None, tokens, width), lambda j: (index, part, 0))


def call(kernel, grid, in_specs, out_specs, out_shape, scratch, name, flops, operands, buffer=None):
    size, count = sum(o.size * o.dtype.itemsize for o in operands), len(operands)
    body, aliases = kernel, {}
    if buffer is not None:
        in_specs, operands = in_specs + [pl.BlockSpec(memory_space=pl.ANY)], (*operands, buffer)
        aliases = {count: 0}

        def body(*refs):
            kernel(*refs[:count], *refs[count + 1 :])

    return pl.pallas_call(
        body,
        grid=(grid,),
        in_specs=in_specs,
        out_specs=out_specs,
        out_shape=out_shape,
        input_output_aliases=aliases,
        scratch_shapes=scratch,
        name=name,
        compiler_params=pltpu.CompilerParams(vmem_limit_bytes=56 * 2**20),
        cost_estimate=pl.CostEstimate(flops=flops, bytes_accessed=size, transcendentals=0),
    )(*operands)


def qkv_kernel(x_ref, gain_ref, shift_ref, own_ref, far_ref, bias_ref, out_ref, halo_ref, normed):
    step = pl.program_id(0)

    @pl.when(step == 0)
    def _():
        def body(span):
            normed[span] = layer_norm(
                x_ref[span].astype(WIDE), gain_ref[...], shift_ref[...]
            ).astype(LOW)

        by_rows(x_ref.shape[0], body)

    def body(weight_ref):
        out_ref[...] = (dot_nn(normed[...], weight_ref[...]) + bias_ref[...]).astype(LOW)

    of_half(step, 3, own_ref, far_ref, body)

    @pl.when(step % 3 != 0)
    def _():
        halo_ref[...] = out_ref[out_ref.shape[0] - BAND :]


def qkv_forward(x, gain, shift, weights, bias):
    tokens, width = x.shape
    half = weights[0].shape[1] // 3
    return call(
        qkv_kernel,
        6,
        [whole(x.shape), whole((1, width)), whole((1, width))]
        + halves((width, half), 3, True)
        + [pl.BlockSpec((1, half), lambda j: (0, j))],
        [
            pl.BlockSpec((tokens, half), lambda j: (0, j)),
            pl.BlockSpec((BAND, half), lambda j: (0, 2 * (j // 3) + jnp.maximum(j % 3 - 1, 0))),
        ],
        [
            jax.ShapeDtypeStruct((tokens, 6 * half), LOW),
            jax.ShapeDtypeStruct((BAND, 4 * half), LOW),
        ],
        [pltpu.VMEM(x.shape, LOW)],
        "qkv",
        12 * tokens * width * half,
        (x, gain, shift, *weights, bias),
    )


def mlp_kernel(count, x_ref, c_ref, po_ref, pf_ref, b0_ref, gain_ref, shift_ref, fo_ref, ff_ref, bias_ref, wo_ref,
               wf_ref, b1_ref, y_ref, h_ref, slope_ref, low_ref, normed):
    step = pl.program_id(0)
    half = po_ref.shape[0]

    @pl.when(step == 0)
    def _():
        def body(span):
            h = x_ref[span].astype(WIDE) + (
                dot_nn(c_ref[span, :half], po_ref[...])
                + dot_nn(c_ref[span, half:], pf_ref[...])
                + b0_ref[...]
            )
            h_ref[span] = h
            normed[span] = layer_norm(h, gain_ref[...], shift_ref[...]).astype(LOW)
            y_ref[span] = h + b1_ref[...]

        by_rows(x_ref.shape[0], body)

    def half_body(up_ref, down_ref):
        def body(span):
            active, slope = gelu_parts(dot_nn(normed[span], up_ref[...]) + bias_ref[...])
            slope_ref[span] = slope.astype(LOW)
            y_ref[span] += dot_nn(active.astype(LOW), down_ref[...])

        by_rows(x_ref.shape[0], body, 256)

    of_half(step, count, (fo_ref, wo_ref), (ff_ref, wf_ref), lambda refs: half_body(*refs))

    @pl.when(step == 2 * count - 1)
    def _():
        low_ref[...] = y_ref[...].astype(LOW)


def mlp_forward(x, c, weights, biases, gain, shift, fc_bias):
    tokens, width = x.shape
    half, count = width // 2, weights["fc"][0].shape[1] // CHUNK
    row = whole((1, width))
    return call(
        functools.partial(mlp_kernel, count),
        2 * count,
        [whole(x.shape), whole(c.shape), whole((half, width)), whole((half, width)), row, row, row]
        + halves((width, CHUNK), count, True)
        + [pl.BlockSpec((1, CHUNK), lambda j: (0, j))]
        + halves((CHUNK, width), count, False)
        + [row],
        [
            slab(0, tokens, width),
            whole(x.shape),
            pl.BlockSpec((tokens, CHUNK), lambda j: (0, j)),
            whole(x.shape),
        ],
        [
            jax.ShapeDtypeStruct((2, tokens, width), WIDE),
            jax.ShapeDtypeStruct(x.shape, WIDE),
            jax.ShapeDtypeStruct((tokens, 2 * count * CHUNK), LOW),
            jax.ShapeDtypeStruct(x.shape, LOW),
        ],
        [pltpu.VMEM(x.shape, LOW)],
        "mlp",
        2 * tokens * width * (width + 4 * count * CHUNK),
        (x, c, *weights["proj"], biases[0], gain, shift, *weights["fc"], fc_bias, *weights["fc2"], biases[1]),
    )


def mlp_back_kernel(count, dy_ref, h_ref, gain_ref, slope_ref, wo_ref, wf_ref, fo_ref, ff_ref, po_ref, pf_ref,
                    dh_ref, dc_ref, total):
    step = pl.program_id(0)
    half = po_ref.shape[0]

    def half_body(first, up_ref, down_ref):
        def body(span):
            du = (dot_nt(dy_ref[span], down_ref[...]) * slope_ref[span].astype(WIDE)).astype(LOW)
            dm = dot_nt(du, up_ref[...])
            total[span] = dm if first else total[span] + dm

        by_rows(dy_ref.shape[0], body, 256)

    @pl.when(step == 0)
    def _():
        half_body(True, fo_ref, wo_ref)

    @pl.when((step > 0) & (step < count))
    def _():
        half_body(False, fo_ref, wo_ref)

    @pl.when(step >= count)
    def _():
        half_body(False, ff_ref, wf_ref)

    @pl.when(step == 2 * count - 1)
    def _():
        def body(span):
            dh = dy_ref[span].astype(WIDE) + norm_back(h_ref[span], gain_ref[...], total[span])
            dh_ref[span] = dh
            low = dh.astype(LOW)
            dc_ref[span, :half] = dot_nt(low, po_ref[...]).astype(LOW)
            dc_ref[span, half:] = dot_nt(low, pf_ref[...]).astype(LOW)

        by_rows(dy_ref.shape[0], body)


def mlp_back(dy, h, gain, slope, weights):
    tokens, width = dy.shape
    half, count = width // 2, weights["fc"][0].shape[1] // CHUNK
    return call(
        functools.partial(mlp_back_kernel, count),
        2 * count,
        [whole(dy.shape), whole(dy.shape), whole((1, width)), pl.BlockSpec((tokens, CHUNK), lambda j: (0, j))]
        + halves((CHUNK, width), count, False)
        + halves((width, CHUNK), count, True)
        + [whole((half, width)), whole((half, width))],
        [whole(dy.shape), whole(dy.shape)],
        [jax.ShapeDtypeStruct(dy.shape, WIDE), jax.ShapeDtypeStruct(dy.shape, LOW)],
        [pltpu.VMEM(dy.shape, WIDE)],
        "mlp_back",
        2 * tokens * width * (width + 4 * count * CHUNK),
        (dy, h, gain, slope, *weights["fc2"], *weights["fc"], *weights["proj"]),
    )


def mlp_both_kernel(count, x_ref, c_ref, dy_ref, po_ref, pf_ref, b0_ref, gain_ref, shift_ref, fo_ref, ff_ref, bias_ref,
                    wo_ref, wf_ref, b1_ref, y_ref, low_ref, dh_ref, dc_ref, h_ref, normed, total):
    step = pl.program_id(0)
    half = po_ref.shape[0]

    @pl.when(step == 0)
    def _():
        def body(span):
            h = x_ref[span].astype(WIDE) + (
                dot_nn(c_ref[span, :half], po_ref[...])
                + dot_nn(c_ref[span, half:], pf_ref[...])
                + b0_ref[...]
            )
            h_ref[span] = h
            normed[span] = layer_norm(h, gain_ref[...], shift_ref[...]).astype(LOW)
            y_ref[span] = h + b1_ref[...]
            total[span] = jnp.zeros_like(h)

        by_rows(x_ref.shape[0], body)

    def half_body(up_ref, down_ref):
        def body(span):
            active, slope = gelu_parts(dot_nn(normed[span], up_ref[...]) + bias_ref[...])
            du = (dot_nt(dy_ref[span], down_ref[...]) * slope).astype(LOW)
            y_ref[span] += dot_nn(active.astype(LOW), down_ref[...])
            total[span] += dot_nt(du, up_ref[...])

        by_rows(x_ref.shape[0], body, 256)

    of_half(step, count, (fo_ref, wo_ref), (ff_ref, wf_ref), lambda refs: half_body(*refs))

    @pl.when(step == 2 * count - 1)
    def _():
        def body(span):
            low_ref[span] = y_ref[span].astype(LOW)
            dh = dy_ref[span].astype(WIDE) + norm_back(h_ref[span], gain_ref[...], total[span])
            dh_ref[span] = dh
            low = dh.astype(LOW)
            dc_ref[span, :half] = dot_nt(low, po_ref[...]).astype(LOW)
            dc_ref[span, half:] = dot_nt(low, pf_ref[...]).astype(LOW)

        by_rows(x_ref.shape[0], body)


def mlp_both(acts, x, c, dy, weights, biases, gain, shift, fc_bias):
    tokens, width = x.shape
    half, count = width // 2, weights["fc"][0].shape[1] // CHUNK
    row, full = whole((1, width)), whole(x.shape)
    return call(
        functools.partial(mlp_both_kernel, count),
        2 * count,
        [full, full, full, whole((half, width)), whole((half, width)), row, row, row]
        + halves((width, CHUNK), count, True)
        + [pl.BlockSpec((1, CHUNK), lambda j: (0, j))]
        + halves((CHUNK, width), count, False)
        + [row],
        [slab(1, tokens, width), full, full, full],
        [jax.ShapeDtypeStruct(acts.shape, WIDE)]
        + [jax.ShapeDtypeStruct(x.shape, kind) for kind in (LOW, WIDE, LOW)],
        [pltpu.VMEM(x.shape, WIDE), pltpu.VMEM(x.shape, LOW), pltpu.VMEM(x.shape, WIDE)],
        "mlp_both",
        4 * tokens * width * (width + 4 * count * CHUNK),
        (x, c, dy, *weights["proj"], biases[0], gain, shift, *weights["fc"], fc_bias, *weights["fc2"], biases[1]),
        acts,
    )


def qkv_back_kernel(reach, dq_ref, dk_ref, dv_ref, hk_ref, hv_ref, own_ref, far_ref, x_ref, dh_ref, gain_ref, other_ref,
                    section_ref, dx_ref, low_ref, total):
    step = pl.program_id(0)

    def chunk(grad_ref, halo_ref, kind):
        def body(weight_ref):
            grad = grad_ref[...]
            early = grad.shape[0] - reach
            if halo_ref is not None and reach:
                late = (grad[early:].astype(WIDE) + halo_ref[...].astype(WIDE)).astype(LOW)
                grad = jnp.concatenate([grad[:early], late], axis=0) if early else late
            total[...] += dot_nt(grad, weight_ref[...])

        @pl.when(step % 3 == kind)
        def _():
            of_half(step, 3, own_ref, far_ref, body)

    @pl.when(step == 0)
    def _():
        total[...] = jnp.zeros_like(total)

    chunk(dq_ref, None, 0)
    chunk(dk_ref, hk_ref, 1)
    chunk(dv_ref, hv_ref, 2)

    @pl.when(step == 5)
    def _():
        def body(span):
            dx = dh_ref[span] + norm_back(x_ref[span].astype(WIDE), gain_ref[...], total[span])
            dx_ref[span] = dx
            low = dx.astype(LOW)
            low_ref[span] = jnp.where(section_ref[0] == 0, other_ref[span], low)

        by_rows(x_ref.shape[0], body)


def qkv_back(grads, halo, weights, x, dh, gain, other, section, layer, buffer=None, part=0, parts=1):
    width = x.shape[1]
    tokens, half = x.shape[0] // parts, width // 2
    reach = BAND if part == parts - 1 else 0
    piece = pl.BlockSpec((tokens, half), lambda j: (part, j // 3))
    edges = [pl.BlockSpec((BAND, half), lambda j, i=i: (i, 1 - j // 3)) for i in range(2)]
    mine, shape = pl.BlockSpec((tokens, width), lambda j: (part, 0)), (tokens, width)
    return call(
        functools.partial(qkv_back_kernel, reach),
        6,
        [piece, piece, piece, *edges]
        + halves((width, half), 3, True)
        + [mine, mine, whole((1, width)), mine, pl.BlockSpec(memory_space=pltpu.SMEM)],
        [slab(layer, tokens, width, part), whole(shape)],
        [jax.ShapeDtypeStruct((2, *x.shape), WIDE), jax.ShapeDtypeStruct(shape, LOW)],
        [pltpu.VMEM(shape, WIDE)],
        "qkv_back",
        12 * tokens * width * half,
        (*grads, halo, halo, *weights, x, dh, gain, other, section),
        buffer,
    )


def take_kernel(section_ref, got_ref, held_ref, out_ref):
    out_ref[0] = got_ref[...].astype(WIDE)


def take(section, got, buffer, start=0):
    rows, width = got.shape
    step = min(256, rows)
    base = start // step
    return pl.pallas_call(
        take_kernel,
        grid_spec=pltpu.PrefetchScalarGridSpec(
            num_scalar_prefetch=1,
            grid=(rows // step,),
            in_specs=[
                pl.BlockSpec((step, width), lambda i, s: (i, 0)),
                pl.BlockSpec(memory_space=pl.ANY),
            ],
            out_specs=pl.BlockSpec((1, step, width), lambda i, s: (1 - s[0], base + i, 0)),
        ),
        out_shape=jax.ShapeDtypeStruct(buffer.shape, WIDE),
        input_output_aliases={2: 0},
        name="take",
        cost_estimate=pl.CostEstimate(flops=0, bytes_accessed=6 * got.size, transcendentals=0),
    )(section, got, buffer)


def attention_backward(stored, dh, dc, weights, small, between):
    x, qkv, halo, probs = stored
    *grads, edge, prefix_term = attend_back(qkv, halo, small["prefix"], probs, dc)
    edge = lax.ppermute(edge, "tensor", [(1, 0)])
    result = between(prefix_term)
    dh, _ = lax.optimization_barrier((dh, result))
    return (grads, edge, weights["qkv"], x, dh, small["gain"][0:1]), result


NAMES = ("qkv", "proj", "fc", "fc2")
JOIN, QKV, ATTEND, MLP = range(4)
ORDER = (
    (0, 0, 0, 0, 0), (2, 0, 0, 0, 0), (1, 0, 0, 0, 0), (0, 2, 0, 0, 0), (1, 1, 0, 0, 0),
    (2, 2, 0, 0, 0), (2, 0, 1, 0, 0), (1, 0, 1, 0, 0), (1, 0, 0, 1, 0), (0, 8, 0, 0, 0),
    (0, 0, 1, 0, 0), (1, 2, 0, 1, 0), (2, 2, 1, 0, 0), (2, 0, 2, 0, 0), (0, 0, 2, 0, 0),
    (1, 0, 2, 0, 0), (0, 2, 1, 0, 0), (2, 9, 0, 0, 0), (1, 0, 2, 1, 0), (0, 2, 2, 0, 0),
    (1, 3, 0, 0, 0), (0, 0, 3, 0, 0), (1, 2, 0, 0, 0), (2, 9, 1, 0, 0), (2, 2, 2, 0, 0),
    (1, 2, 2, 1, 0), (0, 7, 0, 0, 0), (2, 9, 2, 0, 0), (1, 0, 3, 1, 0), (0, 2, 3, 0, 0),
    (2, 6, 0, 0, 0), (1, 2, 3, 0, 0), (0, 6, 0, 0, 0), (1, 2, 2, 0, 0), (2, 7, 0, 0, 0),
    (0, 6, 1, 0, 0), (2, 6, 1, 0, 0), (1, 0, 1, 1, 0), (0, 7, 1, 0, 0), (1, 0, 3, 0, 0),
    (2, 7, 1, 0, 0), (1, 2, 1, 0, 0), (0, 6, 2, 0, 0), (2, 6, 2, 0, 0), (1, 2, 3, 1, 0),
    (0, 7, 2, 0, 0), (2, 7, 2, 0, 0), (1, 2, 1, 1, 0), (0, 6, 3, 0, 0), (0, 7, 3, 0, 0),
    (3, 0, 0, 0, 0), (3, 0, 1, 0, 0), (3, 0, 2, 0, 0), (3, 0, 3, 0, 0), (3, 0, 0, 1, 0),
    (3, 0, 1, 1, 0), (3, 0, 2, 1, 0), (3, 0, 3, 1, 0), (3, 1, 0, 0, 0), (3, 2, 0, 0, 0),
    (3, 3, 0, 0, 0), (3, 1, 0, 1, 0), (3, 2, 0, 1, 0), (3, 3, 0, 1, 0),
)
JOINED = {8: ((1, 0, 0, 0), (1, 0, 0, 1)), 9: ((8, 0, 0, 0), (8, 0, 1, 0))}
DEEP = 2
LATE = 3


def move(block, link):
    if link == 1:
        return swap(block, "section")
    count = lax.axis_size("rows")
    if link == 0:
        return lax.ppermute(block, "rows", [(i, i ^ 1) for i in range(count)])
    return lax.ppermute(block, "rows", [(i, (i + 2) % count) for i in range(count)])


def spread(shards, section, run):
    held = {(base, 0, 0, 0): shards[name] for base, name in enumerate(NAMES)}
    sent, passed, awaited = {}, [], []

    def get(key):
        if key not in held:
            base = key[0]
            if base in JOINED:
                held[key] = jnp.concatenate([get(part) for part in JOINED[base]], axis=0)
            else:
                raw = base // 2
                held[key] = jnp.where(section == base % 2, get((raw, 0, 0, 0)), get((raw, 0, 0, 1)))
        return held[key]

    for link, *key in ORDER:
        if link == 3:
            now, later = run(*key[:3], get)
            passed = [now]
            if later is not None:
                awaited.append([LATE, later])
            continue
        block, ahead = get(tuple(key)), sent.setdefault(link, [])
        behind = list(passed)
        if len(ahead) >= DEEP:
            behind.append(ahead[-DEEP])
        for entry in awaited:
            entry[0] -= 1
            if entry[0] == 0:
                behind.append(entry[1])
        if behind:
            block, *_ = lax.optimization_barrier((block, *behind))
        base, steps, over_x, over_y = key
        target = (base, steps + (link == 2), over_x + (link == 0), over_y + (link == 1))
        held[target] = move(block, link)
        ahead.append(held[target])


def pieces(matrix, layer, resolved):
    result = []
    for steps in range(4):
        for over_x in range(2):
            if matrix == 1:
                key = (9, steps, 0, 0)
                near, away = (key, 2 * over_x), (key, 2 * over_x + 1)
            elif resolved:
                near = away = ((2 * matrix + layer, steps, over_x, 0), 0)
            else:
                near, away = ((matrix, steps, over_x, 0), 0), ((matrix, steps, over_x, 1), 0)
            result.append((steps, over_x, near, away))
    return result


def join_kernel(plan, layer, rows, place_ref, *refs):
    buffers, (out_ref, stage, sems, out_sems) = refs[:-4], refs[-4:]
    section, z, x = place_ref[0], place_ref[1], place_ref[2]

    def copy(index, source):
        buffer, block = source
        return pltpu.make_async_copy(
            buffers[buffer].at[block * rows : (block + 1) * rows], stage.at[index], sems.at[index]
        )

    def out(index):
        steps, over_x = plan[index][:2]
        slot = ((z + 4 - steps) % 4) * 2 + (x + over_x) % 2
        return pltpu.make_async_copy(stage.at[index], out_ref.at[slot], out_sems.at[index])

    @pl.when(section == layer)
    def _():
        for index, entry in enumerate(plan):
            copy(index, entry[2]).start()

    @pl.when(section != layer)
    def _():
        for index, entry in enumerate(plan):
            copy(index, entry[3]).start()

    for index, entry in enumerate(plan):
        copy(index, entry[2]).wait()
        out(index).start()
    for index in range(len(plan)):
        out(index).wait()


def joined(matrix, layer, get, shape, place):
    rows, columns = shape
    keys, plan = [], []
    resolved = any(link < 3 and base == 2 * matrix for link, base, *_ in ORDER if matrix > 1)
    for steps, over_x, *sources in pieces(matrix, layer, resolved):
        spots = []
        for key, block in sources:
            if key not in keys:
                keys.append(key)
            spots.append((keys.index(key), block))
        plan.append((steps, over_x, *spots))
    anywhere = pl.BlockSpec(memory_space=pl.ANY)
    whole = pl.pallas_call(
        functools.partial(join_kernel, plan, layer, rows),
        in_specs=[pl.BlockSpec(memory_space=pltpu.SMEM)] + [anywhere] * len(keys),
        out_specs=anywhere,
        out_shape=jax.ShapeDtypeStruct((8, rows, columns), LOW),
        scratch_shapes=[
            pltpu.VMEM((8, rows, columns), LOW),
            pltpu.SemaphoreType.DMA((8,)),
            pltpu.SemaphoreType.DMA((8,)),
        ],
        name="join",
        cost_estimate=pl.CostEstimate(flops=0, bytes_accessed=4 * 8 * rows * columns, transcendentals=0),
    )(place, *[get(key) for key in keys])
    return whole.reshape(8 * rows, columns)


def forward(shards, x, dy, start, smalls, pref_count):
    section, rows = lax.axis_index("section"), lax.axis_index("rows")
    weights, kept, outputs, slopes = [{}, {}], [None, None], [None, None], []

    def run(kind, matrix, layer, get):
        small, mine = smalls[layer], weights[layer]
        if kind == JOIN:
            name = NAMES[matrix]
            place = jnp.stack([section, rows // 2, rows % 2]).astype(jnp.int32)
            near = joined(matrix, layer, get, shards[name].shape, place)
            mine[name] = (near, swap(near, "tensor"))
            return mine[name]
        if kind == QKV:
            source = outputs[0][1] if layer else x
            qkv, edge = qkv_forward(source, small["gain"][0:1], small["shift"][0:1], mine["qkv"], small["qkv"])
            kept[layer] = (source, qkv, lax.ppermute(edge, "tensor", [(0, 1)]))
            return qkv, kept[layer][2]
        if kind == ATTEND:
            source, qkv, halo = kept[layer]
            c, probs = attend(pref_count, qkv, halo, small["prefix"], start)
            kept[layer] = (source, qkv, halo, probs, c)
            return c, None
        source, qkv, halo, probs, c = kept[layer]
        kept[layer] = (source, qkv, halo, probs)
        biases = (small["out"][0:1], small["out"][1:2])
        norm = (small["gain"][1:2], small["shift"][1:2])
        if layer:
            *outputs[1], dh, dc = mlp_both(outputs[0][0], source, c, dy, mine, biases, *norm, small["fc"])
            slopes.extend((dh, dc))
        else:
            acts, h, slope, low = mlp_forward(source, c, mine, biases, *norm, small["fc"])
            outputs[0] = (acts, low)
            slopes.extend((h, slope))
        return slopes[-1], None

    if lax.axis_size("rows") == 8:
        spread(shards, section, run)
    else:
        for name in NAMES:
            near = lax.all_gather(shards[name], ("section", "rows"), axis=0, tiled=True)
            near = near.reshape(2, -1, near.shape[1])
            far = swap(near, "tensor")
            for layer in range(2):
                weights[layer][name] = (near[layer], far[layer])
        for link, *stage in ORDER:
            if link == 3 and stage[0] != JOIN:
                run(*stage[:3], None)
    return weights, kept, outputs, slopes


def on_device(
    tokens,
    segment_ids,
    cotangent,
    ln_gain,
    ln_bias,
    w_qkv,
    query_key_value_bias,
    w_proj,
    w_fc,
    fc_bias,
    w_fc2,
    out_bias,
    prefix_embed,
    rep_w1,
    rep_b1,
    rep_w2,
    rep_b2,
):
    share, width = tokens.shape[1:]
    section, core = lax.axis_index("section"), lax.axis_index("tensor")
    rows_index, rows = lax.axis_index("rows"), lax.axis_size("rows")
    half = rep_w2.shape[-1]
    pref_count = prefix_embed.shape[0]

    shards = {
        "qkv": w_qkv[0].astype(LOW).reshape(w_qkv.shape[1], -1),
        "proj": w_proj[0].astype(LOW),
        "fc": w_fc[0].astype(LOW),
        "fc2": w_fc2[0].astype(LOW),
    }
    rep_hidden = jnp.tanh(jnp.dot(prefix_embed, rep_w1, precision=HIGHEST) + rep_b1)
    prefix = jnp.einsum("pm,mcd->pcd", rep_hidden, rep_w2[:, 0], precision=HIGHEST) + rep_b2[0]
    prefix = prefix.astype(LOW).astype(WIDE)
    prefix = jnp.pad(prefix, ((0, PREP - pref_count), (0, 0), (0, 0)))
    parts = [ln_gain[0], ln_bias[0], out_bias[0], query_key_value_bias[0], fc_bias[0], prefix]
    packed = jnp.concatenate([part.reshape(-1) for part in parts])
    near = jnp.stack([packed, swap(packed, "tensor")])
    away = swap(near, "section")
    smalls = []
    for layer in range(2):
        cut, place = [], 0
        chosen = jnp.where(section == layer, near, away)
        for part in parts:
            cut.append([chosen[h, place : place + part.size].reshape(part.shape) for h in range(2)])
            place += part.size
        smalls.append(
            {
                "gain": cut[0][0],
                "shift": cut[1][0],
                "out": cut[2][0],
                "qkv": jnp.concatenate([cut[3][h].reshape(1, -1) for h in range(2)], axis=1),
                "fc": jnp.concatenate([cut[4][h].reshape(1, -1) for h in range(2)], axis=1),
                "prefix": jnp.concatenate(
                    [cut[5][h].reshape(PREP, -1).astype(LOW) for h in range(2)], axis=1
                ),
            }
        )

    own = section
    segments = lax.dynamic_index_in_dim(segment_ids, own, 0, keepdims=False).reshape(-1)
    mine = lax.dynamic_slice_in_dim(segments, core * share, share)
    start = jnp.sum(segments[:, None] < mine[None, :], axis=0, dtype=jnp.int32)
    start = (start - core * share + BAND)[None]

    x = lax.dynamic_index_in_dim(tokens, own, 0, keepdims=False)
    dy = lax.dynamic_index_in_dim(cotangent, own, 0, keepdims=False)
    weights, (kept0, kept1), ((_, low0), (acts, low1)), (h, slope, dh, dc) = forward(
        shards, x, dy, start, smalls, pref_count
    )
    dy = lax.dynamic_index_in_dim(cotangent, own, 0, keepdims=False)
    got_acts = swap(jnp.where(section == 0, low1, low0), "section")
    where_at = section.astype(jnp.int32).reshape(1)
    nowhere = jnp.ones((1,), jnp.int32)

    def same(prefix_term):
        return prefix_term

    def reduced(prefix_term):
        pre0, pre1 = [pre.reshape(2, PREP, 2, half) for pre in (prefix_term, pre_last)]
        near = jnp.where(section == 0, pre0, pre1) + swap(jnp.where(section == 0, pre1, pre0), "section")
        total = (near[:, :, 0] + swap(near[:, :, 1], "tensor"))[:, :pref_count]
        return total, jnp.einsum("cpd,mcd->pm", total, rep_w2[:, 0], precision=HIGHEST)

    last, pre_last = attention_backward(kept1, dh, dc, weights[1], smalls[1], same)
    in_grads, down1 = qkv_back(*last, low1, nowhere, 1)
    dh, dc = mlp_back(down1, h, smalls[0]["gain"][1:2], slope, weights[0])
    got_acts, dc = lax.optimization_barrier((got_acts, dc))
    acts = take(where_at, got_acts, acts)
    first, (total, hidden_term) = attention_backward(kept0, dh, dc, weights[0], smalls[0], reduced)
    hidden_term = all_sum(hidden_term, ("section",))
    down1, hidden_term = lax.optimization_barrier((down1, hidden_term))
    got = []
    for part in range(2):
        in_grads, sent = qkv_back(*first, down1, where_at, 0, in_grads, part, 2)
        got.append(swap(sent, "section"))
    hidden_term, _ = lax.optimization_barrier((hidden_term, sent))
    for part in range(2):
        in_grads = take(where_at, got[part], in_grads, part * share // 2)

    hidden_term = all_sum(hidden_term, ("tensor",))
    sums = all_sum(jnp.concatenate([total.reshape(2 * pref_count, half), hidden_term], axis=0), ("rows",))
    total, grad_hidden = sums[: 2 * pref_count].reshape(2, pref_count, half), sums[2 * pref_count :]
    grad_b2 = jnp.sum(total, axis=1)
    mid_part = rep_w1.shape[1] // rows
    width_part = width // rows
    hidden_part = lax.dynamic_slice_in_dim(rep_hidden, rows_index * mid_part, mid_part, 1)
    grad_w2 = jnp.einsum("pm,cpd->mcd", hidden_part, total, precision=HIGHEST)
    grad_pre = grad_hidden * (1.0 - rep_hidden * rep_hidden)
    grad_b1 = jnp.sum(grad_pre, axis=0)
    embed_part = lax.dynamic_slice_in_dim(prefix_embed, rows_index * width_part, width_part, 1)
    grad_w1 = jnp.einsum("pd,pm->dm", embed_part, grad_pre, precision=HIGHEST)
    weight_part = lax.dynamic_slice_in_dim(rep_w1, rows_index * width_part, width_part, 0)
    grad_embed = jnp.einsum("pm,dm->pd", grad_pre, weight_part, precision=HIGHEST)
    return (acts[None], in_grads[None], grad_embed, grad_w1, grad_b1, grad_w2[:, None], grad_b2[None])


def solution(mesh):
    return jax.shard_map(
        on_device,
        mesh=mesh,
        in_specs=(
            P(None, ("rows", "tensor"), None),
            P(None, "rows", None),
            P(None, ("rows", "tensor"), None),
            P("section", None, None),
            P("section", None, None),
            P("section", "rows", None, "tensor"),
            P("section", None, "tensor"),
            P("section", ("tensor", "rows"), None),
            P("section", "rows", "tensor"),
            P("section", "tensor"),
            P("section", ("tensor", "rows"), None),
            P("section", None, None),
            P(),
            P(),
            P(),
            P(None, "section", None, "tensor"),
            P("section", None, "tensor"),
        ),
        out_specs=(
            P("section", None, ("rows", "tensor"), None),
            P("section", None, ("rows", "tensor"), None),
            P(None, "rows"),
            P("rows", None),
            P(),
            P("rows", "section", None, "tensor"),
            P("section", None, "tensor"),
        ),
        check_vma=False,
    )
```

```python
import functools

import jax
import jax.numpy as jnp
from jax import lax
from jax.experimental import pallas as pl
from jax.experimental.pallas import tpu as pltpu
from jax.sharding import PartitionSpec as P

HEAD = 64
EPSILON = 1e-05
NEGATIVE = -1000000000.0
HIGHEST = lax.Precision.HIGHEST
LOW = jnp.bfloat16
WIDE = jnp.float32
QB = 128
BAND = 256
KB = QB + BAND
PREP = 16


def swap(block, axis):
    return lax.ppermute(block, axis, [(0, 1), (1, 0)])


def all_sum(block, axes):
    for axis in axes:
        count = lax.axis_size(axis)
        if count & (count - 1):
            block = lax.psum(block, axis)
            continue
        bit = 1
        while bit < count:
            block = block + lax.ppermute(block, axis, [(i, i ^ bit) for i in range(count)])
            bit *= 2
    return block


def layer_norm(values, gain, shift):
    centre = values - jnp.mean(values, axis=-1, keepdims=True)
    spread = jnp.mean(centre * centre, axis=-1, keepdims=True)
    return centre * lax.rsqrt(spread + EPSILON) * gain + shift


def norm_back(values, gain, grad):
    centre = values - jnp.mean(values, axis=-1, keepdims=True)
    inverse = lax.rsqrt(jnp.mean(centre * centre, axis=-1, keepdims=True) + EPSILON)
    normal = centre * inverse
    scaled = grad * gain
    return inverse * (
        scaled
        - jnp.mean(scaled, axis=-1, keepdims=True)
        - normal * jnp.mean(scaled * normal, axis=-1, keepdims=True)
    )


def gelu_parts(values):
    root = 0.7978845608028654
    square = values * values
    inner = jnp.tanh(root * values * (1.0 + 0.044715 * square))
    half = 0.5 * (1.0 + inner)
    slope = half + 0.5 * values * (1.0 - inner * inner) * root * (1.0 + 3 * 0.044715 * square)
    return values * half, slope


def dot_nn(left, right):
    return jnp.dot(left, right, preferred_element_type=WIDE)


def dot_nt(left, right):
    return lax.dot_general(left, right, (((1,), (1,)), ((), ())), preferred_element_type=WIDE)


def stacked(pair):
    lane = lax.broadcasted_iota(jnp.int32, pair.shape, 1)
    zero = jnp.zeros_like(pair)
    return jnp.concatenate(
        [jnp.where(lane < HEAD, pair, zero), jnp.where(lane >= HEAD, pair, zero)], axis=0
    )


def unstacked(both):
    lane = lax.broadcasted_iota(jnp.int32, (QB, 2 * HEAD), 1)
    return jnp.where(lane < HEAD, both[:QB], both[QB:])


def dot_tn(left, right):
    return lax.dot_general(left, right, (((0,), (0,)), ((), ())), preferred_element_type=WIDE)


def lower():
    row = lax.broadcasted_iota(jnp.int32, (QB, 2 * QB), 0)
    lane = lax.broadcasted_iota(jnp.int32, (QB, 2 * QB), 1)
    return row <= jnp.where(lane < QB, lane, lane - QB)


def fold(band, near):
    return jnp.concatenate([jnp.where(near, band[BAND:], band[:QB]), band[QB:BAND]], axis=0)


def unfold(folded, near):
    zero = jnp.zeros((QB, 2 * QB), folded.dtype)
    edge = folded[:QB]
    return jnp.concatenate(
        [jnp.where(near, zero, edge), folded[QB:], jnp.where(near, edge, zero)], axis=0
    )


def fill_places(places):
    row = lax.broadcasted_iota(jnp.int32, (QB, 2 * QB), 0)
    places[:QB] = jnp.where(lower(), row + BAND, row)
    places[QB:] = row + QB


def fill_keys(scratch, prefix_ref, halo_ref, own_ref):
    scratch[:PREP] = prefix_ref[...]
    scratch[PREP : PREP + BAND] = halo_ref[...]
    scratch[PREP + BAND :] = own_ref[...]


def masked_scores(queries, keys, start_ref, block, pref_count, places, near):
    pre = dot_nt(keys[:PREP], queries)
    pre = jnp.where(
        lax.broadcasted_iota(jnp.int32, pre.shape, 0) < pref_count, pre, NEGATIVE
    )
    band = fold(dot_nt(keys[pl.ds(PREP + block * QB, KB)], queries), near)
    first = start_ref[:, block * QB : (block + 1) * QB] - block * QB
    first = jnp.concatenate([first, first], axis=1)
    return pre, jnp.where(places[...] >= first, band, NEGATIVE)


def attend_kernel(pref_count, q_ref, k_ref, v_ref, hk_ref, hv_ref, pk_ref, pv_ref, start_ref,
                  c_ref, probs_ref, keys, vals, places):
    fill_keys(keys, pk_ref, hk_ref, k_ref)
    fill_keys(vals, pv_ref, hv_ref, v_ref)
    fill_places(places)
    near = lower()
    for block in range(q_ref.shape[0] // QB):
        span = slice(block * QB, (block + 1) * QB)
        seen = pl.ds(PREP + block * QB, KB)
        queries = stacked(q_ref[span, :] * jnp.asarray(HEAD ** (-0.5), LOW))
        pre, band = masked_scores(queries, keys, start_ref, block, pref_count, places, near)
        top = jnp.maximum(jnp.max(pre, axis=0, keepdims=True), jnp.max(band, axis=0, keepdims=True))
        pre = jnp.exp(pre - top)
        band = jnp.exp(band - top)
        total = jnp.sum(pre, axis=0, keepdims=True) + jnp.sum(band, axis=0, keepdims=True)
        inverse = 1.0 / total
        probs = jnp.concatenate([pre * inverse, unfold(band * inverse, near)], axis=0).astype(LOW)
        probs_ref[0, block] = probs
        out = dot_tn(probs, jnp.concatenate([vals[:PREP], vals[seen]], axis=0))
        c_ref[span, :] = unstacked(out).astype(LOW)


def attend_back_kernel(q_ref, k_ref, v_ref, hk_ref, hv_ref, pk_ref, pv_ref, probs_ref, dc_ref,
                       dq_ref, dk_ref, dv_ref, edge_ref, prefix_ref, keys, vals, dkeys, dvals):
    fill_keys(keys, pk_ref, hk_ref, k_ref)
    fill_keys(vals, pv_ref, hv_ref, v_ref)
    dkeys[...] = jnp.zeros_like(dkeys)
    dvals[...] = jnp.zeros_like(dvals)
    scaling = HEAD ** (-0.5)
    for block in range(q_ref.shape[0] // QB):
        span = slice(block * QB, (block + 1) * QB)
        seen = pl.ds(PREP + block * QB, KB)
        queries = stacked(q_ref[span, :] * jnp.asarray(scaling, LOW))
        grads = stacked(dc_ref[span, :])
        low = probs_ref[0, block]
        probs = low.astype(WIDE)
        dprobs = dot_nt(jnp.concatenate([vals[:PREP], vals[seen]], axis=0), grads)
        inside = jnp.sum(probs * dprobs, axis=0, keepdims=True)
        slope = (probs * (dprobs - inside)).astype(LOW)
        terms = dot_nn(low, grads)
        dvals[:PREP] += terms[:PREP]
        dvals[seen] += terms[PREP:]
        terms = dot_nn(slope, queries)
        dkeys[:PREP] += terms[:PREP]
        dkeys[seen] += terms[PREP:]
        out = dot_tn(slope, jnp.concatenate([keys[:PREP], keys[seen]], axis=0))
        dq_ref[span, :] = (unstacked(out) * scaling).astype(LOW)
    dk_ref[...] = dkeys[PREP + BAND :].astype(LOW)
    dv_ref[...] = dvals[PREP + BAND :].astype(LOW)
    edge_ref[:BAND] = dkeys[PREP : PREP + BAND].astype(LOW)
    edge_ref[BAND:] = dvals[PREP : PREP + BAND].astype(LOW)
    prefix_ref[:PREP] = dkeys[:PREP]
    prefix_ref[PREP:] = dvals[:PREP]


def column(rows, place=lambda half, pair: 0, per=0):
    if per == 0:
        return pl.BlockSpec((rows, 2 * HEAD), lambda i: (0, i))
    return pl.BlockSpec((rows, 2 * HEAD), lambda i: (0, place(i // per) + i % per))


def attention_specs(tokens, per):
    return [
        column(tokens, lambda half: 3 * per * half, per),
        column(tokens, lambda half: 3 * per * half + per, per),
        column(tokens, lambda half: 3 * per * half + 2 * per, per),
        column(BAND, lambda half: 2 * per * (1 - half), per),
        column(BAND, lambda half: 2 * per * (1 - half) + per, per),
        column(PREP, lambda half: 2 * per * half, per),
        column(PREP, lambda half: 2 * per * half + per, per),
    ]


def probs_spec(blocks):
    return pl.BlockSpec((1, blocks, PREP + KB, 2 * QB), lambda i: (i, 0, 0, 0))


def attend(pref_count, qkv, halo, prefix, start):
    tokens, width = qkv.shape[0], qkv.shape[1] // 3
    pairs, blocks = width // (2 * HEAD), tokens // QB
    return pl.pallas_call(
        functools.partial(attend_kernel, pref_count),
        grid=(pairs,),
        in_specs=attention_specs(tokens, pairs // 2) + [pl.BlockSpec((1, tokens), lambda i: (0, 0))],
        out_specs=[column(tokens), probs_spec(blocks)],
        out_shape=[
            jax.ShapeDtypeStruct((tokens, width), LOW),
            jax.ShapeDtypeStruct((pairs, blocks, PREP + KB, 2 * QB), LOW),
        ],
        scratch_shapes=[
            pltpu.VMEM((PREP + BAND + tokens, 2 * HEAD), LOW),
            pltpu.VMEM((PREP + BAND + tokens, 2 * HEAD), LOW),
            pltpu.VMEM((2 * QB, 2 * QB), jnp.int32),
        ],
        name="attend",
        cost_estimate=pl.CostEstimate(flops=12 * 10**9, bytes_accessed=2 * qkv.size, transcendentals=0),
    )(qkv, qkv, qkv, halo, halo, prefix, prefix, start)


def attend_back(qkv, halo, prefix, probs, grad):
    tokens, width = qkv.shape[0], qkv.shape[1] // 3
    pairs, blocks = width // (2 * HEAD), tokens // QB
    keys = PREP + BAND + tokens
    sizes = [(tokens, LOW)] * 3 + [(2 * BAND, LOW), (2 * PREP, WIDE)]
    return pl.pallas_call(
        attend_back_kernel,
        grid=(pairs,),
        in_specs=attention_specs(tokens, pairs // 2) + [probs_spec(blocks), column(tokens)],
        out_specs=[column(rows) for rows, _ in sizes],
        out_shape=[jax.ShapeDtypeStruct((rows, width), kind) for rows, kind in sizes],
        scratch_shapes=[
            pltpu.VMEM((keys, 2 * HEAD), LOW),
            pltpu.VMEM((keys, 2 * HEAD), LOW),
            pltpu.VMEM((keys, 2 * HEAD), WIDE),
            pltpu.VMEM((keys, 2 * HEAD), WIDE),
        ],
        name="attend_back",
        cost_estimate=pl.CostEstimate(flops=16 * 10**9, bytes_accessed=4 * qkv.size, transcendentals=0),
    )(qkv, qkv, qkv, halo, halo, prefix, prefix, probs, grad)


CHUNK = 512
ROWS = 512


def by_rows(total, body):
    step = min(ROWS, total)

    @pl.loop(0, total // step)
    def _(index):
        body(pl.ds(pl.multiple_of(index * step, step), step))


def of_half(step, count, own_ref, far_ref, body):
    @pl.when(step < count)
    def _():
        body(own_ref)

    @pl.when(step >= count)
    def _():
        body(far_ref)


def halves(shape, count, across):
    def spec(place):
        return pl.BlockSpec(shape, lambda j: (0, place(j)) if across else (place(j), 0))

    return [spec(lambda j: jnp.minimum(j, count - 1)), spec(lambda j: jnp.maximum(j - count, 0))]


def whole(shape):
    return pl.BlockSpec(shape, lambda j: (0,) * len(shape))


def slab(index, tokens, width, part=0):
    return pl.BlockSpec((None, tokens, width), lambda j: (index, part, 0))


def call(kernel, grid, in_specs, out_specs, out_shape, scratch, name, flops, operands, buffer=None):
    size, count = sum(o.size * o.dtype.itemsize for o in operands), len(operands)
    body, aliases = kernel, {}
    if buffer is not None:
        in_specs, operands = in_specs + [pl.BlockSpec(memory_space=pl.ANY)], (*operands, buffer)
        aliases = {count: 0}

        def body(*refs):
            kernel(*refs[:count], *refs[count + 1 :])

    return pl.pallas_call(
        body,
        grid=(grid,),
        in_specs=in_specs,
        out_specs=out_specs,
        out_shape=out_shape,
        input_output_aliases=aliases,
        scratch_shapes=scratch,
        name=name,
        compiler_params=pltpu.CompilerParams(vmem_limit_bytes=56 * 2**20),
        cost_estimate=pl.CostEstimate(flops=flops, bytes_accessed=size, transcendentals=0),
    )(*operands)


def qkv_kernel(x_ref, gain_ref, shift_ref, own_ref, far_ref, bias_ref, out_ref, halo_ref, normed):
    step = pl.program_id(0)

    @pl.when(step == 0)
    def _():
        def body(span):
            normed[span] = layer_norm(
                x_ref[span].astype(WIDE), gain_ref[...], shift_ref[...]
            ).astype(LOW)

        by_rows(x_ref.shape[0], body)

    def body(weight_ref):
        third = weight_ref.shape[1] // 3
        for part in range(3):
            span = slice(part * third, (part + 1) * third)
            out = (dot_nn(normed[...], weight_ref[:, span]) + bias_ref[:, span]).astype(LOW)
            out_ref[:, span] = out
            if part:
                halo_ref[:, (part - 1) * third : part * third] = out[out.shape[0] - BAND :]

    of_half(step, 1, own_ref, far_ref, body)


def qkv_forward(x, gain, shift, weights, bias):
    tokens, width = x.shape
    half = weights[0].shape[1] // 3
    return call(
        qkv_kernel,
        2,
        [whole(x.shape), whole((1, width)), whole((1, width))]
        + halves((width, 3 * half), 1, True)
        + [pl.BlockSpec((1, 3 * half), lambda j: (0, j))],
        [
            pl.BlockSpec((tokens, 3 * half), lambda j: (0, j)),
            pl.BlockSpec((BAND, 2 * half), lambda j: (0, j)),
        ],
        [
            jax.ShapeDtypeStruct((tokens, 6 * half), LOW),
            jax.ShapeDtypeStruct((BAND, 4 * half), LOW),
        ],
        [pltpu.VMEM(x.shape, LOW)],
        "qkv",
        12 * tokens * width * half,
        (x, gain, shift, *weights, bias),
    )


def mlp_kernel(count, x_ref, c_ref, po_ref, pf_ref, b0_ref, gain_ref, shift_ref, fo_ref, ff_ref, bias_ref, wo_ref,
               wf_ref, b1_ref, y_ref, h_ref, slope_ref, low_ref, normed):
    step = pl.program_id(0)
    half = po_ref.shape[0]

    @pl.when(step == 0)
    def _():
        def body(span):
            h = x_ref[span].astype(WIDE) + (
                dot_nn(c_ref[span, :half], po_ref[...])
                + dot_nn(c_ref[span, half:], pf_ref[...])
                + b0_ref[...]
            )
            h_ref[span] = h
            normed[span] = layer_norm(h, gain_ref[...], shift_ref[...]).astype(LOW)
            y_ref[span] = h + b1_ref[...]

        by_rows(x_ref.shape[0], body)

    def half_body(up_ref, down_ref):
        def body(span):
            active, slope = gelu_parts(dot_nn(normed[span], up_ref[...]) + bias_ref[...])
            slope_ref[span] = slope.astype(LOW)
            y_ref[span] += dot_nn(active.astype(LOW), down_ref[...])

        by_rows(x_ref.shape[0], body)

    of_half(step, count, (fo_ref, wo_ref), (ff_ref, wf_ref), lambda refs: half_body(*refs))

    @pl.when(step == 2 * count - 1)
    def _():
        low_ref[...] = y_ref[...].astype(LOW)


def mlp_forward(x, c, weights, biases, gain, shift, fc_bias):
    tokens, width = x.shape
    half, count = width // 2, weights["fc"][0].shape[1] // CHUNK
    row = whole((1, width))
    return call(
        functools.partial(mlp_kernel, count),
        2 * count,
        [whole(x.shape), whole(c.shape), whole((half, width)), whole((half, width)), row, row, row]
        + halves((width, CHUNK), count, True)
        + [pl.BlockSpec((1, CHUNK), lambda j: (0, j))]
        + halves((CHUNK, width), count, False)
        + [row],
        [
            slab(0, tokens, width),
            whole(x.shape),
            pl.BlockSpec((tokens, CHUNK), lambda j: (0, j)),
            whole(x.shape),
        ],
        [
            jax.ShapeDtypeStruct((2, tokens, width), WIDE),
            jax.ShapeDtypeStruct(x.shape, WIDE),
            jax.ShapeDtypeStruct((tokens, 2 * count * CHUNK), LOW),
            jax.ShapeDtypeStruct(x.shape, LOW),
        ],
        [pltpu.VMEM(x.shape, LOW)],
        "mlp",
        2 * tokens * width * (width + 4 * count * CHUNK),
        (x, c, *weights["proj"], biases[0], gain, shift, *weights["fc"], fc_bias, *weights["fc2"], biases[1]),
    )


def mlp_back_kernel(count, dy_ref, h_ref, gain_ref, slope_ref, wo_ref, wf_ref, fo_ref, ff_ref, po_ref, pf_ref,
                    dh_ref, dc_ref, total):
    step = pl.program_id(0)
    half = po_ref.shape[0]

    def half_body(first, up_ref, down_ref):
        def body(span):
            du = (dot_nt(dy_ref[span], down_ref[...]) * slope_ref[span].astype(WIDE)).astype(LOW)
            dm = dot_nt(du, up_ref[...])
            total[span] = dm if first else total[span] + dm

        by_rows(dy_ref.shape[0], body)

    @pl.when(step == 0)
    def _():
        half_body(True, fo_ref, wo_ref)

    @pl.when((step > 0) & (step < count))
    def _():
        half_body(False, fo_ref, wo_ref)

    @pl.when(step >= count)
    def _():
        half_body(False, ff_ref, wf_ref)

    @pl.when(step == 2 * count - 1)
    def _():
        def body(span):
            dh = dy_ref[span].astype(WIDE) + norm_back(h_ref[span], gain_ref[...], total[span])
            dh_ref[span] = dh
            low = dh.astype(LOW)
            dc_ref[span, :half] = dot_nt(low, po_ref[...]).astype(LOW)
            dc_ref[span, half:] = dot_nt(low, pf_ref[...]).astype(LOW)

        by_rows(dy_ref.shape[0], body)


def mlp_back(dy, h, gain, slope, weights):
    tokens, width = dy.shape
    half, count = width // 2, weights["fc"][0].shape[1] // CHUNK
    return call(
        functools.partial(mlp_back_kernel, count),
        2 * count,
        [whole(dy.shape), whole(dy.shape), whole((1, width)), pl.BlockSpec((tokens, CHUNK), lambda j: (0, j))]
        + halves((CHUNK, width), count, False)
        + halves((width, CHUNK), count, True)
        + [whole((half, width)), whole((half, width))],
        [whole(dy.shape), whole(dy.shape)],
        [jax.ShapeDtypeStruct(dy.shape, WIDE), jax.ShapeDtypeStruct(dy.shape, LOW)],
        [pltpu.VMEM(dy.shape, WIDE)],
        "mlp_back",
        2 * tokens * width * (width + 4 * count * CHUNK),
        (dy, h, gain, slope, *weights["fc2"], *weights["fc"], *weights["proj"]),
    )


def mlp_both_kernel(count, x_ref, c_ref, dy_ref, po_ref, pf_ref, b0_ref, gain_ref, shift_ref, fo_ref, ff_ref, bias_ref,
                    wo_ref, wf_ref, b1_ref, y_ref, low_ref, dh_ref, dc_ref, h_ref, normed, total):
    step = pl.program_id(0)
    half = po_ref.shape[0]

    @pl.when(step == 0)
    def _():
        def body(span):
            h = x_ref[span].astype(WIDE) + (
                dot_nn(c_ref[span, :half], po_ref[...])
                + dot_nn(c_ref[span, half:], pf_ref[...])
                + b0_ref[...]
            )
            h_ref[span] = h
            normed[span] = layer_norm(h, gain_ref[...], shift_ref[...]).astype(LOW)
            y_ref[span] = h + b1_ref[...]
            total[span] = jnp.zeros_like(h)

        by_rows(x_ref.shape[0], body)

    def half_body(up_ref, down_ref):
        def body(span):
            active, slope = gelu_parts(dot_nn(normed[span], up_ref[...]) + bias_ref[...])
            du = (dot_nt(dy_ref[span], down_ref[...]) * slope).astype(LOW)
            y_ref[span] += dot_nn(active.astype(LOW), down_ref[...])
            total[span] += dot_nt(du, up_ref[...])

        by_rows(x_ref.shape[0], body)

    of_half(step, count, (fo_ref, wo_ref), (ff_ref, wf_ref), lambda refs: half_body(*refs))

    @pl.when(step == 2 * count - 1)
    def _():
        def body(span):
            low_ref[span] = y_ref[span].astype(LOW)
            dh = dy_ref[span].astype(WIDE) + norm_back(h_ref[span], gain_ref[...], total[span])
            dh_ref[span] = dh
            low = dh.astype(LOW)
            dc_ref[span, :half] = dot_nt(low, po_ref[...]).astype(LOW)
            dc_ref[span, half:] = dot_nt(low, pf_ref[...]).astype(LOW)

        by_rows(x_ref.shape[0], body)


def mlp_both(acts, x, c, dy, weights, biases, gain, shift, fc_bias):
    tokens, width = x.shape
    half, count = width // 2, weights["fc"][0].shape[1] // CHUNK
    row, full = whole((1, width)), whole(x.shape)
    return call(
        functools.partial(mlp_both_kernel, count),
        2 * count,
        [full, full, full, whole((half, width)), whole((half, width)), row, row, row]
        + halves((width, CHUNK), count, True)
        + [pl.BlockSpec((1, CHUNK), lambda j: (0, j))]
        + halves((CHUNK, width), count, False)
        + [row],
        [slab(1, tokens, width), full, full, full],
        [jax.ShapeDtypeStruct(acts.shape, WIDE)]
        + [jax.ShapeDtypeStruct(x.shape, kind) for kind in (LOW, WIDE, LOW)],
        [pltpu.VMEM(x.shape, WIDE), pltpu.VMEM(x.shape, LOW), pltpu.VMEM(x.shape, WIDE)],
        "mlp_both",
        4 * tokens * width * (width + 4 * count * CHUNK),
        (x, c, dy, *weights["proj"], biases[0], gain, shift, *weights["fc"], fc_bias, *weights["fc2"], biases[1]),
        acts,
    )


def qkv_back_kernel(reach, dq_ref, dk_ref, dv_ref, hk_ref, hv_ref, own_ref, far_ref, x_ref, dh_ref, gain_ref, other_ref,
                    section_ref, dx_ref, low_ref, total):
    step = pl.program_id(0)

    def joined_grads(grad_ref, halo_ref):
        grad = grad_ref[...]
        if not reach:
            return grad
        early = grad.shape[0] - reach
        late = (grad[early:].astype(WIDE) + halo_ref[...].astype(WIDE)).astype(LOW)
        return jnp.concatenate([grad[:early], late], axis=0) if early else late

    def half_body(first, weight_ref):
        grads = (dq_ref[...], joined_grads(dk_ref, hk_ref), joined_grads(dv_ref, hv_ref))
        term = dot_nt(jnp.concatenate(grads, axis=1), weight_ref[...])
        total[...] = term if first else total[...] + term

    @pl.when(step == 0)
    def _():
        half_body(True, own_ref)

    @pl.when(step == 1)
    def _():
        half_body(False, far_ref)

        def body(span):
            dx = dh_ref[span] + norm_back(x_ref[span].astype(WIDE), gain_ref[...], total[span])
            dx_ref[span] = dx
            low = dx.astype(LOW)
            low_ref[span] = jnp.where(section_ref[0] == 0, other_ref[span], low)

        by_rows(x_ref.shape[0], body)


def qkv_back(grads, halo, weights, x, dh, gain, other, section, layer, buffer=None, part=0, parts=1):
    width = x.shape[1]
    tokens, half = x.shape[0] // parts, width // 2
    reach = BAND if part == parts - 1 else 0
    piece = pl.BlockSpec((tokens, half), lambda j: (part, j))
    edges = [pl.BlockSpec((BAND, half), lambda j, i=i: (i, 1 - j)) for i in range(2)]
    mine, shape = pl.BlockSpec((tokens, width), lambda j: (part, 0)), (tokens, width)
    return call(
        functools.partial(qkv_back_kernel, reach),
        2,
        [piece, piece, piece, *edges]
        + halves((width, 3 * half), 1, True)
        + [mine, mine, whole((1, width)), mine, pl.BlockSpec(memory_space=pltpu.SMEM)],
        [slab(layer, tokens, width, part), whole(shape)],
        [jax.ShapeDtypeStruct((2, *x.shape), WIDE), jax.ShapeDtypeStruct(shape, LOW)],
        [pltpu.VMEM(shape, WIDE)],
        "qkv_back",
        12 * tokens * width * half,
        (*grads, halo, halo, *weights, x, dh, gain, other, section),
        buffer,
    )


def take_kernel(section_ref, got_ref, held_ref, out_ref):
    out_ref[0] = got_ref[...].astype(WIDE)


def take(section, got, buffer, start=0):
    rows, width = got.shape
    step = min(256, rows)
    base = start // step
    return pl.pallas_call(
        take_kernel,
        grid_spec=pltpu.PrefetchScalarGridSpec(
            num_scalar_prefetch=1,
            grid=(rows // step,),
            in_specs=[
                pl.BlockSpec((step, width), lambda i, s: (i, 0)),
                pl.BlockSpec(memory_space=pl.ANY),
            ],
            out_specs=pl.BlockSpec((1, step, width), lambda i, s: (1 - s[0], base + i, 0)),
        ),
        out_shape=jax.ShapeDtypeStruct(buffer.shape, WIDE),
        input_output_aliases={2: 0},
        name="take",
        cost_estimate=pl.CostEstimate(flops=0, bytes_accessed=6 * got.size, transcendentals=0),
    )(section, got, buffer)


NAMES = ("qkv", "proj", "fc", "fc2")
JOIN, QKV, ATTEND, MLP = range(4)
ORDER = (
    (0, 0, 0, 0, 0), (2, 0, 0, 0, 0), (1, 0, 0, 0, 0), (0, 2, 0, 0, 0), (1, 1, 0, 0, 0),
    (2, 2, 0, 0, 0), (2, 0, 1, 0, 0), (1, 0, 1, 0, 0), (1, 0, 0, 1, 0), (0, 8, 0, 0, 0),
    (0, 0, 1, 0, 0), (1, 2, 0, 1, 0), (2, 2, 1, 0, 0), (2, 0, 2, 0, 0), (0, 0, 2, 0, 0),
    (1, 0, 2, 0, 0), (0, 2, 1, 0, 0), (2, 9, 0, 0, 0), (1, 0, 2, 1, 0), (0, 2, 2, 0, 0),
    (1, 3, 0, 0, 0), (0, 0, 3, 0, 0), (1, 2, 0, 0, 0), (2, 9, 1, 0, 0), (2, 2, 2, 0, 0),
    (1, 2, 2, 1, 0), (0, 7, 0, 0, 0), (2, 9, 2, 0, 0), (1, 0, 3, 1, 0), (0, 2, 3, 0, 0),
    (2, 6, 0, 0, 0), (1, 2, 3, 0, 0), (0, 6, 0, 0, 0), (1, 2, 2, 0, 0), (2, 7, 0, 0, 0),
    (0, 6, 1, 0, 0), (2, 6, 1, 0, 0), (1, 0, 1, 1, 0), (0, 7, 1, 0, 0), (1, 0, 3, 0, 0),
    (2, 7, 1, 0, 0), (1, 2, 1, 0, 0), (0, 6, 2, 0, 0), (2, 6, 2, 0, 0), (1, 2, 3, 1, 0),
    (0, 7, 2, 0, 0), (2, 7, 2, 0, 0), (1, 2, 1, 1, 0), (0, 6, 3, 0, 0), (0, 7, 3, 0, 0),
    (3, 0, 0, 0, 0), (3, 0, 1, 0, 0), (3, 0, 2, 0, 0), (3, 0, 3, 0, 0), (3, 0, 0, 1, 0),
    (3, 0, 1, 1, 0), (3, 0, 2, 1, 0), (3, 0, 3, 1, 0), (3, 1, 0, 0, 0), (3, 2, 0, 0, 0),
    (3, 3, 0, 0, 0), (3, 1, 0, 1, 0), (3, 2, 0, 1, 0), (3, 3, 0, 1, 0),
)
JOINED = {8: ((1, 0, 0, 0), (1, 0, 0, 1)), 9: ((8, 0, 0, 0), (8, 0, 1, 0))}
DEEP = 2
LATE = 3


def move(block, link):
    if link == 1:
        return swap(block, "section")
    count = lax.axis_size("rows")
    if link == 0:
        return lax.ppermute(block, "rows", [(i, i ^ 1) for i in range(count)])
    return lax.ppermute(block, "rows", [(i, (i + 2) % count) for i in range(count)])


def spread(shards, section, run):
    held = {(base, 0, 0, 0): shards[name] for base, name in enumerate(NAMES)}
    sent, passed, awaited = {}, [], []

    def get(key):
        if key not in held:
            base = key[0]
            if base in JOINED:
                held[key] = jnp.concatenate([get(part) for part in JOINED[base]], axis=0)
            else:
                raw = base // 2
                held[key] = jnp.where(section == base % 2, get((raw, 0, 0, 0)), get((raw, 0, 0, 1)))
        return held[key]

    for link, *key in ORDER:
        if link == 3:
            now, later = run(*key[:3], get)
            passed = [now]
            if later is not None:
                awaited.append([LATE, later])
            continue
        block, ahead = get(tuple(key)), sent.setdefault(link, [])
        behind = list(passed)
        if len(ahead) >= DEEP:
            behind.append(ahead[-DEEP])
        for entry in awaited:
            entry[0] -= 1
            if entry[0] == 0:
                behind.append(entry[1])
        if behind:
            block, *_ = lax.optimization_barrier((block, *behind))
        base, steps, over_x, over_y = key
        target = (base, steps + (link == 2), over_x + (link == 0), over_y + (link == 1))
        held[target] = move(block, link)
        ahead.append(held[target])


def pieces(matrix, layer, resolved):
    result = []
    for steps in range(4):
        for over_x in range(2):
            if matrix == 1:
                key = (9, steps, 0, 0)
                near, away = (key, 2 * over_x), (key, 2 * over_x + 1)
            elif resolved:
                near = away = ((2 * matrix + layer, steps, over_x, 0), 0)
            else:
                near, away = ((matrix, steps, over_x, 0), 0), ((matrix, steps, over_x, 1), 0)
            result.append((steps, over_x, near, away))
    return result


def join_kernel(plan, layer, rows, place_ref, *refs):
    buffers, (out_ref, stage, sems, out_sems) = refs[:-4], refs[-4:]
    section, z, x = place_ref[0], place_ref[1], place_ref[2]

    def copy(index, source):
        buffer, block = source
        return pltpu.make_async_copy(
            buffers[buffer].at[block * rows : (block + 1) * rows], stage.at[index], sems.at[index]
        )

    def out(index):
        steps, over_x = plan[index][:2]
        slot = ((z + 4 - steps) % 4) * 2 + (x + over_x) % 2
        return pltpu.make_async_copy(stage.at[index], out_ref.at[slot], out_sems.at[index])

    @pl.when(section == layer)
    def _():
        for index, entry in enumerate(plan):
            copy(index, entry[2]).start()

    @pl.when(section != layer)
    def _():
        for index, entry in enumerate(plan):
            copy(index, entry[3]).start()

    for index, entry in enumerate(plan):
        copy(index, entry[2]).wait()
        out(index).start()
    for index in range(len(plan)):
        out(index).wait()


def joined(matrix, layer, get, shape, place):
    rows, columns = shape
    keys, plan = [], []
    resolved = any(link < 3 and base == 2 * matrix for link, base, *_ in ORDER if matrix > 1)
    for steps, over_x, *sources in pieces(matrix, layer, resolved):
        spots = []
        for key, block in sources:
            if key not in keys:
                keys.append(key)
            spots.append((keys.index(key), block))
        plan.append((steps, over_x, *spots))
    anywhere = pl.BlockSpec(memory_space=pl.ANY)
    whole = pl.pallas_call(
        functools.partial(join_kernel, plan, layer, rows),
        in_specs=[pl.BlockSpec(memory_space=pltpu.SMEM)] + [anywhere] * len(keys),
        out_specs=anywhere,
        out_shape=jax.ShapeDtypeStruct((8, rows, columns), LOW),
        scratch_shapes=[
            pltpu.VMEM((8, rows, columns), LOW),
            pltpu.SemaphoreType.DMA((8,)),
            pltpu.SemaphoreType.DMA((8,)),
        ],
        name="join",
        cost_estimate=pl.CostEstimate(flops=0, bytes_accessed=4 * 8 * rows * columns, transcendentals=0),
    )(place, *[get(key) for key in keys])
    return whole.reshape(8 * rows, columns)


def forward(shards, x, dy, start, smalls, pref_count):
    section, rows = lax.axis_index("section"), lax.axis_index("rows")
    weights, kept, outputs, slopes = [{}, {}], [None, None], [None, None], []

    def run(kind, matrix, layer, get):
        small, mine = smalls[layer], weights[layer]
        if kind == JOIN:
            name = NAMES[matrix]
            place = jnp.stack([section, rows // 2, rows % 2]).astype(jnp.int32)
            near = joined(matrix, layer, get, shards[name].shape, place)
            mine[name] = (near, swap(near, "tensor"))
            return mine[name]
        if kind == QKV:
            source = outputs[0][1] if layer else x
            qkv, edge = qkv_forward(source, small["gain"][0:1], small["shift"][0:1], mine["qkv"], small["qkv"])
            kept[layer] = (source, qkv, lax.ppermute(edge, "tensor", [(0, 1)]))
            return qkv, kept[layer][2]
        if kind == ATTEND:
            source, qkv, halo = kept[layer]
            c, probs = attend(pref_count, qkv, halo, small["prefix"], start)
            kept[layer] = (source, qkv, halo, probs, c)
            return c, None
        source, qkv, halo, probs, c = kept[layer]
        kept[layer] = (source, qkv, halo, probs)
        biases = (small["out"][0:1], small["out"][1:2])
        norm = (small["gain"][1:2], small["shift"][1:2])
        if layer:
            *outputs[1], dh, dc = mlp_both(outputs[0][0], source, c, dy, mine, biases, *norm, small["fc"])
            slopes.extend((dh, dc))
        else:
            acts, h, slope, low = mlp_forward(source, c, mine, biases, *norm, small["fc"])
            outputs[0] = (acts, low)
            slopes.extend((h, slope))
        return slopes[-1], None

    if lax.axis_size("rows") == 8:
        spread(shards, section, run)
    else:
        for name in NAMES:
            near = lax.all_gather(shards[name], ("section", "rows"), axis=0, tiled=True)
            near = near.reshape(2, -1, near.shape[1])
            far = swap(near, "tensor")
            for layer in range(2):
                weights[layer][name] = (near[layer], far[layer])
        for link, *stage in ORDER:
            if link == 3 and stage[0] != JOIN:
                run(*stage[:3], None)
    return weights, kept, outputs, slopes


def on_device(
    tokens,
    segment_ids,
    cotangent,
    ln_gain,
    ln_bias,
    w_qkv,
    query_key_value_bias,
    w_proj,
    w_fc,
    fc_bias,
    w_fc2,
    out_bias,
    prefix_embed,
    rep_w1,
    rep_b1,
    rep_w2,
    rep_b2,
):
    share, width = tokens.shape[1:]
    section, core = lax.axis_index("section"), lax.axis_index("tensor")
    rows_index, rows = lax.axis_index("rows"), lax.axis_size("rows")
    half = rep_w2.shape[-1]
    pref_count = prefix_embed.shape[0]

    shards = {
        "qkv": w_qkv[0].astype(LOW).reshape(w_qkv.shape[1], -1),
        "proj": w_proj[0].astype(LOW),
        "fc": w_fc[0].astype(LOW),
        "fc2": w_fc2[0].astype(LOW),
    }
    rep_hidden = jnp.tanh(jnp.dot(prefix_embed, rep_w1, precision=HIGHEST) + rep_b1)
    prefix = jnp.einsum("pm,mcd->pcd", rep_hidden, rep_w2[:, 0], precision=HIGHEST) + rep_b2[0]
    prefix = prefix.astype(LOW).astype(WIDE)
    prefix = jnp.pad(prefix, ((0, PREP - pref_count), (0, 0), (0, 0)))
    parts = [ln_gain[0], ln_bias[0], out_bias[0], query_key_value_bias[0], fc_bias[0], prefix]
    packed = jnp.concatenate([part.reshape(-1) for part in parts])
    near = jnp.stack([packed, swap(packed, "tensor")])
    away = swap(near, "section")
    smalls = []
    for layer in range(2):
        cut, place = [], 0
        chosen = jnp.where(section == layer, near, away)
        for part in parts:
            cut.append([chosen[h, place : place + part.size].reshape(part.shape) for h in range(2)])
            place += part.size
        smalls.append(
            {
                "gain": cut[0][0],
                "shift": cut[1][0],
                "out": cut[2][0],
                "qkv": jnp.concatenate([cut[3][h].reshape(1, -1) for h in range(2)], axis=1),
                "fc": jnp.concatenate([cut[4][h].reshape(1, -1) for h in range(2)], axis=1),
                "prefix": jnp.concatenate(
                    [cut[5][h].reshape(PREP, -1).astype(LOW) for h in range(2)], axis=1
                ),
            }
        )

    own = section
    segments = lax.dynamic_index_in_dim(segment_ids, own, 0, keepdims=False).reshape(-1)
    mine = lax.dynamic_slice_in_dim(segments, core * share, share)
    start = jnp.sum(segments[:, None] < mine[None, :], axis=0, dtype=jnp.int32)
    start = (start - core * share + BAND)[None]

    x = lax.dynamic_index_in_dim(tokens, own, 0, keepdims=False)
    dy = lax.dynamic_index_in_dim(cotangent, own, 0, keepdims=False)
    weights, (kept0, kept1), ((_, low0), (acts, low1)), (h, slope, dh, dc) = forward(
        shards, x, dy, start, smalls, pref_count
    )
    dy = lax.dynamic_index_in_dim(cotangent, own, 0, keepdims=False)
    got_acts = swap(jnp.where(section == 0, low1, low0), "section")
    where_at = section.astype(jnp.int32).reshape(1)
    nowhere = jnp.ones((1,), jnp.int32)

    x1, qkv, halo, probs = kept1
    *grads, edge, pre1 = attend_back(qkv, halo, smalls[1]["prefix"], probs, dc)
    edge = lax.ppermute(edge, "tensor", [(1, 0)])
    in_grads, down1 = qkv_back(
        grads, edge, weights[1]["qkv"], x1, dh, smalls[1]["gain"][0:1], low1, nowhere, 1
    )
    dh, dc = mlp_back(down1, h, smalls[0]["gain"][1:2], slope, weights[0])
    got_acts, dc = lax.optimization_barrier((got_acts, dc))
    acts = take(where_at, got_acts, acts)
    x0, qkv, halo, probs = kept0
    *grads, edge, pre0 = attend_back(qkv, halo, smalls[0]["prefix"], probs, dc)
    edge = lax.ppermute(edge, "tensor", [(1, 0)])

    pre0, pre1 = [pre.reshape(2, PREP, 2, half) for pre in (pre0, pre1)]
    near = jnp.where(section == 0, pre0, pre1) + swap(jnp.where(section == 0, pre1, pre0), "section")
    tail = (weights[0]["qkv"], x0)
    gain = smalls[0]["gain"][0:1]
    in_grads, sent = qkv_back(grads, grads[0], *tail, dh, gain, down1, where_at, 0, in_grads, 0, 2)
    got = [swap(sent, "section")]
    near, _ = lax.optimization_barrier((near, sent))
    total = (near[:, :, 0] + swap(near[:, :, 1], "tensor"))[:, :pref_count]
    hidden_term = jnp.einsum("cpd,mcd->pm", total, rep_w2[:, 0], precision=HIGHEST)
    dh, _ = lax.optimization_barrier((dh, hidden_term))
    in_grads, sent = qkv_back(grads, edge, *tail, dh, gain, down1, where_at, 0, in_grads, 1, 2)
    got.append(swap(sent, "section"))
    sums = jnp.concatenate([total.reshape(2 * pref_count, half), hidden_term], axis=0)
    sums, _, _ = lax.optimization_barrier((sums, sent, got[0]))
    sums = all_sum(sums, ("rows",))
    total, hidden_term = sums[: 2 * pref_count].reshape(2, pref_count, half), sums[2 * pref_count :]
    hidden_term, *got = lax.optimization_barrier((hidden_term, *got))
    for part in range(2):
        in_grads = take(where_at, got[part], in_grads, part * share // 2)
    grad_hidden = all_sum(hidden_term, ("section", "tensor"))
    grad_b2 = jnp.sum(total, axis=1)
    mid_part = rep_w1.shape[1] // rows
    width_part = width // rows
    hidden_part = lax.dynamic_slice_in_dim(rep_hidden, rows_index * mid_part, mid_part, 1)
    grad_w2 = jnp.einsum("pm,cpd->mcd", hidden_part, total, precision=HIGHEST)
    grad_pre = grad_hidden * (1.0 - rep_hidden * rep_hidden)
    grad_b1 = jnp.sum(grad_pre, axis=0)
    embed_part = lax.dynamic_slice_in_dim(prefix_embed, rows_index * width_part, width_part, 1)
    grad_w1 = jnp.einsum("pd,pm->dm", embed_part, grad_pre, precision=HIGHEST)
    weight_part = lax.dynamic_slice_in_dim(rep_w1, rows_index * width_part, width_part, 0)
    grad_embed = jnp.einsum("pm,dm->pd", grad_pre, weight_part, precision=HIGHEST)
    return (acts[None], in_grads[None], grad_embed, grad_w1, grad_b1, grad_w2[:, None], grad_b2[None])


def solution(mesh):
    return jax.shard_map(
        on_device,
        mesh=mesh,
        in_specs=(
            P(None, ("rows", "tensor"), None),
            P(None, "rows", None),
            P(None, ("rows", "tensor"), None),
            P("section", None, None),
            P("section", None, None),
            P("section", "rows", None, "tensor"),
            P("section", None, "tensor"),
            P("section", ("tensor", "rows"), None),
            P("section", "rows", "tensor"),
            P("section", "tensor"),
            P("section", ("tensor", "rows"), None),
            P("section", None, None),
            P(),
            P(),
            P(),
            P(None, "section", None, "tensor"),
            P("section", None, "tensor"),
        ),
        out_specs=(
            P("section", None, ("rows", "tensor"), None),
            P("section", None, ("rows", "tensor"), None),
            P(None, "rows"),
            P("rows", None),
            P(),
            P("rows", "section", None, "tensor"),
            P("section", None, "tensor"),
        ),
        check_vma=False,
    )
```

```python
import functools

import jax
import jax.numpy as jnp
from jax import lax
from jax.experimental import pallas as pl
from jax.experimental.pallas import tpu as pltpu
from jax.sharding import PartitionSpec as P

HEAD = 64
EPSILON = 1e-05
NEGATIVE = -1000000000.0
HIGHEST = lax.Precision.HIGHEST
LOW = jnp.bfloat16
WIDE = jnp.float32
QB = 128
BAND = 256
KB = QB + BAND
PREP = 16


def swap(block, axis):
    return lax.ppermute(block, axis, [(0, 1), (1, 0)])


def all_sum(block, axes):
    for axis in axes:
        count = lax.axis_size(axis)
        if count & (count - 1):
            block = lax.psum(block, axis)
            continue
        bit = 1
        while bit < count:
            block = block + lax.ppermute(block, axis, [(i, i ^ bit) for i in range(count)])
            bit *= 2
    return block


def layer_norm(values, gain, shift):
    centre = values - jnp.mean(values, axis=-1, keepdims=True)
    spread = jnp.mean(centre * centre, axis=-1, keepdims=True)
    return centre * lax.rsqrt(spread + EPSILON) * gain + shift


def norm_back(values, gain, grad):
    centre = values - jnp.mean(values, axis=-1, keepdims=True)
    inverse = lax.rsqrt(jnp.mean(centre * centre, axis=-1, keepdims=True) + EPSILON)
    normal = centre * inverse
    scaled = grad * gain
    return inverse * (
        scaled
        - jnp.mean(scaled, axis=-1, keepdims=True)
        - normal * jnp.mean(scaled * normal, axis=-1, keepdims=True)
    )


def gelu_parts(values):
    root = 0.7978845608028654
    square = values * values
    inner = jnp.tanh(root * values * (1.0 + 0.044715 * square))
    half = 0.5 * (1.0 + inner)
    slope = half + 0.5 * values * (1.0 - inner * inner) * root * (1.0 + 3 * 0.044715 * square)
    return values * half, slope


def dot_nn(left, right):
    return jnp.dot(left, right, preferred_element_type=WIDE)


def dot_nt(left, right):
    return lax.dot_general(left, right, (((1,), (1,)), ((), ())), preferred_element_type=WIDE)


class ShardCopies:
    def __init__(self, plan, layer, rows, place_ref, buffers, out_ref, stage, sems, out_sems):
        self.plan, self.layer, self.rows, self.buffers = plan, layer, rows, buffers
        self.section, self.z, self.x = place_ref[0], place_ref[1], place_ref[2]
        self.out_ref, self.stage, self.sems, self.out_sems = out_ref, stage, sems, out_sems

    def inward(self, index, source):
        buffer, block = source
        piece = self.buffers[buffer].at[block * self.rows : (block + 1) * self.rows]
        return pltpu.make_async_copy(piece, self.stage.at[index], self.sems.at[index])

    def outward(self, index):
        steps, over_x = self.plan[index][:2]
        slot = ((self.z + 4 - steps) % 4) * 2 + (self.x + over_x) % 2
        return pltpu.make_async_copy(self.stage.at[index], self.out_ref.at[slot], self.out_sems.at[index])

    def fetch(self, indices):
        @pl.when(self.section == self.layer)
        def _():
            for index in indices:
                self.inward(index, self.plan[index][2]).start()

        @pl.when(self.section != self.layer)
        def _():
            for index in indices:
                self.inward(index, self.plan[index][3]).start()

    def deliver(self, index):
        self.inward(index, self.plan[index][2]).wait()
        self.outward(index).start()

    def finish(self):
        for index in range(len(self.plan)):
            self.outward(index).wait()


def split(refs, counts):
    groups = []
    for count in counts:
        groups.append(refs[:count])
        refs = refs[count:]
    return groups, refs


def stacked(pair):
    lane = lax.broadcasted_iota(jnp.int32, pair.shape, 1)
    zero = jnp.zeros_like(pair)
    return jnp.concatenate(
        [jnp.where(lane < HEAD, pair, zero), jnp.where(lane >= HEAD, pair, zero)], axis=0
    )


def unstacked(both):
    lane = lax.broadcasted_iota(jnp.int32, (QB, 2 * HEAD), 1)
    return jnp.where(lane < HEAD, both[:QB], both[QB:])


def dot_tn(left, right):
    return lax.dot_general(left, right, (((0,), (0,)), ((), ())), preferred_element_type=WIDE)


def lower():
    row = lax.broadcasted_iota(jnp.int32, (QB, 2 * QB), 0)
    lane = lax.broadcasted_iota(jnp.int32, (QB, 2 * QB), 1)
    return row <= jnp.where(lane < QB, lane, lane - QB)


def fold(band, near):
    return jnp.concatenate([jnp.where(near, band[BAND:], band[:QB]), band[QB:BAND]], axis=0)


def unfold(folded, near):
    zero = jnp.zeros((QB, 2 * QB), folded.dtype)
    edge = folded[:QB]
    return jnp.concatenate(
        [jnp.where(near, zero, edge), folded[QB:], jnp.where(near, edge, zero)], axis=0
    )


def fill_places(places):
    row = lax.broadcasted_iota(jnp.int32, (QB, 2 * QB), 0)
    places[:QB] = jnp.where(lower(), row + BAND, row)
    places[QB:] = row + QB


def fill_keys(scratch, prefix_ref, halo_ref, own_ref):
    scratch[:PREP] = prefix_ref[...]
    scratch[PREP : PREP + BAND] = halo_ref[...]
    scratch[PREP + BAND :] = own_ref[...]


def masked_scores(queries, keys, start_ref, block, pref_count, places, near):
    pre = dot_nt(keys[:PREP], queries)
    pre = jnp.where(
        lax.broadcasted_iota(jnp.int32, pre.shape, 0) < pref_count, pre, NEGATIVE
    )
    band = fold(dot_nt(keys[pl.ds(PREP + block * QB, KB)], queries), near)
    first = start_ref[:, block * QB : (block + 1) * QB] - block * QB
    first = jnp.concatenate([first, first], axis=1)
    return pre, jnp.where(places[...] >= first, band, NEGATIVE)


def attend_kernel(pref_count, layer, plans, *refs):
    q_ref, k_ref, v_ref, hk_ref, hv_ref, pk_ref, pv_ref, start_ref, place_ref, *refs = refs
    buffers, refs = split(refs, [names for names, *_ in plans])
    c_ref, probs_ref, *refs = refs
    wholes, (keys, vals, places, *refs) = refs[: len(plans)], refs[len(plans) :]
    copies = [
        ShardCopies(plan, layer, rows, place_ref, mine, whole_ref, *refs[3 * i : 3 * i + 3])
        for i, ((_, plan, rows, _), mine, whole_ref) in enumerate(zip(plans, buffers, wholes))
    ]
    pair, pairs = pl.program_id(0), pl.num_programs(0)

    for index in range(8):

        @pl.when(pair == index)
        def _(index=index):
            for copy in copies:
                if index:
                    copy.deliver(index - 1)
                copy.fetch([index])

    fill_keys(keys, pk_ref, hk_ref, k_ref)
    fill_keys(vals, pv_ref, hv_ref, v_ref)
    fill_places(places)
    near = lower()
    for block in range(q_ref.shape[0] // QB):
        span = slice(block * QB, (block + 1) * QB)
        seen = pl.ds(PREP + block * QB, KB)
        queries = stacked(q_ref[span, :] * jnp.asarray(HEAD ** (-0.5), LOW))
        pre, band = masked_scores(queries, keys, start_ref, block, pref_count, places, near)
        top = jnp.maximum(jnp.max(pre, axis=0, keepdims=True), jnp.max(band, axis=0, keepdims=True))
        pre = jnp.exp(pre - top)
        band = jnp.exp(band - top)
        total = jnp.sum(pre, axis=0, keepdims=True) + jnp.sum(band, axis=0, keepdims=True)
        inverse = 1.0 / total
        probs = jnp.concatenate([pre * inverse, unfold(band * inverse, near)], axis=0).astype(LOW)
        probs_ref[0, block] = probs
        out = dot_tn(probs, jnp.concatenate([vals[:PREP], vals[seen]], axis=0))
        c_ref[span, :] = unstacked(out).astype(LOW)

    @pl.when(pair == pairs - 1)
    def _():
        for copy in copies:
            copy.deliver(7)
            copy.finish()


def attend_back_kernel(q_ref, k_ref, v_ref, hk_ref, hv_ref, pk_ref, pv_ref, probs_ref, dc_ref,
                       dq_ref, dk_ref, dv_ref, edge_ref, prefix_ref, keys, vals, dkeys, dvals):
    fill_keys(keys, pk_ref, hk_ref, k_ref)
    fill_keys(vals, pv_ref, hv_ref, v_ref)
    dkeys[...] = jnp.zeros_like(dkeys)
    dvals[...] = jnp.zeros_like(dvals)
    scaling = HEAD ** (-0.5)
    for block in range(q_ref.shape[0] // QB):
        span = slice(block * QB, (block + 1) * QB)
        seen = pl.ds(PREP + block * QB, KB)
        queries = stacked(q_ref[span, :] * jnp.asarray(scaling, LOW))
        grads = stacked(dc_ref[span, :])
        low = probs_ref[0, block]
        probs = low.astype(WIDE)
        dprobs = dot_nt(jnp.concatenate([vals[:PREP], vals[seen]], axis=0), grads)
        inside = jnp.sum(probs * dprobs, axis=0, keepdims=True)
        slope = (probs * (dprobs - inside)).astype(LOW)
        terms = dot_nn(low, grads)
        dvals[:PREP] += terms[:PREP]
        dvals[seen] += terms[PREP:]
        terms = dot_nn(slope, queries)
        dkeys[:PREP] += terms[:PREP]
        dkeys[seen] += terms[PREP:]
        out = dot_tn(slope, jnp.concatenate([keys[:PREP], keys[seen]], axis=0))
        dq_ref[span, :] = (unstacked(out) * scaling).astype(LOW)
    dk_ref[...] = dkeys[PREP + BAND :].astype(LOW)
    dv_ref[...] = dvals[PREP + BAND :].astype(LOW)
    edge_ref[:BAND] = dkeys[PREP : PREP + BAND].astype(LOW)
    edge_ref[BAND:] = dvals[PREP : PREP + BAND].astype(LOW)
    prefix_ref[:PREP] = dkeys[:PREP]
    prefix_ref[PREP:] = dvals[:PREP]


def column(rows, place=lambda half, pair: 0, per=0):
    if per == 0:
        return pl.BlockSpec((rows, 2 * HEAD), lambda i: (0, i))
    return pl.BlockSpec((rows, 2 * HEAD), lambda i: (0, place(i // per) + i % per))


def attention_specs(tokens, per):
    return [
        column(tokens, lambda half: 3 * per * half, per),
        column(tokens, lambda half: 3 * per * half + per, per),
        column(tokens, lambda half: 3 * per * half + 2 * per, per),
        column(BAND, lambda half: 2 * per * (1 - half), per),
        column(BAND, lambda half: 2 * per * (1 - half) + per, per),
        column(PREP, lambda half: 2 * per * half, per),
        column(PREP, lambda half: 2 * per * half + per, per),
    ]


def probs_spec(blocks):
    return pl.BlockSpec((1, blocks, PREP + KB, 2 * QB), lambda i: (i, 0, 0, 0))


def attend(pref_count, qkv, halo, prefix, start, place, layer=0, chores=()):
    tokens, width = qkv.shape[0], qkv.shape[1] // 3
    pairs, blocks = width // (2 * HEAD), tokens // QB
    chores = chores if pairs == 8 else ()
    anywhere = pl.BlockSpec(memory_space=pl.ANY)
    stages = []
    for _, _, rows, columns in chores:
        stages += [
            pltpu.VMEM((8, rows, columns), LOW),
            pltpu.SemaphoreType.DMA((8,)),
            pltpu.SemaphoreType.DMA((8,)),
        ]
    operands = [buffer for buffers, *_ in chores for buffer in buffers]
    return pl.pallas_call(
        functools.partial(
            attend_kernel, pref_count, layer, [(len(chore[0]), *chore[1:]) for chore in chores]
        ),
        grid=(pairs,),
        in_specs=attention_specs(tokens, pairs // 2)
        + [pl.BlockSpec((1, tokens), lambda i: (0, 0)), pl.BlockSpec(memory_space=pltpu.SMEM)]
        + [anywhere] * len(operands),
        out_specs=[column(tokens), probs_spec(blocks)] + [anywhere] * len(chores),
        out_shape=[
            jax.ShapeDtypeStruct((tokens, width), LOW),
            jax.ShapeDtypeStruct((pairs, blocks, PREP + KB, 2 * QB), LOW),
        ]
        + [jax.ShapeDtypeStruct((8, rows, columns), LOW) for _, _, rows, columns in chores],
        scratch_shapes=[
            pltpu.VMEM((PREP + BAND + tokens, 2 * HEAD), LOW),
            pltpu.VMEM((PREP + BAND + tokens, 2 * HEAD), LOW),
            pltpu.VMEM((2 * QB, 2 * QB), jnp.int32),
            *stages,
        ],
        name="attend",
        compiler_params=pltpu.CompilerParams(vmem_limit_bytes=56 * 2**20),
        cost_estimate=pl.CostEstimate(flops=12 * 10**9, bytes_accessed=2 * qkv.size, transcendentals=0),
    )(qkv, qkv, qkv, halo, halo, prefix, prefix, start, place, *operands)


def attend_back(qkv, halo, prefix, probs, grad):
    tokens, width = qkv.shape[0], qkv.shape[1] // 3
    pairs, blocks = width // (2 * HEAD), tokens // QB
    keys = PREP + BAND + tokens
    sizes = [(tokens, LOW)] * 3 + [(2 * BAND, LOW), (2 * PREP, WIDE)]
    return pl.pallas_call(
        attend_back_kernel,
        grid=(pairs,),
        in_specs=attention_specs(tokens, pairs // 2) + [probs_spec(blocks), column(tokens)],
        out_specs=[column(rows) for rows, _ in sizes],
        out_shape=[jax.ShapeDtypeStruct((rows, width), kind) for rows, kind in sizes],
        scratch_shapes=[
            pltpu.VMEM((keys, 2 * HEAD), LOW),
            pltpu.VMEM((keys, 2 * HEAD), LOW),
            pltpu.VMEM((keys, 2 * HEAD), WIDE),
            pltpu.VMEM((keys, 2 * HEAD), WIDE),
        ],
        name="attend_back",
        cost_estimate=pl.CostEstimate(flops=16 * 10**9, bytes_accessed=4 * qkv.size, transcendentals=0),
    )(qkv, qkv, qkv, halo, halo, prefix, prefix, probs, grad)


CHUNK = 512
ROWS = 512


def by_rows(total, body):
    step = min(ROWS, total)

    @pl.loop(0, total // step)
    def _(index):
        body(pl.ds(pl.multiple_of(index * step, step), step))


def of_half(step, count, own_ref, far_ref, body):
    @pl.when(step < count)
    def _():
        body(own_ref)

    @pl.when(step >= count)
    def _():
        body(far_ref)


def halves(shape, count, across):
    def spec(place):
        return pl.BlockSpec(shape, lambda j: (0, place(j)) if across else (place(j), 0))

    return [spec(lambda j: jnp.minimum(j, count - 1)), spec(lambda j: jnp.maximum(j - count, 0))]


def whole(shape):
    return pl.BlockSpec(shape, lambda j: (0,) * len(shape))


def slab(index, tokens, width, part=0):
    return pl.BlockSpec((None, tokens, width), lambda j: (index, part, 0))


def call(kernel, grid, in_specs, out_specs, out_shape, scratch, name, flops, operands, buffer=None):
    size, count = sum(o.size * o.dtype.itemsize for o in operands), len(operands)
    body, aliases = kernel, {}
    if buffer is not None:
        in_specs, operands = in_specs + [pl.BlockSpec(memory_space=pl.ANY)], (*operands, buffer)
        aliases = {count: 0}

        def body(*refs):
            kernel(*refs[:count], *refs[count + 1 :])

    return pl.pallas_call(
        body,
        grid=(grid,),
        in_specs=in_specs,
        out_specs=out_specs,
        out_shape=out_shape,
        input_output_aliases=aliases,
        scratch_shapes=scratch,
        name=name,
        compiler_params=pltpu.CompilerParams(vmem_limit_bytes=56 * 2**20),
        cost_estimate=pl.CostEstimate(flops=flops, bytes_accessed=size, transcendentals=0),
    )(*operands)


def qkv_kernel(x_ref, gain_ref, shift_ref, own_ref, far_ref, bias_ref, out_ref, halo_ref, normed):
    step = pl.program_id(0)

    @pl.when(step == 0)
    def _():
        def body(span):
            normed[span] = layer_norm(
                x_ref[span].astype(WIDE), gain_ref[...], shift_ref[...]
            ).astype(LOW)

        by_rows(x_ref.shape[0], body)

    def body(weight_ref):
        third = weight_ref.shape[1] // 3
        for part in range(3):
            span = slice(part * third, (part + 1) * third)
            out = (dot_nn(normed[...], weight_ref[:, span]) + bias_ref[:, span]).astype(LOW)
            out_ref[:, span] = out
            if part:
                halo_ref[:, (part - 1) * third : part * third] = out[out.shape[0] - BAND :]

    of_half(step, 1, own_ref, far_ref, body)


def qkv_forward(x, gain, shift, weights, bias):
    tokens, width = x.shape
    half = weights[0].shape[1] // 3
    return call(
        qkv_kernel,
        2,
        [whole(x.shape), whole((1, width)), whole((1, width))]
        + halves((width, 3 * half), 1, True)
        + [pl.BlockSpec((1, 3 * half), lambda j: (0, j))],
        [
            pl.BlockSpec((tokens, 3 * half), lambda j: (0, j)),
            pl.BlockSpec((BAND, 2 * half), lambda j: (0, j)),
        ],
        [
            jax.ShapeDtypeStruct((tokens, 6 * half), LOW),
            jax.ShapeDtypeStruct((BAND, 4 * half), LOW),
        ],
        [pltpu.VMEM(x.shape, LOW)],
        "qkv",
        12 * tokens * width * half,
        (x, gain, shift, *weights, bias),
    )


def mlp_kernel(count, x_ref, c_ref, po_ref, pf_ref, b0_ref, gain_ref, shift_ref, fo_ref, ff_ref, bias_ref, wo_ref,
               wf_ref, b1_ref, y_ref, h_ref, slope_ref, low_ref, normed):
    step = pl.program_id(0)
    half = po_ref.shape[0]

    @pl.when(step == 0)
    def _():
        def body(span):
            h = x_ref[span].astype(WIDE) + (
                dot_nn(c_ref[span, :half], po_ref[...])
                + dot_nn(c_ref[span, half:], pf_ref[...])
                + b0_ref[...]
            )
            h_ref[span] = h
            normed[span] = layer_norm(h, gain_ref[...], shift_ref[...]).astype(LOW)
            y_ref[span] = h + b1_ref[...]

        by_rows(x_ref.shape[0], body)

    def half_body(up_ref, down_ref):
        def body(span):
            active, slope = gelu_parts(dot_nn(normed[span], up_ref[...]) + bias_ref[...])
            slope_ref[span] = slope.astype(LOW)
            y_ref[span] += dot_nn(active.astype(LOW), down_ref[...])

        by_rows(x_ref.shape[0], body)

    of_half(step, count, (fo_ref, wo_ref), (ff_ref, wf_ref), lambda refs: half_body(*refs))

    @pl.when(step == 2 * count - 1)
    def _():
        low_ref[...] = y_ref[...].astype(LOW)


def mlp_forward(x, c, weights, biases, gain, shift, fc_bias):
    tokens, width = x.shape
    half, count = width // 2, weights["fc"][0].shape[1] // CHUNK
    row = whole((1, width))
    return call(
        functools.partial(mlp_kernel, count),
        2 * count,
        [whole(x.shape), whole(c.shape), whole((half, width)), whole((half, width)), row, row, row]
        + halves((width, CHUNK), count, True)
        + [pl.BlockSpec((1, CHUNK), lambda j: (0, j))]
        + halves((CHUNK, width), count, False)
        + [row],
        [
            slab(0, tokens, width),
            whole(x.shape),
            pl.BlockSpec((tokens, CHUNK), lambda j: (0, j)),
            whole(x.shape),
        ],
        [
            jax.ShapeDtypeStruct((2, tokens, width), WIDE),
            jax.ShapeDtypeStruct(x.shape, WIDE),
            jax.ShapeDtypeStruct((tokens, 2 * count * CHUNK), LOW),
            jax.ShapeDtypeStruct(x.shape, LOW),
        ],
        [pltpu.VMEM(x.shape, LOW)],
        "mlp",
        2 * tokens * width * (width + 4 * count * CHUNK),
        (x, c, *weights["proj"], biases[0], gain, shift, *weights["fc"], fc_bias, *weights["fc2"], biases[1]),
    )


def mlp_back_kernel(count, dy_ref, h_ref, gain_ref, slope_ref, wo_ref, wf_ref, fo_ref, ff_ref, po_ref, pf_ref,
                    dh_ref, dc_ref, total):
    step = pl.program_id(0)
    half = po_ref.shape[0]

    def half_body(first, up_ref, down_ref):
        def body(span):
            du = (dot_nt(dy_ref[span], down_ref[...]) * slope_ref[span].astype(WIDE)).astype(LOW)
            dm = dot_nt(du, up_ref[...])
            total[span] = dm if first else total[span] + dm

        by_rows(dy_ref.shape[0], body)

    @pl.when(step == 0)
    def _():
        half_body(True, fo_ref, wo_ref)

    @pl.when((step > 0) & (step < count))
    def _():
        half_body(False, fo_ref, wo_ref)

    @pl.when(step >= count)
    def _():
        half_body(False, ff_ref, wf_ref)

    @pl.when(step == 2 * count - 1)
    def _():
        def body(span):
            dh = dy_ref[span].astype(WIDE) + norm_back(h_ref[span], gain_ref[...], total[span])
            dh_ref[span] = dh
            low = dh.astype(LOW)
            dc_ref[span, :half] = dot_nt(low, po_ref[...]).astype(LOW)
            dc_ref[span, half:] = dot_nt(low, pf_ref[...]).astype(LOW)

        by_rows(dy_ref.shape[0], body)


def mlp_back(dy, h, gain, slope, weights):
    tokens, width = dy.shape
    half, count = width // 2, weights["fc"][0].shape[1] // CHUNK
    return call(
        functools.partial(mlp_back_kernel, count),
        2 * count,
        [whole(dy.shape), whole(dy.shape), whole((1, width)), pl.BlockSpec((tokens, CHUNK), lambda j: (0, j))]
        + halves((CHUNK, width), count, False)
        + halves((width, CHUNK), count, True)
        + [whole((half, width)), whole((half, width))],
        [whole(dy.shape), whole(dy.shape)],
        [jax.ShapeDtypeStruct(dy.shape, WIDE), jax.ShapeDtypeStruct(dy.shape, LOW)],
        [pltpu.VMEM(dy.shape, WIDE)],
        "mlp_back",
        2 * tokens * width * (width + 4 * count * CHUNK),
        (dy, h, gain, slope, *weights["fc2"], *weights["fc"], *weights["proj"]),
    )


def mlp_both_kernel(count, x_ref, c_ref, dy_ref, po_ref, pf_ref, b0_ref, gain_ref, shift_ref, fo_ref, ff_ref, bias_ref,
                    wo_ref, wf_ref, b1_ref, y_ref, low_ref, dh_ref, dc_ref, h_ref, normed, total):
    step = pl.program_id(0)
    half = po_ref.shape[0]

    @pl.when(step == 0)
    def _():
        def body(span):
            h = x_ref[span].astype(WIDE) + (
                dot_nn(c_ref[span, :half], po_ref[...])
                + dot_nn(c_ref[span, half:], pf_ref[...])
                + b0_ref[...]
            )
            h_ref[span] = h
            normed[span] = layer_norm(h, gain_ref[...], shift_ref[...]).astype(LOW)
            y_ref[span] = h + b1_ref[...]
            total[span] = jnp.zeros_like(h)

        by_rows(x_ref.shape[0], body)

    def half_body(up_ref, down_ref):
        def body(span):
            active, slope = gelu_parts(dot_nn(normed[span], up_ref[...]) + bias_ref[...])
            du = (dot_nt(dy_ref[span], down_ref[...]) * slope).astype(LOW)
            y_ref[span] += dot_nn(active.astype(LOW), down_ref[...])
            total[span] += dot_nt(du, up_ref[...])

        by_rows(x_ref.shape[0], body)

    of_half(step, count, (fo_ref, wo_ref), (ff_ref, wf_ref), lambda refs: half_body(*refs))

    @pl.when(step == 2 * count - 1)
    def _():
        def body(span):
            low_ref[span] = y_ref[span].astype(LOW)
            dh = dy_ref[span].astype(WIDE) + norm_back(h_ref[span], gain_ref[...], total[span])
            dh_ref[span] = dh
            low = dh.astype(LOW)
            dc_ref[span, :half] = dot_nt(low, po_ref[...]).astype(LOW)
            dc_ref[span, half:] = dot_nt(low, pf_ref[...]).astype(LOW)

        by_rows(x_ref.shape[0], body)


def mlp_both(acts, x, c, dy, weights, biases, gain, shift, fc_bias):
    tokens, width = x.shape
    half, count = width // 2, weights["fc"][0].shape[1] // CHUNK
    row, full = whole((1, width)), whole(x.shape)
    return call(
        functools.partial(mlp_both_kernel, count),
        2 * count,
        [full, full, full, whole((half, width)), whole((half, width)), row, row, row]
        + halves((width, CHUNK), count, True)
        + [pl.BlockSpec((1, CHUNK), lambda j: (0, j))]
        + halves((CHUNK, width), count, False)
        + [row],
        [slab(1, tokens, width), full, full, full],
        [jax.ShapeDtypeStruct(acts.shape, WIDE)]
        + [jax.ShapeDtypeStruct(x.shape, kind) for kind in (LOW, WIDE, LOW)],
        [pltpu.VMEM(x.shape, WIDE), pltpu.VMEM(x.shape, LOW), pltpu.VMEM(x.shape, WIDE)],
        "mlp_both",
        4 * tokens * width * (width + 4 * count * CHUNK),
        (x, c, dy, *weights["proj"], biases[0], gain, shift, *weights["fc"], fc_bias, *weights["fc2"], biases[1]),
        acts,
    )


def qkv_back_kernel(reach, dq_ref, dk_ref, dv_ref, hk_ref, hv_ref, own_ref, far_ref, x_ref, dh_ref, gain_ref, other_ref,
                    section_ref, dx_ref, low_ref, total):
    step = pl.program_id(0)

    def joined_grads(grad_ref, halo_ref):
        grad = grad_ref[...]
        if not reach:
            return grad
        early = grad.shape[0] - reach
        late = (grad[early:].astype(WIDE) + halo_ref[...].astype(WIDE)).astype(LOW)
        return jnp.concatenate([grad[:early], late], axis=0) if early else late

    def half_body(first, weight_ref):
        grads = (dq_ref[...], joined_grads(dk_ref, hk_ref), joined_grads(dv_ref, hv_ref))
        term = dot_nt(jnp.concatenate(grads, axis=1), weight_ref[...])
        total[...] = term if first else total[...] + term

    @pl.when(step == 0)
    def _():
        half_body(True, own_ref)

    @pl.when(step == 1)
    def _():
        half_body(False, far_ref)

        def body(span):
            dx = dh_ref[span] + norm_back(x_ref[span].astype(WIDE), gain_ref[...], total[span])
            dx_ref[span] = dx
            low = dx.astype(LOW)
            low_ref[span] = jnp.where(section_ref[0] == 0, other_ref[span], low)

        by_rows(x_ref.shape[0], body)


def qkv_back(grads, halo, weights, x, dh, gain, other, section, layer, buffer=None, part=0, parts=1):
    width = x.shape[1]
    tokens, half = x.shape[0] // parts, width // 2
    reach = BAND if part == parts - 1 else 0
    piece = pl.BlockSpec((tokens, half), lambda j: (part, j))
    edges = [pl.BlockSpec((BAND, half), lambda j, i=i: (i, 1 - j)) for i in range(2)]
    mine, shape = pl.BlockSpec((tokens, width), lambda j: (part, 0)), (tokens, width)
    return call(
        functools.partial(qkv_back_kernel, reach),
        2,
        [piece, piece, piece, *edges]
        + halves((width, 3 * half), 1, True)
        + [mine, mine, whole((1, width)), mine, pl.BlockSpec(memory_space=pltpu.SMEM)],
        [slab(layer, tokens, width, part), whole(shape)],
        [jax.ShapeDtypeStruct((2, *x.shape), WIDE), jax.ShapeDtypeStruct(shape, LOW)],
        [pltpu.VMEM(shape, WIDE)],
        "qkv_back",
        12 * tokens * width * half,
        (*grads, halo, halo, *weights, x, dh, gain, other, section),
        buffer,
    )


def take_kernel(section_ref, got_ref, held_ref, out_ref):
    out_ref[0] = got_ref[...].astype(WIDE)


def take(section, got, buffer, start=0):
    rows, width = got.shape
    step = min(256, rows)
    base = start // step
    return pl.pallas_call(
        take_kernel,
        grid_spec=pltpu.PrefetchScalarGridSpec(
            num_scalar_prefetch=1,
            grid=(rows // step,),
            in_specs=[
                pl.BlockSpec((step, width), lambda i, s: (i, 0)),
                pl.BlockSpec(memory_space=pl.ANY),
            ],
            out_specs=pl.BlockSpec((1, step, width), lambda i, s: (1 - s[0], base + i, 0)),
        ),
        out_shape=jax.ShapeDtypeStruct(buffer.shape, WIDE),
        input_output_aliases={2: 0},
        name="take",
        cost_estimate=pl.CostEstimate(flops=0, bytes_accessed=6 * got.size, transcendentals=0),
    )(section, got, buffer)


NAMES = ("qkv", "proj", "fc", "fc2")
JOIN, QKV, ATTEND, MLP = range(4)
BESIDE = (0, 1, 2, 3)
ORDER = (
    (0, 0, 0, 0, 0), (2, 0, 0, 0, 0), (1, 0, 0, 0, 0), (0, 2, 0, 0, 0), (1, 1, 0, 0, 0),
    (2, 2, 0, 0, 0), (2, 0, 1, 0, 0), (1, 0, 1, 0, 0), (1, 0, 0, 1, 0), (0, 8, 0, 0, 0),
    (0, 0, 1, 0, 0), (1, 2, 0, 1, 0), (2, 2, 1, 0, 0), (2, 0, 2, 0, 0), (0, 0, 2, 0, 0),
    (1, 0, 2, 0, 0), (0, 2, 1, 0, 0), (2, 9, 0, 0, 0), (1, 0, 2, 1, 0), (0, 2, 2, 0, 0),
    (1, 3, 0, 0, 0), (0, 0, 3, 0, 0), (1, 2, 0, 0, 0), (2, 9, 1, 0, 0), (2, 2, 2, 0, 0),
    (1, 2, 2, 1, 0), (0, 7, 0, 0, 0), (2, 9, 2, 0, 0), (1, 0, 3, 1, 0), (0, 2, 3, 0, 0),
    (2, 6, 0, 0, 0), (1, 2, 3, 0, 0), (0, 6, 0, 0, 0), (1, 2, 2, 0, 0), (2, 7, 0, 0, 0),
    (0, 6, 1, 0, 0), (2, 6, 1, 0, 0), (1, 0, 1, 1, 0), (0, 7, 1, 0, 0), (1, 0, 3, 0, 0),
    (2, 7, 1, 0, 0), (1, 2, 1, 0, 0), (0, 6, 2, 0, 0), (2, 6, 2, 0, 0), (1, 2, 3, 1, 0),
    (0, 7, 2, 0, 0), (2, 7, 2, 0, 0), (1, 2, 1, 1, 0), (0, 6, 3, 0, 0), (0, 7, 3, 0, 0),
    (3, 0, 0, 0, 0), (3, 0, 1, 0, 0), (3, 0, 2, 0, 0), (3, 0, 3, 0, 0), (3, 0, 0, 1, 0),
    (3, 0, 1, 1, 0), (3, 0, 2, 1, 0), (3, 0, 3, 1, 0), (3, 1, 0, 0, 0), (3, 2, 0, 0, 0),
    (3, 3, 0, 0, 0), (3, 1, 0, 1, 0), (3, 2, 0, 1, 0), (3, 3, 0, 1, 0),
)
JOINED = {8: ((1, 0, 0, 0), (1, 0, 0, 1)), 9: ((8, 0, 0, 0), (8, 0, 1, 0))}
DEEP = 2
LATE = 3


def move(block, link):
    if link == 1:
        return swap(block, "section")
    count = lax.axis_size("rows")
    if link == 0:
        return lax.ppermute(block, "rows", [(i, i ^ 1) for i in range(count)])
    return lax.ppermute(block, "rows", [(i, (i + 2) % count) for i in range(count)])


def spread(shards, section, run):
    held = {(base, 0, 0, 0): shards[name] for base, name in enumerate(NAMES)}
    sent, passed, awaited = {}, [], []

    def get(key):
        if key not in held:
            base = key[0]
            if base in JOINED:
                held[key] = jnp.concatenate([get(part) for part in JOINED[base]], axis=0)
            else:
                raw = base // 2
                held[key] = jnp.where(section == base % 2, get((raw, 0, 0, 0)), get((raw, 0, 0, 1)))
        return held[key]

    for link, *key in ORDER:
        if link == 3:
            now, later = run(*key[:3], get)
            passed = [now] if now is not None else passed
            if later is not None:
                awaited.append([LATE, later])
            continue
        block, ahead = get(tuple(key)), sent.setdefault(link, [])
        behind = list(passed)
        if len(ahead) >= DEEP:
            behind.append(ahead[-DEEP])
        for entry in awaited:
            entry[0] -= 1
            if entry[0] == 0:
                behind.append(entry[1])
        if behind:
            block, *_ = lax.optimization_barrier((block, *behind))
        base, steps, over_x, over_y = key
        target = (base, steps + (link == 2), over_x + (link == 0), over_y + (link == 1))
        held[target] = move(block, link)
        ahead.append(held[target])


def pieces(matrix, layer, resolved):
    result = []
    for steps in range(4):
        for over_x in range(2):
            if matrix == 1:
                key = (9, steps, 0, 0)
                near, away = (key, 2 * over_x), (key, 2 * over_x + 1)
            elif resolved:
                near = away = ((2 * matrix + layer, steps, over_x, 0), 0)
            else:
                near, away = ((matrix, steps, over_x, 0), 0), ((matrix, steps, over_x, 1), 0)
            result.append((steps, over_x, near, away))
    return result


def join_kernel(plan, layer, rows, place_ref, *refs):
    copies = ShardCopies(plan, layer, rows, place_ref, refs[:-4], *refs[-4:])
    copies.fetch(range(8))
    for index in range(8):
        copies.deliver(index)
    copies.finish()


def plan_of(matrix, layer, get):
    keys, plan = [], []
    resolved = any(link < 3 and base == 2 * matrix for link, base, *_ in ORDER if matrix > 1)
    for steps, over_x, *sources in pieces(matrix, layer, resolved):
        spots = []
        for key, block in sources:
            if key not in keys:
                keys.append(key)
            spots.append((keys.index(key), block))
        plan.append((steps, over_x, *spots))
    return [get(key) for key in keys], plan


def joined(matrix, layer, get, shape, place):
    rows, columns = shape
    buffers, plan = plan_of(matrix, layer, get)
    anywhere = pl.BlockSpec(memory_space=pl.ANY)
    whole = pl.pallas_call(
        functools.partial(join_kernel, plan, layer, rows),
        in_specs=[pl.BlockSpec(memory_space=pltpu.SMEM)] + [anywhere] * len(buffers),
        out_specs=anywhere,
        out_shape=jax.ShapeDtypeStruct((8, rows, columns), LOW),
        scratch_shapes=[
            pltpu.VMEM((8, rows, columns), LOW),
            pltpu.SemaphoreType.DMA((8,)),
            pltpu.SemaphoreType.DMA((8,)),
        ],
        name="join",
        cost_estimate=pl.CostEstimate(flops=0, bytes_accessed=4 * 8 * rows * columns, transcendentals=0),
    )(place, *buffers)
    return whole.reshape(8 * rows, columns)


def forward(shards, x, dy, start, smalls, pref_count):
    section, rows = lax.axis_index("section"), lax.axis_index("rows")
    weights, kept, outputs, slopes = [{}, {}], [None, None], [None, None], []

    def run(kind, matrix, layer, get):
        small, mine = smalls[layer], weights[layer]
        place = jnp.stack([section, rows // 2, rows % 2]).astype(jnp.int32)
        if kind == JOIN:
            name = NAMES[matrix]
            if layer and matrix in BESIDE:
                return None, None
            near = joined(matrix, layer, get, shards[name].shape, place)
            mine[name] = (near, swap(near, "tensor"))
            return mine[name]
        if kind == QKV:
            source = outputs[0][1] if layer else x
            qkv, edge = qkv_forward(source, small["gain"][0:1], small["shift"][0:1], mine["qkv"], small["qkv"])
            kept[layer] = (source, qkv, lax.ppermute(edge, "tensor", [(0, 1)]))
            return qkv, kept[layer][2]
        if kind == ATTEND:
            source, qkv, halo = kept[layer]
            chores = []
            if get is not None and not layer:
                chores = [(*plan_of(other, 1, get), *shards[NAMES[other]].shape) for other in BESIDE]
            ahead = start
            if chores:
                ahead, _ = lax.optimization_barrier((start, mine["proj"][1]))
            c, probs, *wholes = attend(pref_count, qkv, halo, small["prefix"], ahead, place, 1, chores)
            for name, near in zip([NAMES[other] for other in BESIDE], wholes):
                near = near.reshape(-1, near.shape[-1])
                weights[1][name] = (near, swap(near, "tensor"))
            kept[layer] = (source, qkv, halo, probs, c)
            return c, None
        source, qkv, halo, probs, c = kept[layer]
        kept[layer] = (source, qkv, halo, probs)
        biases = (small["out"][0:1], small["out"][1:2])
        norm = (small["gain"][1:2], small["shift"][1:2])
        if layer:
            *outputs[1], dh, dc = mlp_both(outputs[0][0], source, c, dy, mine, biases, *norm, small["fc"])
            slopes.extend((dh, dc))
        else:
            acts, h, slope, low = mlp_forward(source, c, mine, biases, *norm, small["fc"])
            outputs[0] = (acts, low)
            slopes.extend((h, slope))
        return slopes[-1], None

    if lax.axis_size("rows") == 8:
        spread(shards, section, run)
    else:
        for name in NAMES:
            near = lax.all_gather(shards[name], ("section", "rows"), axis=0, tiled=True)
            near = near.reshape(2, -1, near.shape[1])
            far = swap(near, "tensor")
            for layer in range(2):
                weights[layer][name] = (near[layer], far[layer])
        for link, *stage in ORDER:
            if link == 3 and stage[0] != JOIN:
                run(*stage[:3], None)
    return weights, kept, outputs, slopes


def on_device(
    tokens,
    segment_ids,
    cotangent,
    ln_gain,
    ln_bias,
    w_qkv,
    query_key_value_bias,
    w_proj,
    w_fc,
    fc_bias,
    w_fc2,
    out_bias,
    prefix_embed,
    rep_w1,
    rep_b1,
    rep_w2,
    rep_b2,
):
    share, width = tokens.shape[1:]
    section, core = lax.axis_index("section"), lax.axis_index("tensor")
    rows_index, rows = lax.axis_index("rows"), lax.axis_size("rows")
    half = rep_w2.shape[-1]
    pref_count = prefix_embed.shape[0]

    shards = {
        "qkv": w_qkv[0].astype(LOW).reshape(w_qkv.shape[1], -1),
        "proj": w_proj[0].astype(LOW),
        "fc": w_fc[0].astype(LOW),
        "fc2": w_fc2[0].astype(LOW),
    }
    rep_hidden = jnp.tanh(jnp.dot(prefix_embed, rep_w1, precision=HIGHEST) + rep_b1)
    prefix = jnp.einsum("pm,mcd->pcd", rep_hidden, rep_w2[:, 0], precision=HIGHEST) + rep_b2[0]
    prefix = prefix.astype(LOW).astype(WIDE)
    prefix = jnp.pad(prefix, ((0, PREP - pref_count), (0, 0), (0, 0)))
    parts = [ln_gain[0], ln_bias[0], out_bias[0], query_key_value_bias[0], fc_bias[0], prefix]
    packed = jnp.concatenate([part.reshape(-1) for part in parts])
    near = jnp.stack([packed, swap(packed, "tensor")])
    away = swap(near, "section")
    smalls = []
    for layer in range(2):
        cut, place = [], 0
        chosen = jnp.where(section == layer, near, away)
        for part in parts:
            cut.append([chosen[h, place : place + part.size].reshape(part.shape) for h in range(2)])
            place += part.size
        smalls.append(
            {
                "gain": cut[0][0],
                "shift": cut[1][0],
                "out": cut[2][0],
                "qkv": jnp.concatenate([cut[3][h].reshape(1, -1) for h in range(2)], axis=1),
                "fc": jnp.concatenate([cut[4][h].reshape(1, -1) for h in range(2)], axis=1),
                "prefix": jnp.concatenate(
                    [cut[5][h].reshape(PREP, -1).astype(LOW) for h in range(2)], axis=1
                ),
            }
        )

    own = section
    segments = lax.dynamic_index_in_dim(segment_ids, own, 0, keepdims=False).reshape(-1)
    mine = lax.dynamic_slice_in_dim(segments, core * share, share)
    start = jnp.sum(segments[:, None] < mine[None, :], axis=0, dtype=jnp.int32)
    start = (start - core * share + BAND)[None]

    x = lax.dynamic_index_in_dim(tokens, own, 0, keepdims=False)
    dy = lax.dynamic_index_in_dim(cotangent, own, 0, keepdims=False)
    weights, (kept0, kept1), ((_, low0), (acts, low1)), (h, slope, dh, dc) = forward(
        shards, x, dy, start, smalls, pref_count
    )
    dy = lax.dynamic_index_in_dim(cotangent, own, 0, keepdims=False)
    got_acts = swap(jnp.where(section == 0, low1, low0), "section")
    where_at = section.astype(jnp.int32).reshape(1)
    nowhere = jnp.ones((1,), jnp.int32)

    x1, qkv, halo, probs = kept1
    *grads, edge, pre1 = attend_back(qkv, halo, smalls[1]["prefix"], probs, dc)
    edge = lax.ppermute(edge, "tensor", [(1, 0)])
    in_grads, down1 = qkv_back(
        grads, edge, weights[1]["qkv"], x1, dh, smalls[1]["gain"][0:1], low1, nowhere, 1
    )
    dh, dc = mlp_back(down1, h, smalls[0]["gain"][1:2], slope, weights[0])
    got_acts, dc = lax.optimization_barrier((got_acts, dc))
    acts = take(where_at, got_acts, acts)
    x0, qkv, halo, probs = kept0
    *grads, edge, pre0 = attend_back(qkv, halo, smalls[0]["prefix"], probs, dc)
    edge = lax.ppermute(edge, "tensor", [(1, 0)])

    pre0, pre1 = [pre.reshape(2, PREP, 2, half) for pre in (pre0, pre1)]
    near = jnp.where(section == 0, pre0, pre1) + swap(jnp.where(section == 0, pre1, pre0), "section")
    tail = (weights[0]["qkv"], x0)
    gain = smalls[0]["gain"][0:1]
    in_grads, sent = qkv_back(grads, grads[0], *tail, dh, gain, down1, where_at, 0, in_grads, 0, 2)
    got = [swap(sent, "section")]
    near, _ = lax.optimization_barrier((near, sent))
    total = (near[:, :, 0] + swap(near[:, :, 1], "tensor"))[:, :pref_count]
    hidden_term = jnp.einsum("cpd,mcd->pm", total, rep_w2[:, 0], precision=HIGHEST)
    dh, _ = lax.optimization_barrier((dh, hidden_term))
    in_grads, sent = qkv_back(grads, edge, *tail, dh, gain, down1, where_at, 0, in_grads, 1, 2)
    got.append(swap(sent, "section"))
    sums = jnp.concatenate([total.reshape(2 * pref_count, half), hidden_term], axis=0)
    sums, _, _ = lax.optimization_barrier((sums, sent, got[0]))
    sums = all_sum(sums, ("rows",))
    total, hidden_term = sums[: 2 * pref_count].reshape(2, pref_count, half), sums[2 * pref_count :]
    hidden_term, *got = lax.optimization_barrier((hidden_term, *got))
    for part in range(2):
        in_grads = take(where_at, got[part], in_grads, part * share // 2)
    grad_hidden = all_sum(hidden_term, ("section", "tensor"))
    grad_b2 = jnp.sum(total, axis=1)
    mid_part = rep_w1.shape[1] // rows
    width_part = width // rows
    hidden_part = lax.dynamic_slice_in_dim(rep_hidden, rows_index * mid_part, mid_part, 1)
    grad_w2 = jnp.einsum("pm,cpd->mcd", hidden_part, total, precision=HIGHEST)
    grad_pre = grad_hidden * (1.0 - rep_hidden * rep_hidden)
    grad_b1 = jnp.sum(grad_pre, axis=0)
    embed_part = lax.dynamic_slice_in_dim(prefix_embed, rows_index * width_part, width_part, 1)
    grad_w1 = jnp.einsum("pd,pm->dm", embed_part, grad_pre, precision=HIGHEST)
    weight_part = lax.dynamic_slice_in_dim(rep_w1, rows_index * width_part, width_part, 0)
    grad_embed = jnp.einsum("pm,dm->pd", grad_pre, weight_part, precision=HIGHEST)
    return (acts[None], in_grads[None], grad_embed, grad_w1, grad_b1, grad_w2[:, None], grad_b2[None])


def solution(mesh):
    return jax.shard_map(
        on_device,
        mesh=mesh,
        in_specs=(
            P(None, ("rows", "tensor"), None),
            P(None, "rows", None),
            P(None, ("rows", "tensor"), None),
            P("section", None, None),
            P("section", None, None),
            P("section", "rows", None, "tensor"),
            P("section", None, "tensor"),
            P("section", ("tensor", "rows"), None),
            P("section", "rows", "tensor"),
            P("section", "tensor"),
            P("section", ("tensor", "rows"), None),
            P("section", None, None),
            P(),
            P(),
            P(),
            P(None, "section", None, "tensor"),
            P("section", None, "tensor"),
        ),
        out_specs=(
            P("section", None, ("rows", "tensor"), None),
            P("section", None, ("rows", "tensor"), None),
            P(None, "rows"),
            P("rows", None),
            P(),
            P("rows", "section", None, "tensor"),
            P("section", None, "tensor"),
        ),
        check_vma=False,
    )
```

```python
import functools

import jax
import jax.numpy as jnp
from jax import lax
from jax.experimental import pallas as pl
from jax.experimental.pallas import tpu as pltpu
from jax.sharding import PartitionSpec as P

HEAD = 64
EPSILON = 1e-05
NEGATIVE = -1000000000.0
HIGHEST = lax.Precision.HIGHEST
LOW = jnp.bfloat16
WIDE = jnp.float32
QB = 128
BAND = 256
KB = QB + BAND
PREP = 16


def swap(block, axis):
    return lax.ppermute(block, axis, [(0, 1), (1, 0)])


def all_sum(block, axes):
    for axis in axes:
        count = lax.axis_size(axis)
        if count & (count - 1):
            block = lax.psum(block, axis)
            continue
        bit = 1
        while bit < count:
            block = block + lax.ppermute(block, axis, [(i, i ^ bit) for i in range(count)])
            bit *= 2
    return block


def layer_norm(values, gain, shift):
    centre = values - jnp.mean(values, axis=-1, keepdims=True)
    spread = jnp.mean(centre * centre, axis=-1, keepdims=True)
    return centre * lax.rsqrt(spread + EPSILON) * gain + shift


def norm_back(values, gain, grad):
    centre = values - jnp.mean(values, axis=-1, keepdims=True)
    inverse = lax.rsqrt(jnp.mean(centre * centre, axis=-1, keepdims=True) + EPSILON)
    normal = centre * inverse
    scaled = grad * gain
    return inverse * (
        scaled
        - jnp.mean(scaled, axis=-1, keepdims=True)
        - normal * jnp.mean(scaled * normal, axis=-1, keepdims=True)
    )


def gelu_parts(values):
    root = 0.7978845608028654
    square = values * values
    inner = jnp.tanh(root * values * (1.0 + 0.044715 * square))
    half = 0.5 * (1.0 + inner)
    slope = half + 0.5 * values * (1.0 - inner * inner) * root * (1.0 + 3 * 0.044715 * square)
    return values * half, slope


def dot_nn(left, right):
    return jnp.dot(left, right, preferred_element_type=WIDE)


def dot_nt(left, right):
    return lax.dot_general(left, right, (((1,), (1,)), ((), ())), preferred_element_type=WIDE)


class ShardCopies:
    def __init__(self, plan, layer, rows, place_ref, buffers, out_ref, stage, sems, out_sems):
        self.plan, self.layer, self.rows, self.buffers = plan, layer, rows, buffers
        self.section, self.z, self.x = place_ref[0], place_ref[1], place_ref[2]
        self.out_ref, self.stage, self.sems, self.out_sems = out_ref, stage, sems, out_sems

    def inward(self, index, source):
        buffer, block = source
        piece = self.buffers[buffer].at[block * self.rows : (block + 1) * self.rows]
        return pltpu.make_async_copy(piece, self.stage.at[index], self.sems.at[index])

    def outward(self, index):
        steps, over_x = self.plan[index][:2]
        slot = ((self.z + 4 - steps) % 4) * 2 + (self.x + over_x) % 2
        return pltpu.make_async_copy(self.stage.at[index], self.out_ref.at[slot], self.out_sems.at[index])

    def fetch(self, indices):
        @pl.when(self.section == self.layer)
        def _():
            for index in indices:
                self.inward(index, self.plan[index][2]).start()

        @pl.when(self.section != self.layer)
        def _():
            for index in indices:
                self.inward(index, self.plan[index][3]).start()

    def deliver(self, index):
        self.inward(index, self.plan[index][2]).wait()
        self.outward(index).start()

    def finish(self):
        for index in range(len(self.plan)):
            self.outward(index).wait()


def split(refs, counts):
    groups = []
    for count in counts:
        groups.append(refs[:count])
        refs = refs[count:]
    return groups, refs


def stacked(pair):
    lane = lax.broadcasted_iota(jnp.int32, pair.shape, 1)
    zero = jnp.zeros_like(pair)
    return jnp.concatenate(
        [jnp.where(lane < HEAD, pair, zero), jnp.where(lane >= HEAD, pair, zero)], axis=0
    )


def unstacked(both):
    lane = lax.broadcasted_iota(jnp.int32, (QB, 2 * HEAD), 1)
    return jnp.where(lane < HEAD, both[:QB], both[QB:])


def dot_tn(left, right):
    return lax.dot_general(left, right, (((0,), (0,)), ((), ())), preferred_element_type=WIDE)


def lower():
    row = lax.broadcasted_iota(jnp.int32, (QB, 2 * QB), 0)
    lane = lax.broadcasted_iota(jnp.int32, (QB, 2 * QB), 1)
    return row <= jnp.where(lane < QB, lane, lane - QB)


def fold(band, near):
    return jnp.concatenate([jnp.where(near, band[BAND:], band[:QB]), band[QB:BAND]], axis=0)


def unfold(folded, near):
    zero = jnp.zeros((QB, 2 * QB), folded.dtype)
    edge = folded[:QB]
    return jnp.concatenate(
        [jnp.where(near, zero, edge), folded[QB:], jnp.where(near, edge, zero)], axis=0
    )


def fill_places(places):
    row = lax.broadcasted_iota(jnp.int32, (QB, 2 * QB), 0)
    places[:QB] = jnp.where(lower(), row + BAND, row)
    places[QB:] = row + QB


def fill_keys(scratch, prefix_ref, halo_ref, own_ref):
    scratch[:PREP] = prefix_ref[...]
    scratch[PREP : PREP + BAND] = halo_ref[...]
    scratch[PREP + BAND :] = own_ref[...]


def masked_scores(queries, keys, start_ref, block, pref_count, places, near):
    pre = dot_nt(keys[:PREP], queries)
    pre = jnp.where(
        lax.broadcasted_iota(jnp.int32, pre.shape, 0) < pref_count, pre, NEGATIVE
    )
    band = fold(dot_nt(keys[pl.ds(PREP + block * QB, KB)], queries), near)
    first = start_ref[:, block * QB : (block + 1) * QB] - block * QB
    first = jnp.concatenate([first, first], axis=1)
    return pre, jnp.where(places[...] >= first, band, NEGATIVE)


def attend_kernel(pref_count, layer, plans, *refs):
    q_ref, k_ref, v_ref, hk_ref, hv_ref, pk_ref, pv_ref, start_ref, place_ref, *refs = refs
    buffers, refs = split(refs, [names for names, *_ in plans])
    c_ref, probs_ref, *refs = refs
    wholes, (keys, vals, places, *refs) = refs[: len(plans)], refs[len(plans) :]
    copies = [
        ShardCopies(plan, layer, rows, place_ref, mine, whole_ref, *refs[3 * i : 3 * i + 3])
        for i, ((_, plan, rows, _), mine, whole_ref) in enumerate(zip(plans, buffers, wholes))
    ]
    pair, pairs = pl.program_id(0), pl.num_programs(0)

    for index in range(8):

        @pl.when(pair == index)
        def _(index=index):
            for copy in copies:
                if index:
                    copy.deliver(index - 1)
                copy.fetch([index])

    fill_keys(keys, pk_ref, hk_ref, k_ref)
    fill_keys(vals, pv_ref, hv_ref, v_ref)
    fill_places(places)
    near = lower()
    for block in range(q_ref.shape[0] // QB):
        span = slice(block * QB, (block + 1) * QB)
        seen = pl.ds(PREP + block * QB, KB)
        queries = stacked(q_ref[span, :] * jnp.asarray(HEAD ** (-0.5), LOW))
        pre, band = masked_scores(queries, keys, start_ref, block, pref_count, places, near)
        top = jnp.maximum(jnp.max(pre, axis=0, keepdims=True), jnp.max(band, axis=0, keepdims=True))
        pre = jnp.exp(pre - top)
        band = jnp.exp(band - top)
        total = jnp.sum(pre, axis=0, keepdims=True) + jnp.sum(band, axis=0, keepdims=True)
        inverse = 1.0 / total
        probs = jnp.concatenate([pre * inverse, unfold(band * inverse, near)], axis=0).astype(LOW)
        probs_ref[0, block] = probs
        out = dot_tn(probs, jnp.concatenate([vals[:PREP], vals[seen]], axis=0))
        c_ref[span, :] = unstacked(out).astype(LOW)

    @pl.when(pair == pairs - 1)
    def _():
        for copy in copies:
            copy.deliver(7)
            copy.finish()


def attend_back_kernel(q_ref, k_ref, v_ref, hk_ref, hv_ref, pk_ref, pv_ref, probs_ref, dc_ref,
                       dq_ref, dk_ref, dv_ref, edge_ref, prefix_ref, keys, vals, dkeys, dvals):
    fill_keys(keys, pk_ref, hk_ref, k_ref)
    fill_keys(vals, pv_ref, hv_ref, v_ref)
    dkeys[...] = jnp.zeros_like(dkeys)
    dvals[...] = jnp.zeros_like(dvals)
    scaling = HEAD ** (-0.5)
    for block in range(q_ref.shape[0] // QB):
        span = slice(block * QB, (block + 1) * QB)
        seen = pl.ds(PREP + block * QB, KB)
        queries = stacked(q_ref[span, :] * jnp.asarray(scaling, LOW))
        grads = stacked(dc_ref[span, :])
        low = probs_ref[0, block]
        probs = low.astype(WIDE)
        dprobs = dot_nt(jnp.concatenate([vals[:PREP], vals[seen]], axis=0), grads)
        inside = jnp.sum(probs * dprobs, axis=0, keepdims=True)
        slope = (probs * (dprobs - inside)).astype(LOW)
        terms = dot_nn(low, grads)
        dvals[:PREP] += terms[:PREP]
        dvals[seen] += terms[PREP:]
        terms = dot_nn(slope, queries)
        dkeys[:PREP] += terms[:PREP]
        dkeys[seen] += terms[PREP:]
        out = dot_tn(slope, jnp.concatenate([keys[:PREP], keys[seen]], axis=0))
        dq_ref[span, :] = (unstacked(out) * scaling).astype(LOW)
    dk_ref[...] = dkeys[PREP + BAND :].astype(LOW)
    dv_ref[...] = dvals[PREP + BAND :].astype(LOW)
    edge_ref[:BAND] = dkeys[PREP : PREP + BAND].astype(LOW)
    edge_ref[BAND:] = dvals[PREP : PREP + BAND].astype(LOW)
    prefix_ref[:PREP] = dkeys[:PREP]
    prefix_ref[PREP:] = dvals[:PREP]


def column(rows, place=lambda half, pair: 0, per=0):
    if per == 0:
        return pl.BlockSpec((rows, 2 * HEAD), lambda i: (0, i))
    return pl.BlockSpec((rows, 2 * HEAD), lambda i: (0, place(i // per) + i % per))


def attention_specs(tokens, per):
    return [
        column(tokens, lambda half: 3 * per * half, per),
        column(tokens, lambda half: 3 * per * half + per, per),
        column(tokens, lambda half: 3 * per * half + 2 * per, per),
        column(BAND, lambda half: 2 * per * (1 - half), per),
        column(BAND, lambda half: 2 * per * (1 - half) + per, per),
        column(PREP, lambda half: 2 * per * half, per),
        column(PREP, lambda half: 2 * per * half + per, per),
    ]


def probs_spec(blocks):
    return pl.BlockSpec((1, blocks, PREP + KB, 2 * QB), lambda i: (i, 0, 0, 0))


def attend(pref_count, qkv, halo, prefix, start, place, layer=0, chores=()):
    tokens, width = qkv.shape[0], qkv.shape[1] // 3
    pairs, blocks = width // (2 * HEAD), tokens // QB
    chores = chores if pairs == 8 else ()
    anywhere = pl.BlockSpec(memory_space=pl.ANY)
    stages = []
    for _, _, rows, columns in chores:
        stages += [
            pltpu.VMEM((8, rows, columns), LOW),
            pltpu.SemaphoreType.DMA((8,)),
            pltpu.SemaphoreType.DMA((8,)),
        ]
    operands = [buffer for buffers, *_ in chores for buffer in buffers]
    return pl.pallas_call(
        functools.partial(
            attend_kernel, pref_count, layer, [(len(chore[0]), *chore[1:]) for chore in chores]
        ),
        grid=(pairs,),
        in_specs=attention_specs(tokens, pairs // 2)
        + [pl.BlockSpec((1, tokens), lambda i: (0, 0)), pl.BlockSpec(memory_space=pltpu.SMEM)]
        + [anywhere] * len(operands),
        out_specs=[column(tokens), probs_spec(blocks)] + [anywhere] * len(chores),
        out_shape=[
            jax.ShapeDtypeStruct((tokens, width), LOW),
            jax.ShapeDtypeStruct((pairs, blocks, PREP + KB, 2 * QB), LOW),
        ]
        + [jax.ShapeDtypeStruct((8, rows, columns), LOW) for _, _, rows, columns in chores],
        scratch_shapes=[
            pltpu.VMEM((PREP + BAND + tokens, 2 * HEAD), LOW),
            pltpu.VMEM((PREP + BAND + tokens, 2 * HEAD), LOW),
            pltpu.VMEM((2 * QB, 2 * QB), jnp.int32),
            *stages,
        ],
        name="attend",
        compiler_params=pltpu.CompilerParams(vmem_limit_bytes=56 * 2**20),
        cost_estimate=pl.CostEstimate(flops=12 * 10**9, bytes_accessed=2 * qkv.size, transcendentals=0),
    )(qkv, qkv, qkv, halo, halo, prefix, prefix, start, place, *operands)


def attend_back(qkv, halo, prefix, probs, grad):
    tokens, width = qkv.shape[0], qkv.shape[1] // 3
    pairs, blocks = width // (2 * HEAD), tokens // QB
    keys = PREP + BAND + tokens
    sizes = [(tokens, LOW)] * 3 + [(2 * BAND, LOW), (2 * PREP, WIDE)]
    return pl.pallas_call(
        attend_back_kernel,
        grid=(pairs,),
        in_specs=attention_specs(tokens, pairs // 2) + [probs_spec(blocks), column(tokens)],
        out_specs=[column(rows) for rows, _ in sizes],
        out_shape=[jax.ShapeDtypeStruct((rows, width), kind) for rows, kind in sizes],
        scratch_shapes=[
            pltpu.VMEM((keys, 2 * HEAD), LOW),
            pltpu.VMEM((keys, 2 * HEAD), LOW),
            pltpu.VMEM((keys, 2 * HEAD), WIDE),
            pltpu.VMEM((keys, 2 * HEAD), WIDE),
        ],
        name="attend_back",
        cost_estimate=pl.CostEstimate(flops=16 * 10**9, bytes_accessed=4 * qkv.size, transcendentals=0),
    )(qkv, qkv, qkv, halo, halo, prefix, prefix, probs, grad)


CHUNK = 512
ROWS = 512


def by_rows(total, body):
    step = min(ROWS, total)

    @pl.loop(0, total // step)
    def _(index):
        body(pl.ds(pl.multiple_of(index * step, step), step))


def of_half(step, count, own_ref, far_ref, body):
    @pl.when(step < count)
    def _():
        body(own_ref)

    @pl.when(step >= count)
    def _():
        body(far_ref)


def halves(shape, count, across):
    def spec(place):
        return pl.BlockSpec(shape, lambda j: (0, place(j)) if across else (place(j), 0))

    return [spec(lambda j: jnp.minimum(j, count - 1)), spec(lambda j: jnp.maximum(j - count, 0))]


def whole(shape):
    return pl.BlockSpec(shape, lambda j: (0,) * len(shape))


def slab(index, tokens, width, part=0):
    return pl.BlockSpec((None, tokens, width), lambda j: (index, part, 0))


def call(kernel, grid, in_specs, out_specs, out_shape, scratch, name, flops, operands, buffer=None):
    size, count = sum(o.size * o.dtype.itemsize for o in operands), len(operands)
    body, aliases = kernel, {}
    if buffer is not None:
        in_specs, operands = in_specs + [pl.BlockSpec(memory_space=pl.ANY)], (*operands, buffer)
        aliases = {count: 0}

        def body(*refs):
            kernel(*refs[:count], *refs[count + 1 :])

    return pl.pallas_call(
        body,
        grid=(grid,),
        in_specs=in_specs,
        out_specs=out_specs,
        out_shape=out_shape,
        input_output_aliases=aliases,
        scratch_shapes=scratch,
        name=name,
        compiler_params=pltpu.CompilerParams(vmem_limit_bytes=56 * 2**20),
        cost_estimate=pl.CostEstimate(flops=flops, bytes_accessed=size, transcendentals=0),
    )(*operands)


def qkv_kernel(x_ref, gain_ref, shift_ref, own_ref, far_ref, bias_ref, out_ref, halo_ref, normed):
    step = pl.program_id(0)

    @pl.when(step == 0)
    def _():
        def body(span):
            normed[span] = layer_norm(
                x_ref[span].astype(WIDE), gain_ref[...], shift_ref[...]
            ).astype(LOW)

        by_rows(x_ref.shape[0], body)

    def body(weight_ref):
        third = weight_ref.shape[1] // 3
        for part in range(3):
            span = slice(part * third, (part + 1) * third)
            out = (dot_nn(normed[...], weight_ref[:, span]) + bias_ref[:, span]).astype(LOW)
            out_ref[:, span] = out
            if part:
                halo_ref[:, (part - 1) * third : part * third] = out[out.shape[0] - BAND :]

    of_half(step, 1, own_ref, far_ref, body)


def qkv_forward(x, gain, shift, weights, bias):
    tokens, width = x.shape
    half = weights[0].shape[1] // 3
    return call(
        qkv_kernel,
        2,
        [whole(x.shape), whole((1, width)), whole((1, width))]
        + halves((width, 3 * half), 1, True)
        + [pl.BlockSpec((1, 3 * half), lambda j: (0, j))],
        [
            pl.BlockSpec((tokens, 3 * half), lambda j: (0, j)),
            pl.BlockSpec((BAND, 2 * half), lambda j: (0, j)),
        ],
        [
            jax.ShapeDtypeStruct((tokens, 6 * half), LOW),
            jax.ShapeDtypeStruct((BAND, 4 * half), LOW),
        ],
        [pltpu.VMEM(x.shape, LOW)],
        "qkv",
        12 * tokens * width * half,
        (x, gain, shift, *weights, bias),
    )


def mlp_kernel(count, x_ref, c_ref, po_ref, pf_ref, b0_ref, gain_ref, shift_ref, fo_ref, ff_ref, bias_ref, wo_ref,
               wf_ref, b1_ref, y_ref, h_ref, slope_ref, low_ref, normed):
    step = pl.program_id(0)
    half = po_ref.shape[0]

    @pl.when(step == 0)
    def _():
        def body(span):
            h = x_ref[span].astype(WIDE) + (
                dot_nn(c_ref[span, :half], po_ref[...])
                + dot_nn(c_ref[span, half:], pf_ref[...])
                + b0_ref[...]
            )
            h_ref[span] = h
            normed[span] = layer_norm(h, gain_ref[...], shift_ref[...]).astype(LOW)
            y_ref[span] = h + b1_ref[...]

        by_rows(x_ref.shape[0], body)

    def half_body(up_ref, down_ref):
        def body(span):
            active, slope = gelu_parts(dot_nn(normed[span], up_ref[...]) + bias_ref[...])
            slope_ref[span] = slope.astype(LOW)
            y_ref[span] += dot_nn(active.astype(LOW), down_ref[...])

        by_rows(x_ref.shape[0], body)

    of_half(step, count, (fo_ref, wo_ref), (ff_ref, wf_ref), lambda refs: half_body(*refs))

    @pl.when(step == 2 * count - 1)
    def _():
        low_ref[...] = y_ref[...].astype(LOW)


def mlp_forward(x, c, weights, biases, gain, shift, fc_bias):
    tokens, width = x.shape
    half, count = width // 2, weights["fc"][0].shape[1] // CHUNK
    row = whole((1, width))
    return call(
        functools.partial(mlp_kernel, count),
        2 * count,
        [whole(x.shape), whole(c.shape), whole((half, width)), whole((half, width)), row, row, row]
        + halves((width, CHUNK), count, True)
        + [pl.BlockSpec((1, CHUNK), lambda j: (0, j))]
        + halves((CHUNK, width), count, False)
        + [row],
        [
            slab(0, tokens, width),
            whole(x.shape),
            pl.BlockSpec((tokens, CHUNK), lambda j: (0, j)),
            whole(x.shape),
        ],
        [
            jax.ShapeDtypeStruct((2, tokens, width), WIDE),
            jax.ShapeDtypeStruct(x.shape, WIDE),
            jax.ShapeDtypeStruct((tokens, 2 * count * CHUNK), LOW),
            jax.ShapeDtypeStruct(x.shape, LOW),
        ],
        [pltpu.VMEM(x.shape, LOW)],
        "mlp",
        2 * tokens * width * (width + 4 * count * CHUNK),
        (x, c, *weights["proj"], biases[0], gain, shift, *weights["fc"], fc_bias, *weights["fc2"], biases[1]),
    )


def mlp_back_kernel(count, dy_ref, h_ref, gain_ref, slope_ref, wo_ref, wf_ref, fo_ref, ff_ref, po_ref, pf_ref,
                    dh_ref, dc_ref, total):
    step = pl.program_id(0)
    half = po_ref.shape[0]

    def half_body(first, up_ref, down_ref):
        def body(span):
            du = (dot_nt(dy_ref[span], down_ref[...]) * slope_ref[span].astype(WIDE)).astype(LOW)
            dm = dot_nt(du, up_ref[...])
            total[span] = dm if first else total[span] + dm

        by_rows(dy_ref.shape[0], body)

    @pl.when(step == 0)
    def _():
        half_body(True, fo_ref, wo_ref)

    @pl.when((step > 0) & (step < count))
    def _():
        half_body(False, fo_ref, wo_ref)

    @pl.when(step >= count)
    def _():
        half_body(False, ff_ref, wf_ref)

    @pl.when(step == 2 * count - 1)
    def _():
        def body(span):
            dh = dy_ref[span].astype(WIDE) + norm_back(h_ref[span], gain_ref[...], total[span])
            dh_ref[span] = dh
            low = dh.astype(LOW)
            dc_ref[span, :half] = dot_nt(low, po_ref[...]).astype(LOW)
            dc_ref[span, half:] = dot_nt(low, pf_ref[...]).astype(LOW)

        by_rows(dy_ref.shape[0], body)


def mlp_back(dy, h, gain, slope, weights):
    tokens, width = dy.shape
    half, count = width // 2, weights["fc"][0].shape[1] // CHUNK
    return call(
        functools.partial(mlp_back_kernel, count),
        2 * count,
        [whole(dy.shape), whole(dy.shape), whole((1, width)), pl.BlockSpec((tokens, CHUNK), lambda j: (0, j))]
        + halves((CHUNK, width), count, False)
        + halves((width, CHUNK), count, True)
        + [whole((half, width)), whole((half, width))],
        [whole(dy.shape), whole(dy.shape)],
        [jax.ShapeDtypeStruct(dy.shape, WIDE), jax.ShapeDtypeStruct(dy.shape, LOW)],
        [pltpu.VMEM(dy.shape, WIDE)],
        "mlp_back",
        2 * tokens * width * (width + 4 * count * CHUNK),
        (dy, h, gain, slope, *weights["fc2"], *weights["fc"], *weights["proj"]),
    )


def mlp_both_kernel(count, x_ref, c_ref, dy_ref, po_ref, pf_ref, b0_ref, gain_ref, shift_ref, fo_ref, ff_ref, bias_ref,
                    wo_ref, wf_ref, b1_ref, y_ref, low_ref, dh_ref, dc_ref, h_ref, normed, total):
    step = pl.program_id(0)
    half = po_ref.shape[0]

    @pl.when(step == 0)
    def _():
        def body(span):
            h = x_ref[span].astype(WIDE) + (
                dot_nn(c_ref[span, :half], po_ref[...])
                + dot_nn(c_ref[span, half:], pf_ref[...])
                + b0_ref[...]
            )
            h_ref[span] = h
            normed[span] = layer_norm(h, gain_ref[...], shift_ref[...]).astype(LOW)
            y_ref[span] = h + b1_ref[...]
            total[span] = jnp.zeros_like(h)

        by_rows(x_ref.shape[0], body)

    def half_body(up_ref, down_ref):
        def body(span):
            active, slope = gelu_parts(dot_nn(normed[span], up_ref[...]) + bias_ref[...])
            du = (dot_nt(dy_ref[span], down_ref[...]) * slope).astype(LOW)
            y_ref[span] += dot_nn(active.astype(LOW), down_ref[...])
            total[span] += dot_nt(du, up_ref[...])

        by_rows(x_ref.shape[0], body)

    of_half(step, count, (fo_ref, wo_ref), (ff_ref, wf_ref), lambda refs: half_body(*refs))

    @pl.when(step == 2 * count - 1)
    def _():
        def body(span):
            low_ref[span] = y_ref[span].astype(LOW)
            dh = dy_ref[span].astype(WIDE) + norm_back(h_ref[span], gain_ref[...], total[span])
            dh_ref[span] = dh
            low = dh.astype(LOW)
            dc_ref[span, :half] = dot_nt(low, po_ref[...]).astype(LOW)
            dc_ref[span, half:] = dot_nt(low, pf_ref[...]).astype(LOW)

        by_rows(x_ref.shape[0], body)


def mlp_both(acts, x, c, dy, weights, biases, gain, shift, fc_bias):
    tokens, width = x.shape
    half, count = width // 2, weights["fc"][0].shape[1] // CHUNK
    row, full = whole((1, width)), whole(x.shape)
    return call(
        functools.partial(mlp_both_kernel, count),
        2 * count,
        [full, full, full, whole((half, width)), whole((half, width)), row, row, row]
        + halves((width, CHUNK), count, True)
        + [pl.BlockSpec((1, CHUNK), lambda j: (0, j))]
        + halves((CHUNK, width), count, False)
        + [row],
        [slab(1, tokens, width), full, full, full],
        [jax.ShapeDtypeStruct(acts.shape, WIDE)]
        + [jax.ShapeDtypeStruct(x.shape, kind) for kind in (LOW, WIDE, LOW)],
        [pltpu.VMEM(x.shape, WIDE), pltpu.VMEM(x.shape, LOW), pltpu.VMEM(x.shape, WIDE)],
        "mlp_both",
        4 * tokens * width * (width + 4 * count * CHUNK),
        (x, c, dy, *weights["proj"], biases[0], gain, shift, *weights["fc"], fc_bias, *weights["fc2"], biases[1]),
        acts,
    )


def qkv_back_kernel(reach, dq_ref, dk_ref, dv_ref, hk_ref, hv_ref, own_ref, far_ref, x_ref, dh_ref, gain_ref, other_ref,
                    section_ref, dx_ref, low_ref, total):
    step = pl.program_id(0)

    def joined_grads(grad_ref, halo_ref):
        grad = grad_ref[...]
        if not reach:
            return grad
        early = grad.shape[0] - reach
        late = (grad[early:].astype(WIDE) + halo_ref[...].astype(WIDE)).astype(LOW)
        return jnp.concatenate([grad[:early], late], axis=0) if early else late

    def half_body(first, weight_ref):
        grads = (dq_ref[...], joined_grads(dk_ref, hk_ref), joined_grads(dv_ref, hv_ref))
        term = dot_nt(jnp.concatenate(grads, axis=1), weight_ref[...])
        total[...] = term if first else total[...] + term

    @pl.when(step == 0)
    def _():
        half_body(True, own_ref)

    @pl.when(step == 1)
    def _():
        half_body(False, far_ref)

        def body(span):
            dx = dh_ref[span] + norm_back(x_ref[span].astype(WIDE), gain_ref[...], total[span])
            dx_ref[span] = dx
            low = dx.astype(LOW)
            low_ref[span] = jnp.where(section_ref[0] == 0, other_ref[span], low)

        by_rows(x_ref.shape[0], body)


def qkv_back(grads, halo, weights, x, dh, gain, other, section, layer, buffer=None, part=0, parts=1):
    width = x.shape[1]
    tokens, half = x.shape[0] // parts, width // 2
    reach = BAND if part == parts - 1 else 0
    piece = pl.BlockSpec((tokens, half), lambda j: (part, j))
    edges = [pl.BlockSpec((BAND, half), lambda j, i=i: (i, 1 - j)) for i in range(2)]
    mine, shape = pl.BlockSpec((tokens, width), lambda j: (part, 0)), (tokens, width)
    return call(
        functools.partial(qkv_back_kernel, reach),
        2,
        [piece, piece, piece, *edges]
        + halves((width, 3 * half), 1, True)
        + [mine, mine, whole((1, width)), mine, pl.BlockSpec(memory_space=pltpu.SMEM)],
        [slab(layer, tokens, width, part), whole(shape)],
        [jax.ShapeDtypeStruct((2, *x.shape), WIDE), jax.ShapeDtypeStruct(shape, LOW)],
        [pltpu.VMEM(shape, WIDE)],
        "qkv_back",
        12 * tokens * width * half,
        (*grads, halo, halo, *weights, x, dh, gain, other, section),
        buffer,
    )


def take_kernel(section_ref, got_ref, held_ref, out_ref):
    out_ref[0] = got_ref[...].astype(WIDE)


def take(section, got, buffer, start=0):
    rows, width = got.shape
    step = min(256, rows)
    base = start // step
    return pl.pallas_call(
        take_kernel,
        grid_spec=pltpu.PrefetchScalarGridSpec(
            num_scalar_prefetch=1,
            grid=(rows // step,),
            in_specs=[
                pl.BlockSpec((step, width), lambda i, s: (i, 0)),
                pl.BlockSpec(memory_space=pl.ANY),
            ],
            out_specs=pl.BlockSpec((1, step, width), lambda i, s: (1 - s[0], base + i, 0)),
        ),
        out_shape=jax.ShapeDtypeStruct(buffer.shape, WIDE),
        input_output_aliases={2: 0},
        name="take",
        cost_estimate=pl.CostEstimate(flops=0, bytes_accessed=6 * got.size, transcendentals=0),
    )(section, got, buffer)


NAMES = ("qkv", "proj", "fc", "fc2")
JOIN, QKV, ATTEND, MLP = range(4)
BESIDE = (0, 1, 2, 3)
ORDER = (
    (1, 0, 0, 0, 0), (0, 0, 0, 0, 0), (2, 0, 0, 0, 0), (1, 1, 0, 0, 0), (0, 2, 0, 0, 0),
    (1, 3, 0, 0, 0), (2, 2, 0, 0, 0), (1, 0, 0, 1, 0), (0, 8, 0, 0, 0), (0, 0, 1, 0, 0),
    (1, 2, 0, 1, 0), (2, 2, 1, 0, 0), (0, 2, 1, 0, 0), (1, 0, 1, 0, 0), (2, 9, 0, 0, 0),
    (0, 2, 2, 0, 0), (1, 0, 1, 1, 0), (2, 6, 0, 0, 0), (2, 9, 1, 0, 0), (1, 2, 1, 0, 0),
    (0, 7, 0, 0, 0), (1, 2, 1, 1, 0), (2, 0, 1, 0, 0), (1, 2, 2, 0, 0), (0, 6, 0, 0, 0),
    (2, 9, 2, 0, 0), (2, 0, 2, 0, 0), (0, 0, 2, 0, 0), (1, 0, 2, 0, 0), (2, 2, 2, 0, 0),
    (1, 2, 0, 0, 0), (0, 6, 1, 0, 0), (0, 0, 3, 0, 0), (1, 0, 3, 0, 0), (2, 7, 0, 0, 0),
    (0, 2, 3, 0, 0), (1, 0, 2, 1, 0), (2, 6, 1, 0, 0), (1, 0, 3, 1, 0), (0, 7, 1, 0, 0),
    (2, 7, 1, 0, 0), (1, 2, 3, 0, 0), (0, 6, 2, 0, 0), (1, 2, 2, 1, 0), (2, 6, 2, 0, 0),
    (0, 7, 2, 0, 0), (1, 2, 3, 1, 0), (2, 7, 2, 0, 0), (0, 6, 3, 0, 0), (0, 7, 3, 0, 0),
    (3, 0, 0, 0, 0), (3, 0, 1, 0, 0), (3, 0, 2, 0, 0), (3, 0, 3, 0, 0), (3, 0, 0, 1, 0),
    (3, 0, 1, 1, 0), (3, 0, 2, 1, 0), (3, 0, 3, 1, 0), (3, 1, 0, 0, 0), (3, 2, 0, 0, 0),
    (3, 3, 0, 0, 0), (3, 1, 0, 1, 0), (3, 2, 0, 1, 0), (3, 3, 0, 1, 0),
)
JOINED = {8: ((1, 0, 0, 0), (1, 0, 0, 1)), 9: ((8, 0, 0, 0), (8, 0, 1, 0))}
DEEP = 2
LATE = 3


def move(block, link):
    if link == 1:
        return swap(block, "section")
    count = lax.axis_size("rows")
    if link == 0:
        return lax.ppermute(block, "rows", [(i, i ^ 1) for i in range(count)])
    return lax.ppermute(block, "rows", [(i, (i + 2) % count) for i in range(count)])


def spread(shards, section, run):
    held = {(base, 0, 0, 0): shards[name] for base, name in enumerate(NAMES)}
    sent, passed, awaited = {}, [], []

    def get(key):
        if key not in held:
            base = key[0]
            if base in JOINED:
                held[key] = jnp.concatenate([get(part) for part in JOINED[base]], axis=0)
            else:
                raw = base // 2
                held[key] = jnp.where(section == base % 2, get((raw, 0, 0, 0)), get((raw, 0, 0, 1)))
        return held[key]

    for link, *key in ORDER:
        if link == 3:
            now, later = run(*key[:3], get)
            passed = [now] if now is not None else passed
            if later is not None:
                awaited.append([LATE, later])
            continue
        block, ahead = get(tuple(key)), sent.setdefault(link, [])
        behind = list(passed)
        if len(ahead) >= DEEP:
            behind.append(ahead[-DEEP])
        for entry in awaited:
            entry[0] -= 1
            if entry[0] == 0:
                behind.append(entry[1])
        if behind:
            block, *_ = lax.optimization_barrier((block, *behind))
        base, steps, over_x, over_y = key
        target = (base, steps + (link == 2), over_x + (link == 0), over_y + (link == 1))
        held[target] = move(block, link)
        ahead.append(held[target])


def pieces(matrix, layer, resolved):
    result = []
    for steps in range(4):
        for over_x in range(2):
            if matrix == 1:
                key = (9, steps, 0, 0)
                near, away = (key, 2 * over_x), (key, 2 * over_x + 1)
            elif resolved:
                near = away = ((2 * matrix + layer, steps, over_x, 0), 0)
            else:
                near, away = ((matrix, steps, over_x, 0), 0), ((matrix, steps, over_x, 1), 0)
            result.append((steps, over_x, near, away))
    return result


def join_kernel(plan, layer, rows, place_ref, *refs):
    copies = ShardCopies(plan, layer, rows, place_ref, refs[:-4], *refs[-4:])
    copies.fetch(range(8))
    for index in range(8):
        copies.deliver(index)
    copies.finish()


def plan_of(matrix, layer, get):
    keys, plan = [], []
    resolved = any(link < 3 and base == 2 * matrix for link, base, *_ in ORDER if matrix > 1)
    for steps, over_x, *sources in pieces(matrix, layer, resolved):
        spots = []
        for key, block in sources:
            if key not in keys:
                keys.append(key)
            spots.append((keys.index(key), block))
        plan.append((steps, over_x, *spots))
    return [get(key) for key in keys], plan


def joined(matrix, layer, get, shape, place):
    rows, columns = shape
    buffers, plan = plan_of(matrix, layer, get)
    anywhere = pl.BlockSpec(memory_space=pl.ANY)
    whole = pl.pallas_call(
        functools.partial(join_kernel, plan, layer, rows),
        in_specs=[pl.BlockSpec(memory_space=pltpu.SMEM)] + [anywhere] * len(buffers),
        out_specs=anywhere,
        out_shape=jax.ShapeDtypeStruct((8, rows, columns), LOW),
        scratch_shapes=[
            pltpu.VMEM((8, rows, columns), LOW),
            pltpu.SemaphoreType.DMA((8,)),
            pltpu.SemaphoreType.DMA((8,)),
        ],
        name="join",
        cost_estimate=pl.CostEstimate(flops=0, bytes_accessed=4 * 8 * rows * columns, transcendentals=0),
    )(place, *buffers)
    return whole.reshape(8 * rows, columns)


def forward(shards, x, dy, start, smalls, pref_count):
    section, rows = lax.axis_index("section"), lax.axis_index("rows")
    weights, kept, outputs, slopes = [{}, {}], [None, None], [None, None], []

    def run(kind, matrix, layer, get):
        small, mine = smalls[layer], weights[layer]
        place = jnp.stack([section, rows // 2, rows % 2]).astype(jnp.int32)
        if kind == JOIN:
            name = NAMES[matrix]
            if layer and matrix in BESIDE:
                return None, None
            near = joined(matrix, layer, get, shards[name].shape, place)
            mine[name] = (near, swap(near, "tensor"))
            return mine[name]
        if kind == QKV:
            source = outputs[0][1] if layer else x
            qkv, edge = qkv_forward(source, small["gain"][0:1], small["shift"][0:1], mine["qkv"], small["qkv"])
            kept[layer] = (source, qkv, lax.ppermute(edge, "tensor", [(0, 1)]))
            return qkv, kept[layer][2]
        if kind == ATTEND:
            source, qkv, halo = kept[layer]
            chores = []
            if get is not None and not layer:
                chores = [(*plan_of(other, 1, get), *shards[NAMES[other]].shape) for other in BESIDE]
            ahead = start
            if chores:
                ahead, _ = lax.optimization_barrier((start, mine["proj"][1]))
            c, probs, *wholes = attend(pref_count, qkv, halo, small["prefix"], ahead, place, 1, chores)
            for name, near in zip([NAMES[other] for other in BESIDE], wholes):
                near = near.reshape(-1, near.shape[-1])
                weights[1][name] = (near, swap(near, "tensor"))
            kept[layer] = (source, qkv, halo, probs, c)
            return c, None
        source, qkv, halo, probs, c = kept[layer]
        kept[layer] = (source, qkv, halo, probs)
        biases = (small["out"][0:1], small["out"][1:2])
        norm = (small["gain"][1:2], small["shift"][1:2])
        if layer:
            *outputs[1], dh, dc = mlp_both(outputs[0][0], source, c, dy, mine, biases, *norm, small["fc"])
            slopes.extend((dh, dc))
        else:
            acts, h, slope, low = mlp_forward(source, c, mine, biases, *norm, small["fc"])
            outputs[0] = (acts, low)
            slopes.extend((h, slope))
        return slopes[-1], None

    if lax.axis_size("rows") == 8:
        spread(shards, section, run)
    else:
        for name in NAMES:
            near = lax.all_gather(shards[name], ("section", "rows"), axis=0, tiled=True)
            near = near.reshape(2, -1, near.shape[1])
            far = swap(near, "tensor")
            for layer in range(2):
                weights[layer][name] = (near[layer], far[layer])
        for link, *stage in ORDER:
            if link == 3 and stage[0] != JOIN:
                run(*stage[:3], None)
    return weights, kept, outputs, slopes


def on_device(
    tokens,
    segment_ids,
    cotangent,
    ln_gain,
    ln_bias,
    w_qkv,
    query_key_value_bias,
    w_proj,
    w_fc,
    fc_bias,
    w_fc2,
    out_bias,
    prefix_embed,
    rep_w1,
    rep_b1,
    rep_w2,
    rep_b2,
):
    share, width = tokens.shape[1:]
    section, core = lax.axis_index("section"), lax.axis_index("tensor")
    rows_index, rows = lax.axis_index("rows"), lax.axis_size("rows")
    half = rep_w2.shape[-1]
    pref_count = prefix_embed.shape[0]

    shards = {
        "qkv": w_qkv[0].astype(LOW).reshape(w_qkv.shape[1], -1),
        "proj": w_proj[0].astype(LOW),
        "fc": w_fc[0].astype(LOW),
        "fc2": w_fc2[0].astype(LOW),
    }
    rep_hidden = jnp.tanh(jnp.dot(prefix_embed, rep_w1, precision=HIGHEST) + rep_b1)
    prefix = jnp.einsum("pm,mcd->pcd", rep_hidden, rep_w2[:, 0], precision=HIGHEST) + rep_b2[0]
    prefix = prefix.astype(LOW).astype(WIDE)
    prefix = jnp.pad(prefix, ((0, PREP - pref_count), (0, 0), (0, 0)))
    parts = [ln_gain[0], ln_bias[0], out_bias[0], query_key_value_bias[0], fc_bias[0], prefix]
    packed = jnp.concatenate([part.reshape(-1) for part in parts])
    near = jnp.stack([packed, swap(packed, "tensor")])
    away = swap(near, "section")
    smalls = []
    for layer in range(2):
        cut, place = [], 0
        chosen = jnp.where(section == layer, near, away)
        for part in parts:
            cut.append([chosen[h, place : place + part.size].reshape(part.shape) for h in range(2)])
            place += part.size
        smalls.append(
            {
                "gain": cut[0][0],
                "shift": cut[1][0],
                "out": cut[2][0],
                "qkv": jnp.concatenate([cut[3][h].reshape(1, -1) for h in range(2)], axis=1),
                "fc": jnp.concatenate([cut[4][h].reshape(1, -1) for h in range(2)], axis=1),
                "prefix": jnp.concatenate(
                    [cut[5][h].reshape(PREP, -1).astype(LOW) for h in range(2)], axis=1
                ),
            }
        )

    own = section
    segments = lax.dynamic_index_in_dim(segment_ids, own, 0, keepdims=False).reshape(-1)
    mine = lax.dynamic_slice_in_dim(segments, core * share, share)
    start = jnp.sum(segments[:, None] < mine[None, :], axis=0, dtype=jnp.int32)
    start = (start - core * share + BAND)[None]

    x = lax.dynamic_index_in_dim(tokens, own, 0, keepdims=False)
    dy = lax.dynamic_index_in_dim(cotangent, own, 0, keepdims=False)
    x, dy = lax.optimization_barrier((x, dy))
    weights, (kept0, kept1), ((_, low0), (acts, low1)), (h, slope, dh, dc) = forward(
        shards, x, dy, start, smalls, pref_count
    )
    dy = lax.dynamic_index_in_dim(cotangent, own, 0, keepdims=False)
    got_acts = swap(jnp.where(section == 0, low1, low0), "section")
    where_at = section.astype(jnp.int32).reshape(1)
    nowhere = jnp.ones((1,), jnp.int32)

    x1, qkv, halo, probs = kept1
    *grads, edge, pre1 = attend_back(qkv, halo, smalls[1]["prefix"], probs, dc)
    edge = lax.ppermute(edge, "tensor", [(1, 0)])
    in_grads, down1 = qkv_back(
        grads, edge, weights[1]["qkv"], x1, dh, smalls[1]["gain"][0:1], low1, nowhere, 1
    )
    dh, dc = mlp_back(down1, h, smalls[0]["gain"][1:2], slope, weights[0])
    got_acts, dc = lax.optimization_barrier((got_acts, dc))
    acts = take(where_at, got_acts, acts)
    x0, qkv, halo, probs = kept0
    *grads, edge, pre0 = attend_back(qkv, halo, smalls[0]["prefix"], probs, dc)
    edge = lax.ppermute(edge, "tensor", [(1, 0)])

    pre0, pre1 = [pre.reshape(2, PREP, 2, half) for pre in (pre0, pre1)]
    near = jnp.where(section == 0, pre0, pre1) + swap(jnp.where(section == 0, pre1, pre0), "section")
    tail = (weights[0]["qkv"], x0)
    gain = smalls[0]["gain"][0:1]
    in_grads, sent = qkv_back(grads, grads[0], *tail, dh, gain, down1, where_at, 0, in_grads, 0, 2)
    got = [swap(sent, "section")]
    near, _ = lax.optimization_barrier((near, sent))
    total = (near[:, :, 0] + swap(near[:, :, 1], "tensor"))[:, :pref_count]
    hidden_term = jnp.einsum("cpd,mcd->pm", total, rep_w2[:, 0], precision=HIGHEST)
    dh, _ = lax.optimization_barrier((dh, hidden_term))
    in_grads, sent = qkv_back(grads, edge, *tail, dh, gain, down1, where_at, 0, in_grads, 1, 2)
    got.append(swap(sent, "section"))
    sums = jnp.concatenate([total.reshape(2 * pref_count, half), hidden_term], axis=0)
    sums, _, _ = lax.optimization_barrier((sums, sent, got[0]))
    sums = all_sum(sums, ("rows",))
    total, hidden_term = sums[: 2 * pref_count].reshape(2, pref_count, half), sums[2 * pref_count :]
    hidden_term, *got = lax.optimization_barrier((hidden_term, *got))
    for part in range(2):
        in_grads = take(where_at, got[part], in_grads, part * share // 2)
    grad_hidden = all_sum(hidden_term, ("section", "tensor"))
    grad_b2 = jnp.sum(total, axis=1)
    mid_part = rep_w1.shape[1] // rows
    width_part = width // rows
    hidden_part = lax.dynamic_slice_in_dim(rep_hidden, rows_index * mid_part, mid_part, 1)
    grad_w2 = jnp.einsum("pm,cpd->mcd", hidden_part, total, precision=HIGHEST)
    grad_pre = grad_hidden * (1.0 - rep_hidden * rep_hidden)
    grad_b1 = jnp.sum(grad_pre, axis=0)
    embed_part = lax.dynamic_slice_in_dim(prefix_embed, rows_index * width_part, width_part, 1)
    grad_w1 = jnp.einsum("pd,pm->dm", embed_part, grad_pre, precision=HIGHEST)
    weight_part = lax.dynamic_slice_in_dim(rep_w1, rows_index * width_part, width_part, 0)
    grad_embed = jnp.einsum("pm,dm->pd", grad_pre, weight_part, precision=HIGHEST)
    return (acts[None], in_grads[None], grad_embed, grad_w1, grad_b1, grad_w2[:, None], grad_b2[None])


def solution(mesh):
    return jax.shard_map(
        on_device,
        mesh=mesh,
        in_specs=(
            P(None, ("rows", "tensor"), None),
            P(None, "rows", None),
            P(None, ("rows", "tensor"), None),
            P("section", None, None),
            P("section", None, None),
            P("section", "rows", None, "tensor"),
            P("section", None, "tensor"),
            P("section", ("tensor", "rows"), None),
            P("section", "rows", "tensor"),
            P("section", "tensor"),
            P("section", ("tensor", "rows"), None),
            P("section", None, None),
            P(),
            P(),
            P(),
            P(None, "section", None, "tensor"),
            P("section", None, "tensor"),
        ),
        out_specs=(
            P("section", None, ("rows", "tensor"), None),
            P("section", None, ("rows", "tensor"), None),
            P(None, "rows"),
            P("rows", None),
            P(),
            P("rows", "section", None, "tensor"),
            P("section", None, "tensor"),
        ),
        check_vma=False,
    )
```

```python
import functools

import jax
import jax.numpy as jnp
from jax import lax
from jax.experimental import pallas as pl
from jax.experimental.pallas import tpu as pltpu
from jax.sharding import PartitionSpec as P

HEAD = 64
EPSILON = 1e-05
NEGATIVE = -1000000000.0
HIGHEST = lax.Precision.HIGHEST
LOW = jnp.bfloat16
WIDE = jnp.float32
QB = 128
BAND = 256
KB = QB + BAND
PREP = 16


def swap(block, axis):
    return lax.ppermute(block, axis, [(0, 1), (1, 0)])


def all_sum(block, axes):
    for axis in axes:
        count = lax.axis_size(axis)
        if count & (count - 1):
            block = lax.psum(block, axis)
            continue
        bit = 1
        while bit < count:
            block = block + lax.ppermute(block, axis, [(i, i ^ bit) for i in range(count)])
            bit *= 2
    return block


def layer_norm(values, gain, shift):
    centre = values - jnp.mean(values, axis=-1, keepdims=True)
    spread = jnp.mean(centre * centre, axis=-1, keepdims=True)
    return centre * lax.rsqrt(spread + EPSILON) * gain + shift


def norm_back(values, gain, grad):
    centre = values - jnp.mean(values, axis=-1, keepdims=True)
    inverse = lax.rsqrt(jnp.mean(centre * centre, axis=-1, keepdims=True) + EPSILON)
    normal = centre * inverse
    scaled = grad * gain
    return inverse * (
        scaled
        - jnp.mean(scaled, axis=-1, keepdims=True)
        - normal * jnp.mean(scaled * normal, axis=-1, keepdims=True)
    )


def gelu_parts(values):
    root = 0.7978845608028654
    square = values * values
    inner = jnp.tanh(root * values * (1.0 + 0.044715 * square))
    half = 0.5 * (1.0 + inner)
    slope = half + 0.5 * values * (1.0 - inner * inner) * root * (1.0 + 3 * 0.044715 * square)
    return values * half, slope


def dot_nn(left, right):
    return jnp.dot(left, right, preferred_element_type=WIDE)


def dot_nt(left, right):
    return lax.dot_general(left, right, (((1,), (1,)), ((), ())), preferred_element_type=WIDE)


class ShardCopies:
    def __init__(self, plan, layer, rows, place_ref, buffers, out_ref, stage, sems, out_sems):
        self.plan, self.layer, self.rows, self.buffers = plan, layer, rows, buffers
        self.section, self.z, self.x = place_ref[0], place_ref[1], place_ref[2]
        self.out_ref, self.stage, self.sems, self.out_sems = out_ref, stage, sems, out_sems

    def inward(self, index, source):
        buffer, block = source
        piece = self.buffers[buffer].at[block * self.rows : (block + 1) * self.rows]
        return pltpu.make_async_copy(piece, self.stage.at[index], self.sems.at[index])

    def outward(self, index):
        steps, over_x = self.plan[index][:2]
        slot = ((self.z + 4 - steps) % 4) * 2 + (self.x + over_x) % 2
        return pltpu.make_async_copy(self.stage.at[index], self.out_ref.at[slot], self.out_sems.at[index])

    def fetch(self, indices):
        @pl.when(self.section == self.layer)
        def _():
            for index in indices:
                self.inward(index, self.plan[index][2]).start()

        @pl.when(self.section != self.layer)
        def _():
            for index in indices:
                self.inward(index, self.plan[index][3]).start()

    def deliver(self, index):
        self.inward(index, self.plan[index][2]).wait()
        self.outward(index).start()

    def finish(self):
        for index in range(len(self.plan)):
            self.outward(index).wait()


def split(refs, counts):
    groups = []
    for count in counts:
        groups.append(refs[:count])
        refs = refs[count:]
    return groups, refs


def stacked(pair):
    lane = lax.broadcasted_iota(jnp.int32, pair.shape, 1)
    zero = jnp.zeros_like(pair)
    return jnp.concatenate(
        [jnp.where(lane < HEAD, pair, zero), jnp.where(lane >= HEAD, pair, zero)], axis=0
    )


def unstacked(both):
    lane = lax.broadcasted_iota(jnp.int32, (QB, 2 * HEAD), 1)
    return jnp.where(lane < HEAD, both[:QB], both[QB:])


def dot_tn(left, right):
    return lax.dot_general(left, right, (((0,), (0,)), ((), ())), preferred_element_type=WIDE)


def lower():
    row = lax.broadcasted_iota(jnp.int32, (QB, 2 * QB), 0)
    lane = lax.broadcasted_iota(jnp.int32, (QB, 2 * QB), 1)
    return row <= jnp.where(lane < QB, lane, lane - QB)


def fold(band, near):
    return jnp.concatenate([jnp.where(near, band[BAND:], band[:QB]), band[QB:BAND]], axis=0)


def unfold(folded, near):
    zero = jnp.zeros((QB, 2 * QB), folded.dtype)
    edge = folded[:QB]
    return jnp.concatenate(
        [jnp.where(near, zero, edge), folded[QB:], jnp.where(near, edge, zero)], axis=0
    )


def fill_places(places):
    row = lax.broadcasted_iota(jnp.int32, (QB, 2 * QB), 0)
    places[:QB] = jnp.where(lower(), row + BAND, row)
    places[QB:] = row + QB


def fill_keys(scratch, prefix_ref, halo_ref, own_ref):
    scratch[:PREP] = prefix_ref[...]
    scratch[PREP : PREP + BAND] = halo_ref[...]
    scratch[PREP + BAND :] = own_ref[...]


def masked_scores(queries, keys, start_ref, block, pref_count, places, near):
    pre = dot_nt(keys[:PREP], queries)
    pre = jnp.where(
        lax.broadcasted_iota(jnp.int32, pre.shape, 0) < pref_count, pre, NEGATIVE
    )
    band = fold(dot_nt(keys[pl.ds(PREP + block * QB, KB)], queries), near)
    first = start_ref[:, block * QB : (block + 1) * QB] - block * QB
    first = jnp.concatenate([first, first], axis=1)
    return pre, jnp.where(places[...] >= first, band, NEGATIVE)


def attend_kernel(pref_count, layer, plans, *refs):
    q_ref, k_ref, v_ref, hk_ref, hv_ref, pk_ref, pv_ref, start_ref, place_ref, *refs = refs
    buffers, refs = split(refs, [names for names, *_ in plans])
    c_ref, probs_ref, *refs = refs
    wholes, (keys, vals, places, *refs) = refs[: len(plans)], refs[len(plans) :]
    copies = [
        ShardCopies(plan, layer, rows, place_ref, mine, whole_ref, *refs[3 * i : 3 * i + 3])
        for i, ((_, plan, rows, _), mine, whole_ref) in enumerate(zip(plans, buffers, wholes))
    ]
    pair, pairs = pl.program_id(0), pl.num_programs(0)

    for index in range(8):

        @pl.when(pair == index)
        def _(index=index):
            for copy in copies:
                if index:
                    copy.deliver(index - 1)
                copy.fetch([index])

    fill_keys(keys, pk_ref, hk_ref, k_ref)
    fill_keys(vals, pv_ref, hv_ref, v_ref)
    fill_places(places)
    near = lower()
    for block in range(q_ref.shape[0] // QB):
        span = slice(block * QB, (block + 1) * QB)
        seen = pl.ds(PREP + block * QB, KB)
        queries = stacked(q_ref[span, :] * jnp.asarray(HEAD ** (-0.5), LOW))
        pre, band = masked_scores(queries, keys, start_ref, block, pref_count, places, near)
        top = jnp.maximum(jnp.max(pre, axis=0, keepdims=True), jnp.max(band, axis=0, keepdims=True))
        pre = jnp.exp(pre - top)
        band = jnp.exp(band - top)
        total = jnp.sum(pre, axis=0, keepdims=True) + jnp.sum(band, axis=0, keepdims=True)
        inverse = 1.0 / total
        probs = jnp.concatenate([pre * inverse, unfold(band * inverse, near)], axis=0).astype(LOW)
        probs_ref[0, block] = probs
        out = dot_tn(probs, jnp.concatenate([vals[:PREP], vals[seen]], axis=0))
        c_ref[span, :] = unstacked(out).astype(LOW)

    @pl.when(pair == pairs - 1)
    def _():
        for copy in copies:
            copy.deliver(7)
            copy.finish()


def attend_back_kernel(q_ref, k_ref, v_ref, hk_ref, hv_ref, pk_ref, pv_ref, probs_ref, dc_ref,
                       dq_ref, dk_ref, dv_ref, edge_ref, prefix_ref, keys, vals, dkeys, dvals):
    fill_keys(keys, pk_ref, hk_ref, k_ref)
    fill_keys(vals, pv_ref, hv_ref, v_ref)
    dkeys[...] = jnp.zeros_like(dkeys)
    dvals[...] = jnp.zeros_like(dvals)
    scaling = HEAD ** (-0.5)
    for block in range(q_ref.shape[0] // QB):
        span = slice(block * QB, (block + 1) * QB)
        seen = pl.ds(PREP + block * QB, KB)
        queries = stacked(q_ref[span, :] * jnp.asarray(scaling, LOW))
        grads = stacked(dc_ref[span, :])
        low = probs_ref[0, block]
        probs = low.astype(WIDE)
        dprobs = dot_nt(jnp.concatenate([vals[:PREP], vals[seen]], axis=0), grads)
        inside = jnp.sum(probs * dprobs, axis=0, keepdims=True)
        slope = (probs * (dprobs - inside)).astype(LOW)
        terms = dot_nn(low, grads)
        dvals[:PREP] += terms[:PREP]
        dvals[seen] += terms[PREP:]
        terms = dot_nn(slope, queries)
        dkeys[:PREP] += terms[:PREP]
        dkeys[seen] += terms[PREP:]
        out = dot_tn(slope, jnp.concatenate([keys[:PREP], keys[seen]], axis=0))
        dq_ref[span, :] = (unstacked(out) * scaling).astype(LOW)
    dk_ref[...] = dkeys[PREP + BAND :].astype(LOW)
    dv_ref[...] = dvals[PREP + BAND :].astype(LOW)
    edge_ref[:BAND] = dkeys[PREP : PREP + BAND].astype(LOW)
    edge_ref[BAND:] = dvals[PREP : PREP + BAND].astype(LOW)
    prefix_ref[:PREP] = dkeys[:PREP]
    prefix_ref[PREP:] = dvals[:PREP]


def column(rows, place=lambda half, pair: 0, per=0):
    if per == 0:
        return pl.BlockSpec((rows, 2 * HEAD), lambda i: (0, i))
    return pl.BlockSpec((rows, 2 * HEAD), lambda i: (0, place(i // per) + i % per))


def attention_specs(tokens, per):
    return [
        column(tokens, lambda half: 3 * per * half, per),
        column(tokens, lambda half: 3 * per * half + per, per),
        column(tokens, lambda half: 3 * per * half + 2 * per, per),
        column(BAND, lambda half: 2 * per * (1 - half), per),
        column(BAND, lambda half: 2 * per * (1 - half) + per, per),
        column(PREP, lambda half: 2 * per * half, per),
        column(PREP, lambda half: 2 * per * half + per, per),
    ]


def probs_spec(blocks):
    return pl.BlockSpec((1, blocks, PREP + KB, 2 * QB), lambda i: (i, 0, 0, 0))


def attend(pref_count, qkv, halo, prefix, start, place, layer=0, chores=()):
    tokens, width = qkv.shape[0], qkv.shape[1] // 3
    pairs, blocks = width // (2 * HEAD), tokens // QB
    chores = chores if pairs == 8 else ()
    anywhere = pl.BlockSpec(memory_space=pl.ANY)
    stages = []
    for _, _, rows, columns in chores:
        stages += [
            pltpu.VMEM((8, rows, columns), LOW),
            pltpu.SemaphoreType.DMA((8,)),
            pltpu.SemaphoreType.DMA((8,)),
        ]
    operands = [buffer for buffers, *_ in chores for buffer in buffers]
    return pl.pallas_call(
        functools.partial(
            attend_kernel, pref_count, layer, [(len(chore[0]), *chore[1:]) for chore in chores]
        ),
        grid=(pairs,),
        in_specs=attention_specs(tokens, pairs // 2)
        + [pl.BlockSpec((1, tokens), lambda i: (0, 0)), pl.BlockSpec(memory_space=pltpu.SMEM)]
        + [anywhere] * len(operands),
        out_specs=[column(tokens), probs_spec(blocks)] + [anywhere] * len(chores),
        out_shape=[
            jax.ShapeDtypeStruct((tokens, width), LOW),
            jax.ShapeDtypeStruct((pairs, blocks, PREP + KB, 2 * QB), LOW),
        ]
        + [jax.ShapeDtypeStruct((8, rows, columns), LOW) for _, _, rows, columns in chores],
        scratch_shapes=[
            pltpu.VMEM((PREP + BAND + tokens, 2 * HEAD), LOW),
            pltpu.VMEM((PREP + BAND + tokens, 2 * HEAD), LOW),
            pltpu.VMEM((2 * QB, 2 * QB), jnp.int32),
            *stages,
        ],
        name="attend",
        compiler_params=pltpu.CompilerParams(vmem_limit_bytes=56 * 2**20),
        cost_estimate=pl.CostEstimate(flops=12 * 10**9, bytes_accessed=2 * qkv.size, transcendentals=0),
    )(qkv, qkv, qkv, halo, halo, prefix, prefix, start, place, *operands)


def attend_back(qkv, halo, prefix, probs, grad):
    tokens, width = qkv.shape[0], qkv.shape[1] // 3
    pairs, blocks = width // (2 * HEAD), tokens // QB
    keys = PREP + BAND + tokens
    sizes = [(tokens, LOW)] * 3 + [(2 * BAND, LOW), (2 * PREP, WIDE)]
    return pl.pallas_call(
        attend_back_kernel,
        grid=(pairs,),
        in_specs=attention_specs(tokens, pairs // 2) + [probs_spec(blocks), column(tokens)],
        out_specs=[column(rows) for rows, _ in sizes],
        out_shape=[jax.ShapeDtypeStruct((rows, width), kind) for rows, kind in sizes],
        scratch_shapes=[
            pltpu.VMEM((keys, 2 * HEAD), LOW),
            pltpu.VMEM((keys, 2 * HEAD), LOW),
            pltpu.VMEM((keys, 2 * HEAD), WIDE),
            pltpu.VMEM((keys, 2 * HEAD), WIDE),
        ],
        name="attend_back",
        cost_estimate=pl.CostEstimate(flops=16 * 10**9, bytes_accessed=4 * qkv.size, transcendentals=0),
    )(qkv, qkv, qkv, halo, halo, prefix, prefix, probs, grad)


CHUNK = 512
ROWS = 512


def by_rows(total, body):
    step = min(ROWS, total)

    @pl.loop(0, total // step)
    def _(index):
        body(pl.ds(pl.multiple_of(index * step, step), step))


def of_half(step, count, own_ref, far_ref, body):
    @pl.when(step < count)
    def _():
        body(own_ref)

    @pl.when(step >= count)
    def _():
        body(far_ref)


def halves(shape, count, across):
    def spec(place):
        return pl.BlockSpec(shape, lambda j: (0, place(j)) if across else (place(j), 0))

    return [spec(lambda j: jnp.minimum(j, count - 1)), spec(lambda j: jnp.maximum(j - count, 0))]


def whole(shape):
    return pl.BlockSpec(shape, lambda j: (0,) * len(shape))


def slab(index, tokens, width, part=0):
    return pl.BlockSpec((None, tokens, width), lambda j: (index, part, 0))


def call(kernel, grid, in_specs, out_specs, out_shape, scratch, name, flops, operands, buffer=None):
    size, count = sum(o.size * o.dtype.itemsize for o in operands), len(operands)
    body, aliases = kernel, {}
    if buffer is not None:
        in_specs, operands = in_specs + [pl.BlockSpec(memory_space=pl.ANY)], (*operands, buffer)
        aliases = {count: 0}

        def body(*refs):
            kernel(*refs[:count], *refs[count + 1 :])

    return pl.pallas_call(
        body,
        grid=(grid,),
        in_specs=in_specs,
        out_specs=out_specs,
        out_shape=out_shape,
        input_output_aliases=aliases,
        scratch_shapes=scratch,
        name=name,
        compiler_params=pltpu.CompilerParams(vmem_limit_bytes=56 * 2**20),
        cost_estimate=pl.CostEstimate(flops=flops, bytes_accessed=size, transcendentals=0),
    )(*operands)


def qkv_kernel(x_ref, gain_ref, shift_ref, own_ref, far_ref, bias_ref, out_ref, halo_ref, normed):
    step = pl.program_id(0)

    @pl.when(step == 0)
    def _():
        def body(span):
            normed[span] = layer_norm(
                x_ref[span].astype(WIDE), gain_ref[...], shift_ref[...]
            ).astype(LOW)

        by_rows(x_ref.shape[0], body)

    def body(weight_ref):
        third = weight_ref.shape[1] // 3
        for part in range(3):
            span = slice(part * third, (part + 1) * third)
            out = (dot_nn(normed[...], weight_ref[:, span]) + bias_ref[:, span]).astype(LOW)
            out_ref[:, span] = out
            if part:
                halo_ref[:, (part - 1) * third : part * third] = out[out.shape[0] - BAND :]

    of_half(step, 1, own_ref, far_ref, body)


def qkv_forward(x, gain, shift, weights, bias):
    tokens, width = x.shape
    half = weights[0].shape[1] // 3
    return call(
        qkv_kernel,
        2,
        [whole(x.shape), whole((1, width)), whole((1, width))]
        + halves((width, 3 * half), 1, True)
        + [pl.BlockSpec((1, 3 * half), lambda j: (0, j))],
        [
            pl.BlockSpec((tokens, 3 * half), lambda j: (0, j)),
            pl.BlockSpec((BAND, 2 * half), lambda j: (0, j)),
        ],
        [
            jax.ShapeDtypeStruct((tokens, 6 * half), LOW),
            jax.ShapeDtypeStruct((BAND, 4 * half), LOW),
        ],
        [pltpu.VMEM(x.shape, LOW)],
        "qkv",
        12 * tokens * width * half,
        (x, gain, shift, *weights, bias),
    )


def mlp_kernel(count, x_ref, c_ref, po_ref, pf_ref, b0_ref, gain_ref, shift_ref, fo_ref, ff_ref, bias_ref, wo_ref,
               wf_ref, b1_ref, y_ref, h_ref, slope_ref, low_ref, normed):
    step = pl.program_id(0)
    half = po_ref.shape[0]

    @pl.when(step == 0)
    def _():
        def body(span):
            h = x_ref[span].astype(WIDE) + (
                dot_nn(c_ref[span, :half], po_ref[...])
                + dot_nn(c_ref[span, half:], pf_ref[...])
                + b0_ref[...]
            )
            h_ref[span] = h
            normed[span] = layer_norm(h, gain_ref[...], shift_ref[...]).astype(LOW)
            y_ref[span] = h + b1_ref[...]

        by_rows(x_ref.shape[0], body)

    def half_body(up_ref, down_ref):
        def body(span):
            active, slope = gelu_parts(dot_nn(normed[span], up_ref[...]) + bias_ref[...])
            slope_ref[span] = slope.astype(LOW)
            y_ref[span] += dot_nn(active.astype(LOW), down_ref[...])

        by_rows(x_ref.shape[0], body)

    of_half(step, count, (fo_ref, wo_ref), (ff_ref, wf_ref), lambda refs: half_body(*refs))

    @pl.when(step == 2 * count - 1)
    def _():
        low_ref[...] = y_ref[...].astype(LOW)


def mlp_forward(x, c, weights, biases, gain, shift, fc_bias):
    tokens, width = x.shape
    half, count = width // 2, weights["fc"][0].shape[1] // CHUNK
    row = whole((1, width))
    return call(
        functools.partial(mlp_kernel, count),
        2 * count,
        [whole(x.shape), whole(c.shape), whole((half, width)), whole((half, width)), row, row, row]
        + halves((width, CHUNK), count, True)
        + [pl.BlockSpec((1, CHUNK), lambda j: (0, j))]
        + halves((CHUNK, width), count, False)
        + [row],
        [
            slab(0, tokens, width),
            whole(x.shape),
            pl.BlockSpec((tokens, CHUNK), lambda j: (0, j)),
            whole(x.shape),
        ],
        [
            jax.ShapeDtypeStruct((2, tokens, width), WIDE),
            jax.ShapeDtypeStruct(x.shape, WIDE),
            jax.ShapeDtypeStruct((tokens, 2 * count * CHUNK), LOW),
            jax.ShapeDtypeStruct(x.shape, LOW),
        ],
        [pltpu.VMEM(x.shape, LOW)],
        "mlp",
        2 * tokens * width * (width + 4 * count * CHUNK),
        (x, c, *weights["proj"], biases[0], gain, shift, *weights["fc"], fc_bias, *weights["fc2"], biases[1]),
    )


def mlp_back_kernel(count, dy_ref, h_ref, gain_ref, slope_ref, wo_ref, wf_ref, fo_ref, ff_ref, po_ref, pf_ref,
                    dh_ref, dc_ref, total):
    step = pl.program_id(0)
    half = po_ref.shape[0]

    def half_body(first, up_ref, down_ref):
        def body(span):
            du = (dot_nt(dy_ref[span], down_ref[...]) * slope_ref[span].astype(WIDE)).astype(LOW)
            dm = dot_nt(du, up_ref[...])
            total[span] = dm if first else total[span] + dm

        by_rows(dy_ref.shape[0], body)

    @pl.when(step == 0)
    def _():
        half_body(True, fo_ref, wo_ref)

    @pl.when((step > 0) & (step < count))
    def _():
        half_body(False, fo_ref, wo_ref)

    @pl.when(step >= count)
    def _():
        half_body(False, ff_ref, wf_ref)

    @pl.when(step == 2 * count - 1)
    def _():
        def body(span):
            dh = dy_ref[span].astype(WIDE) + norm_back(h_ref[span], gain_ref[...], total[span])
            dh_ref[span] = dh
            low = dh.astype(LOW)
            dc_ref[span, :half] = dot_nt(low, po_ref[...]).astype(LOW)
            dc_ref[span, half:] = dot_nt(low, pf_ref[...]).astype(LOW)

        by_rows(dy_ref.shape[0], body)


def mlp_back(dy, h, gain, slope, weights):
    tokens, width = dy.shape
    half, count = width // 2, weights["fc"][0].shape[1] // CHUNK
    return call(
        functools.partial(mlp_back_kernel, count),
        2 * count,
        [whole(dy.shape), whole(dy.shape), whole((1, width)), pl.BlockSpec((tokens, CHUNK), lambda j: (0, j))]
        + halves((CHUNK, width), count, False)
        + halves((width, CHUNK), count, True)
        + [whole((half, width)), whole((half, width))],
        [whole(dy.shape), whole(dy.shape)],
        [jax.ShapeDtypeStruct(dy.shape, WIDE), jax.ShapeDtypeStruct(dy.shape, LOW)],
        [pltpu.VMEM(dy.shape, WIDE)],
        "mlp_back",
        2 * tokens * width * (width + 4 * count * CHUNK),
        (dy, h, gain, slope, *weights["fc2"], *weights["fc"], *weights["proj"]),
    )


def mlp_both_kernel(count, x_ref, c_ref, dy_ref, po_ref, pf_ref, b0_ref, gain_ref, shift_ref, fo_ref, ff_ref, bias_ref,
                    wo_ref, wf_ref, b1_ref, y_ref, low_ref, dh_ref, dc_ref, h_ref, normed, total):
    step = pl.program_id(0)
    half = po_ref.shape[0]

    @pl.when(step == 0)
    def _():
        def body(span):
            h = x_ref[span].astype(WIDE) + (
                dot_nn(c_ref[span, :half], po_ref[...])
                + dot_nn(c_ref[span, half:], pf_ref[...])
                + b0_ref[...]
            )
            h_ref[span] = h
            normed[span] = layer_norm(h, gain_ref[...], shift_ref[...]).astype(LOW)
            y_ref[span] = h + b1_ref[...]
            total[span] = jnp.zeros_like(h)

        by_rows(x_ref.shape[0], body)

    def half_body(up_ref, down_ref):
        def body(span):
            active, slope = gelu_parts(dot_nn(normed[span], up_ref[...]) + bias_ref[...])
            du = (dot_nt(dy_ref[span], down_ref[...]) * slope).astype(LOW)
            y_ref[span] += dot_nn(active.astype(LOW), down_ref[...])
            total[span] += dot_nt(du, up_ref[...])

        by_rows(x_ref.shape[0], body)

    of_half(step, count, (fo_ref, wo_ref), (ff_ref, wf_ref), lambda refs: half_body(*refs))

    @pl.when(step == 2 * count - 1)
    def _():
        def body(span):
            low_ref[span] = y_ref[span].astype(LOW)
            dh = dy_ref[span].astype(WIDE) + norm_back(h_ref[span], gain_ref[...], total[span])
            dh_ref[span] = dh
            low = dh.astype(LOW)
            dc_ref[span, :half] = dot_nt(low, po_ref[...]).astype(LOW)
            dc_ref[span, half:] = dot_nt(low, pf_ref[...]).astype(LOW)

        by_rows(x_ref.shape[0], body)


def mlp_both(acts, x, c, dy, weights, biases, gain, shift, fc_bias):
    tokens, width = x.shape
    half, count = width // 2, weights["fc"][0].shape[1] // CHUNK
    row, full = whole((1, width)), whole(x.shape)
    return call(
        functools.partial(mlp_both_kernel, count),
        2 * count,
        [full, full, full, whole((half, width)), whole((half, width)), row, row, row]
        + halves((width, CHUNK), count, True)
        + [pl.BlockSpec((1, CHUNK), lambda j: (0, j))]
        + halves((CHUNK, width), count, False)
        + [row],
        [slab(1, tokens, width), full, full, full],
        [jax.ShapeDtypeStruct(acts.shape, WIDE)]
        + [jax.ShapeDtypeStruct(x.shape, kind) for kind in (LOW, WIDE, LOW)],
        [pltpu.VMEM(x.shape, WIDE), pltpu.VMEM(x.shape, LOW), pltpu.VMEM(x.shape, WIDE)],
        "mlp_both",
        4 * tokens * width * (width + 4 * count * CHUNK),
        (x, c, dy, *weights["proj"], biases[0], gain, shift, *weights["fc"], fc_bias, *weights["fc2"], biases[1]),
        acts,
    )


def qkv_back_kernel(reach, dq_ref, dk_ref, dv_ref, hk_ref, hv_ref, own_ref, far_ref, x_ref, dh_ref, gain_ref, other_ref,
                    section_ref, dx_ref, low_ref, total):
    step = pl.program_id(0)

    def joined_grads(grad_ref, halo_ref):
        grad = grad_ref[...]
        if not reach:
            return grad
        early = grad.shape[0] - reach
        late = (grad[early:].astype(WIDE) + halo_ref[...].astype(WIDE)).astype(LOW)
        return jnp.concatenate([grad[:early], late], axis=0) if early else late

    def half_body(first, weight_ref):
        grads = (dq_ref[...], joined_grads(dk_ref, hk_ref), joined_grads(dv_ref, hv_ref))
        term = dot_nt(jnp.concatenate(grads, axis=1), weight_ref[...])
        total[...] = term if first else total[...] + term

    @pl.when(step == 0)
    def _():
        half_body(True, own_ref)

    @pl.when(step == 1)
    def _():
        half_body(False, far_ref)

        def body(span):
            dx = dh_ref[span] + norm_back(x_ref[span].astype(WIDE), gain_ref[...], total[span])
            dx_ref[span] = dx
            low = dx.astype(LOW)
            low_ref[span] = jnp.where(section_ref[0] == 0, other_ref[span], low)

        by_rows(x_ref.shape[0], body)


def qkv_back(grads, halo, weights, x, dh, gain, other, section, layer, buffer=None, part=0, parts=1):
    width = x.shape[1]
    tokens, half = x.shape[0] // parts, width // 2
    reach = BAND if part == parts - 1 else 0
    piece = pl.BlockSpec((tokens, half), lambda j: (part, j))
    edges = [pl.BlockSpec((BAND, half), lambda j, i=i: (i, 1 - j)) for i in range(2)]
    mine, shape = pl.BlockSpec((tokens, width), lambda j: (part, 0)), (tokens, width)
    return call(
        functools.partial(qkv_back_kernel, reach),
        2,
        [piece, piece, piece, *edges]
        + halves((width, 3 * half), 1, True)
        + [mine, mine, whole((1, width)), mine, pl.BlockSpec(memory_space=pltpu.SMEM)],
        [slab(layer, tokens, width, part), whole(shape)],
        [jax.ShapeDtypeStruct((2, *x.shape), WIDE), jax.ShapeDtypeStruct(shape, LOW)],
        [pltpu.VMEM(shape, WIDE)],
        "qkv_back",
        12 * tokens * width * half,
        (*grads, halo, halo, *weights, x, dh, gain, other, section),
        buffer,
    )


def take_kernel(section_ref, got_ref, held_ref, out_ref):
    out_ref[0] = got_ref[...].astype(WIDE)


def take(section, got, buffer, start=0):
    rows, width = got.shape
    step = min(128, rows)
    base = start // step
    return pl.pallas_call(
        take_kernel,
        grid_spec=pltpu.PrefetchScalarGridSpec(
            num_scalar_prefetch=1,
            grid=(rows // step,),
            in_specs=[
                pl.BlockSpec((step, width), lambda i, s: (i, 0)),
                pl.BlockSpec(memory_space=pl.ANY),
            ],
            out_specs=pl.BlockSpec((1, step, width), lambda i, s: (1 - s[0], base + i, 0)),
        ),
        out_shape=jax.ShapeDtypeStruct(buffer.shape, WIDE),
        input_output_aliases={2: 0},
        name="take",
        cost_estimate=pl.CostEstimate(flops=0, bytes_accessed=6 * got.size, transcendentals=0),
    )(section, got, buffer)


NAMES = ("qkv", "proj", "fc", "fc2")
JOIN, QKV, ATTEND, MLP = range(4)
BESIDE = (0, 1, 2, 3)
ORDER = (
    (1, 0, 0, 0, 0), (0, 0, 0, 0, 0), (2, 0, 0, 0, 0), (1, 1, 0, 0, 0), (0, 2, 0, 0, 0),
    (1, 3, 0, 0, 0), (2, 2, 0, 0, 0), (1, 0, 0, 1, 0), (0, 8, 0, 0, 0), (0, 0, 1, 0, 0),
    (1, 2, 0, 1, 0), (2, 2, 1, 0, 0), (0, 2, 1, 0, 0), (1, 0, 1, 0, 0), (2, 9, 0, 0, 0),
    (0, 2, 2, 0, 0), (1, 0, 1, 1, 0), (2, 6, 0, 0, 0), (2, 9, 1, 0, 0), (1, 2, 1, 0, 0),
    (0, 7, 0, 0, 0), (1, 2, 1, 1, 0), (2, 0, 1, 0, 0), (1, 2, 2, 0, 0), (0, 6, 0, 0, 0),
    (2, 9, 2, 0, 0), (2, 0, 2, 0, 0), (0, 0, 2, 0, 0), (1, 0, 2, 0, 0), (2, 2, 2, 0, 0),
    (1, 2, 0, 0, 0), (0, 6, 1, 0, 0), (0, 0, 3, 0, 0), (1, 0, 3, 0, 0), (2, 7, 0, 0, 0),
    (0, 2, 3, 0, 0), (1, 0, 2, 1, 0), (2, 6, 1, 0, 0), (1, 0, 3, 1, 0), (0, 7, 1, 0, 0),
    (2, 7, 1, 0, 0), (1, 2, 3, 0, 0), (0, 6, 2, 0, 0), (1, 2, 2, 1, 0), (2, 6, 2, 0, 0),
    (0, 7, 2, 0, 0), (1, 2, 3, 1, 0), (2, 7, 2, 0, 0), (0, 6, 3, 0, 0), (0, 7, 3, 0, 0),
    (3, 0, 0, 0, 0), (3, 0, 1, 0, 0), (3, 0, 2, 0, 0), (3, 0, 3, 0, 0), (3, 0, 0, 1, 0),
    (3, 0, 1, 1, 0), (3, 0, 2, 1, 0), (3, 0, 3, 1, 0), (3, 1, 0, 0, 0), (3, 2, 0, 0, 0),
    (3, 3, 0, 0, 0), (3, 1, 0, 1, 0), (3, 2, 0, 1, 0), (3, 3, 0, 1, 0),
)
JOINED = {8: ((1, 0, 0, 0), (1, 0, 0, 1)), 9: ((8, 0, 0, 0), (8, 0, 1, 0))}
DEEP = 2
LATE = 3


def move(block, link):
    if link == 1:
        return swap(block, "section")
    count = lax.axis_size("rows")
    if link == 0:
        return lax.ppermute(block, "rows", [(i, i ^ 1) for i in range(count)])
    return lax.ppermute(block, "rows", [(i, (i + 2) % count) for i in range(count)])


def spread(shards, section, run):
    held = {(base, 0, 0, 0): shards[name] for base, name in enumerate(NAMES)}
    sent, passed, awaited = {}, [], []

    def get(key):
        if key not in held:
            base = key[0]
            if base in JOINED:
                held[key] = jnp.concatenate([get(part) for part in JOINED[base]], axis=0)
            else:
                raw = base // 2
                held[key] = jnp.where(section == base % 2, get((raw, 0, 0, 0)), get((raw, 0, 0, 1)))
        return held[key]

    for link, *key in ORDER:
        if link == 3:
            now, later = run(*key[:3], get)
            passed = [now] if now is not None else passed
            if later is not None:
                awaited.append([LATE, later])
            continue
        block, ahead = get(tuple(key)), sent.setdefault(link, [])
        behind = list(passed)
        if len(ahead) >= DEEP:
            behind.append(ahead[-DEEP])
        for entry in awaited:
            entry[0] -= 1
            if entry[0] == 0:
                behind.append(entry[1])
        if behind:
            block, *_ = lax.optimization_barrier((block, *behind))
        base, steps, over_x, over_y = key
        target = (base, steps + (link == 2), over_x + (link == 0), over_y + (link == 1))
        held[target] = move(block, link)
        ahead.append(held[target])


def pieces(matrix, layer, resolved):
    result = []
    for steps in range(4):
        for over_x in range(2):
            if matrix == 1:
                key = (9, steps, 0, 0)
                near, away = (key, 2 * over_x), (key, 2 * over_x + 1)
            elif resolved:
                near = away = ((2 * matrix + layer, steps, over_x, 0), 0)
            else:
                near, away = ((matrix, steps, over_x, 0), 0), ((matrix, steps, over_x, 1), 0)
            result.append((steps, over_x, near, away))
    return result


def join_kernel(plan, layer, rows, place_ref, *refs):
    copies = ShardCopies(plan, layer, rows, place_ref, refs[:-4], *refs[-4:])
    copies.fetch(range(8))
    for index in range(8):
        copies.deliver(index)
    copies.finish()


def plan_of(matrix, layer, get):
    keys, plan = [], []
    resolved = any(link < 3 and base == 2 * matrix for link, base, *_ in ORDER if matrix > 1)
    for steps, over_x, *sources in pieces(matrix, layer, resolved):
        spots = []
        for key, block in sources:
            if key not in keys:
                keys.append(key)
            spots.append((keys.index(key), block))
        plan.append((steps, over_x, *spots))
    return [get(key) for key in keys], plan


def joined(matrix, layer, get, shape, place):
    rows, columns = shape
    buffers, plan = plan_of(matrix, layer, get)
    anywhere = pl.BlockSpec(memory_space=pl.ANY)
    whole = pl.pallas_call(
        functools.partial(join_kernel, plan, layer, rows),
        in_specs=[pl.BlockSpec(memory_space=pltpu.SMEM)] + [anywhere] * len(buffers),
        out_specs=anywhere,
        out_shape=jax.ShapeDtypeStruct((8, rows, columns), LOW),
        scratch_shapes=[
            pltpu.VMEM((8, rows, columns), LOW),
            pltpu.SemaphoreType.DMA((8,)),
            pltpu.SemaphoreType.DMA((8,)),
        ],
        name="join",
        cost_estimate=pl.CostEstimate(flops=0, bytes_accessed=4 * 8 * rows * columns, transcendentals=0),
    )(place, *buffers)
    return whole.reshape(8 * rows, columns)


def forward(shards, x, dy, start, smalls, pref_count):
    section, rows = lax.axis_index("section"), lax.axis_index("rows")
    weights, kept, outputs, slopes = [{}, {}], [None, None], [None, None], []

    def run(kind, matrix, layer, get):
        small, mine = smalls[layer], weights[layer]
        place = jnp.stack([section, rows // 2, rows % 2]).astype(jnp.int32)
        if kind == JOIN:
            name = NAMES[matrix]
            if layer and matrix in BESIDE:
                return None, None
            near = joined(matrix, layer, get, shards[name].shape, place)
            mine[name] = (near, swap(near, "tensor"))
            return mine[name]
        if kind == QKV:
            source = outputs[0][1] if layer else x
            qkv, edge = qkv_forward(source, small["gain"][0:1], small["shift"][0:1], mine["qkv"], small["qkv"])
            kept[layer] = (source, qkv, lax.ppermute(edge, "tensor", [(0, 1)]))
            return qkv, kept[layer][2]
        if kind == ATTEND:
            source, qkv, halo = kept[layer]
            chores = []
            if get is not None and not layer:
                chores = [(*plan_of(other, 1, get), *shards[NAMES[other]].shape) for other in BESIDE]
            ahead = start
            if chores:
                ahead, _ = lax.optimization_barrier((start, mine["proj"][1]))
            c, probs, *wholes = attend(pref_count, qkv, halo, small["prefix"], ahead, place, 1, chores)
            for name, near in zip([NAMES[other] for other in BESIDE], wholes):
                near = near.reshape(-1, near.shape[-1])
                weights[1][name] = (near, swap(near, "tensor"))
            kept[layer] = (source, qkv, halo, probs, c)
            return c, None
        source, qkv, halo, probs, c = kept[layer]
        kept[layer] = (source, qkv, halo, probs)
        biases = (small["out"][0:1], small["out"][1:2])
        norm = (small["gain"][1:2], small["shift"][1:2])
        if layer:
            *outputs[1], dh, dc = mlp_both(outputs[0][0], source, c, dy, mine, biases, *norm, small["fc"])
            slopes.extend((dh, dc))
        else:
            acts, h, slope, low = mlp_forward(source, c, mine, biases, *norm, small["fc"])
            outputs[0] = (acts, low)
            slopes.extend((h, slope))
        return slopes[-1], None

    if lax.axis_size("rows") == 8:
        spread(shards, section, run)
    else:
        for name in NAMES:
            near = lax.all_gather(shards[name], ("section", "rows"), axis=0, tiled=True)
            near = near.reshape(2, -1, near.shape[1])
            far = swap(near, "tensor")
            for layer in range(2):
                weights[layer][name] = (near[layer], far[layer])
        for link, *stage in ORDER:
            if link == 3 and stage[0] != JOIN:
                run(*stage[:3], None)
    return weights, kept, outputs, slopes


def on_device(
    tokens,
    segment_ids,
    cotangent,
    ln_gain,
    ln_bias,
    w_qkv,
    query_key_value_bias,
    w_proj,
    w_fc,
    fc_bias,
    w_fc2,
    out_bias,
    prefix_embed,
    rep_w1,
    rep_b1,
    rep_w2,
    rep_b2,
):
    share, width = tokens.shape[1:]
    section, core = lax.axis_index("section"), lax.axis_index("tensor")
    rows_index, rows = lax.axis_index("rows"), lax.axis_size("rows")
    half = rep_w2.shape[-1]
    pref_count = prefix_embed.shape[0]

    shards = {
        "qkv": w_qkv[0].astype(LOW).reshape(w_qkv.shape[1], -1),
        "proj": w_proj[0].astype(LOW),
        "fc": w_fc[0].astype(LOW),
        "fc2": w_fc2[0].astype(LOW),
    }
    rep_hidden = jnp.tanh(jnp.dot(prefix_embed, rep_w1, precision=HIGHEST) + rep_b1)
    prefix = jnp.einsum("pm,mcd->pcd", rep_hidden, rep_w2[:, 0], precision=HIGHEST) + rep_b2[0]
    prefix = prefix.astype(LOW).astype(WIDE)
    prefix = jnp.pad(prefix, ((0, PREP - pref_count), (0, 0), (0, 0)))
    parts = [ln_gain[0], ln_bias[0], out_bias[0], query_key_value_bias[0], fc_bias[0], prefix]
    packed = jnp.concatenate([part.reshape(-1) for part in parts])
    near = jnp.stack([packed, swap(packed, "tensor")])
    away = swap(near, "section")
    smalls = []
    for layer in range(2):
        cut, place = [], 0
        chosen = jnp.where(section == layer, near, away)
        for part in parts:
            cut.append([chosen[h, place : place + part.size].reshape(part.shape) for h in range(2)])
            place += part.size
        smalls.append(
            {
                "gain": cut[0][0],
                "shift": cut[1][0],
                "out": cut[2][0],
                "qkv": jnp.concatenate([cut[3][h].reshape(1, -1) for h in range(2)], axis=1),
                "fc": jnp.concatenate([cut[4][h].reshape(1, -1) for h in range(2)], axis=1),
                "prefix": jnp.concatenate(
                    [cut[5][h].reshape(PREP, -1).astype(LOW) for h in range(2)], axis=1
                ),
            }
        )

    own = section
    segments = lax.dynamic_index_in_dim(segment_ids, own, 0, keepdims=False).reshape(-1)
    mine = lax.dynamic_slice_in_dim(segments, core * share, share)
    start = jnp.sum(segments[:, None] < mine[None, :], axis=0, dtype=jnp.int32)
    start = (start - core * share + BAND)[None]

    x = lax.dynamic_index_in_dim(tokens, own, 0, keepdims=False)
    dy = lax.dynamic_index_in_dim(cotangent, own, 0, keepdims=False)
    x, dy = lax.optimization_barrier((x, dy))
    weights, (kept0, kept1), ((_, low0), (acts, low1)), (h, slope, dh, dc) = forward(
        shards, x, dy, start, smalls, pref_count
    )
    dy = lax.dynamic_index_in_dim(cotangent, own, 0, keepdims=False)
    got_acts = swap(jnp.where(section == 0, low1, low0), "section")
    where_at = section.astype(jnp.int32).reshape(1)
    nowhere = jnp.ones((1,), jnp.int32)

    x1, qkv, halo, probs = kept1
    *grads, edge, pre1 = attend_back(qkv, halo, smalls[1]["prefix"], probs, dc)
    edge = lax.ppermute(edge, "tensor", [(1, 0)])
    in_grads, down1 = qkv_back(
        grads, edge, weights[1]["qkv"], x1, dh, smalls[1]["gain"][0:1], low1, nowhere, 1
    )
    dh, dc = mlp_back(down1, h, smalls[0]["gain"][1:2], slope, weights[0])
    got_acts, dc = lax.optimization_barrier((got_acts, dc))
    acts = take(where_at, got_acts, acts)
    x0, qkv, halo, probs = kept0
    *grads, edge, pre0 = attend_back(qkv, halo, smalls[0]["prefix"], probs, dc)
    edge = lax.ppermute(edge, "tensor", [(1, 0)])

    pre0, pre1 = [pre.reshape(2, PREP, 2, half) for pre in (pre0, pre1)]
    near = jnp.where(section == 0, pre0, pre1) + swap(jnp.where(section == 0, pre1, pre0), "section")
    tail = (weights[0]["qkv"], x0)
    gain = smalls[0]["gain"][0:1]
    in_grads, sent = qkv_back(grads, grads[0], *tail, dh, gain, down1, where_at, 0, in_grads, 0, 2)
    got = [swap(sent, "section")]
    near, _ = lax.optimization_barrier((near, sent))
    total = (near[:, :, 0] + swap(near[:, :, 1], "tensor"))[:, :pref_count]
    hidden_term = jnp.einsum("cpd,mcd->pm", total, rep_w2[:, 0], precision=HIGHEST)
    dh, _ = lax.optimization_barrier((dh, hidden_term))
    in_grads, sent = qkv_back(grads, edge, *tail, dh, gain, down1, where_at, 0, in_grads, 1, 2)
    got.append(swap(sent, "section"))
    sums = jnp.concatenate([total.reshape(2 * pref_count, half), hidden_term], axis=0)
    sums, _, _ = lax.optimization_barrier((sums, sent, got[0]))
    sums = all_sum(sums, ("rows",))
    total, hidden_term = sums[: 2 * pref_count].reshape(2, pref_count, half), sums[2 * pref_count :]
    hidden_term, *got = lax.optimization_barrier((hidden_term, *got))
    for part in range(2):
        in_grads = take(where_at, got[part], in_grads, part * share // 2)
    grad_hidden = all_sum(hidden_term, ("section", "tensor"))
    grad_b2 = jnp.sum(total, axis=1)
    mid_part = rep_w1.shape[1] // rows
    width_part = width // rows
    hidden_part = lax.dynamic_slice_in_dim(rep_hidden, rows_index * mid_part, mid_part, 1)
    grad_w2 = jnp.einsum("pm,cpd->mcd", hidden_part, total, precision=HIGHEST)
    grad_pre = grad_hidden * (1.0 - rep_hidden * rep_hidden)
    grad_b1 = jnp.sum(grad_pre, axis=0)
    embed_part = lax.dynamic_slice_in_dim(prefix_embed, rows_index * width_part, width_part, 1)
    grad_w1 = jnp.einsum("pd,pm->dm", embed_part, grad_pre, precision=HIGHEST)
    weight_part = lax.dynamic_slice_in_dim(rep_w1, rows_index * width_part, width_part, 0)
    grad_embed = jnp.einsum("pm,dm->pd", grad_pre, weight_part, precision=HIGHEST)
    return (acts[None], in_grads[None], grad_embed, grad_w1, grad_b1, grad_w2[:, None], grad_b2[None])


def solution(mesh):
    return jax.shard_map(
        on_device,
        mesh=mesh,
        in_specs=(
            P(None, ("rows", "tensor"), None),
            P(None, "rows", None),
            P(None, ("rows", "tensor"), None),
            P("section", None, None),
            P("section", None, None),
            P("section", "rows", None, "tensor"),
            P("section", None, "tensor"),
            P("section", ("tensor", "rows"), None),
            P("section", "rows", "tensor"),
            P("section", "tensor"),
            P("section", ("tensor", "rows"), None),
            P("section", None, None),
            P(),
            P(),
            P(),
            P(None, "section", None, "tensor"),
            P("section", None, "tensor"),
        ),
        out_specs=(
            P("section", None, ("rows", "tensor"), None),
            P("section", None, ("rows", "tensor"), None),
            P(None, "rows"),
            P("rows", None),
            P(),
            P("rows", "section", None, "tensor"),
            P("section", None, "tensor"),
        ),
        check_vma=False,
    )
```
